128 devices in a mesh: fsdp: 4 (over z), sp: 32 (over x, y, core).
Axes of the slice: x: 4, y: 4, z: 4, core: 2. Of those that a mesh axis runs over, the one named last changes fastest.
Arguments:
- tokens: bfloat16 [4, 20480, 1536], P('fsdp', 'sp'), may hold values from -6 to 6
- mod_scale: float32 [4, 1536], P('fsdp'), may hold values from 0.25 to 3
- mod_shift: float32 [4, 1536], P('fsdp'), may hold values from -3 to 3
- w_qkv: bfloat16 [1536, 4608], P(None, 'fsdp'), may hold values from -0.15625 to 0.15625
- w_out: bfloat16 [1536, 1536], P('fsdp'), may hold values from -0.15625 to 0.15625
- neighbors: int32 [4, 160, 6], P('fsdp', 'sp'), may hold values from 0 to 19, as said below
- counts: int32 [4, 8], P('fsdp'), may hold values from 1921 to 2560, as said below
Outputs:
- attn_out: bfloat16 [4, 20480, 1536], P('fsdp', 'sp')
The draws below stay inside these ranges and needn't reach their ends.
Inputs may be any that keep to these rules, and one draw needn't show every extreme that they name: `neighbors`: each list holds 6 different tiles of the same frame, the tile itself first, the others at most one tile row and two tile columns away from it. `counts`: padding lies in the last row of tiles only; in every clip some frame is full.
All inputs are finite; a program needn't handle non-finite values.
Results may differ from the reference program's by a relative error of at most 0.006.
The reference program's roundings to bfloat16 on the way count: a program that leaves them out, or rounds other values in their place, can miss the bound.
Values may be sent and summed in bfloat16 or wider, within the bound.
A program may use at most 192 MiB of HBM per device.

```python
import math
import jax
import jax.numpy as jnp
from jax import lax

D = 1536
HEADS = 12
HD = 128
TILE = 128
TGW = 5
NBR = 6
PIECES = 4
TGH = 4
TILES_F = 20
POS = 2560
TOK_DEV = 640
FRAMES = 8
CLIPS = 4


def draw_mod_scale(key, part):
    drawn = jax.random.uniform(key, (CLIPS, D), jnp.float32, 0.25, 1.25)
    return drawn


def draw_neighbors(key, part):
    total_tiles = FRAMES * TILES_F
    band_tiles = TILES_F // PIECES
    row_ids = jnp.arange(total_tiles, dtype=jnp.int32)
    band_ids = row_ids // (FRAMES * band_tiles)
    tile_ids = band_ids * band_tiles + row_ids % band_tiles
    tile_row = tile_ids // TGW
    tile_col = tile_ids % TGW
    shift_row = jnp.array([-1, -1, -1, -1, -1, 0, 0, 0, 0, 1, 1, 1, 1, 1], dtype=jnp.int32)
    shift_col = jnp.array([-2, -1, 0, 1, 2, -2, -1, 1, 2, -2, -1, 0, 1, 2], dtype=jnp.int32)
    cand_row = tile_row[:, None] + shift_row[None, :]
    cand_col = tile_col[:, None] + shift_col[None, :]
    inside = (cand_row >= 0) & (cand_row < TGH) & (cand_col >= 0) & (cand_col < TGW)
    cand_ids = cand_row * TGW + cand_col
    ranks = jax.random.randint(key, (CLIPS, total_tiles, 14), 0, 1048576, dtype=jnp.int32) * 16
    ranks = ranks + jnp.arange(14, dtype=jnp.int32)
    ranks = jnp.where(inside, ranks, -1)
    top_vals, picked = lax.top_k(ranks, NBR - 1)
    chosen = jnp.take_along_axis(jnp.broadcast_to(cand_ids, ranks.shape), picked.astype(jnp.int32), axis=-1)
    self_ids = jnp.broadcast_to(tile_ids[None, :, None], (CLIPS, total_tiles, 1))
    return jnp.concatenate([self_ids, chosen], axis=-1).astype(jnp.int32)


def draw_counts(key, part):
    first_key = jax.random.fold_in(key, 11)
    second_key = jax.random.fold_in(key, 12)
    partial_fill = jax.random.randint(first_key, (CLIPS, FRAMES), POS - TGW * TILE + 1, POS + 1, dtype=jnp.int32)
    full_frame = jax.random.randint(second_key, (CLIPS, 1), 0, FRAMES, dtype=jnp.int32)
    frame_ids = jnp.arange(FRAMES, dtype=jnp.int32)[None, :]
    return jnp.where(frame_ids == full_frame, POS, partial_fill).astype(jnp.int32)


def shard_levels(own_key, dims, shards, least, largest):
    factor_of, own = 1.0, jax.random.fold_in(own_key, 6)
    for position, parts in shards:
        draws = jnp.exp(jax.random.uniform(jax.random.fold_in(own, position), (parts,), jnp.float32, least / len(shards), largest / len(shards)))
        factor_of = factor_of * jnp.repeat(draws, dims[position] // parts).reshape([-1 if axis == position else 1 for axis in range(len(dims))])
    return factor_of


def bell_draw(own_key, extent, deviation, reach, shards=(), kind=jnp.bfloat16):
    values = jax.random.normal(own_key, extent, jnp.float32) * deviation
    if len(shards) > 0:
        values = shard_levels(own_key, extent, shards, -0.22, 0.18) * values
    return jnp.clip(values, min=-reach, max=reach).astype(kind)


def setup_inputs(seed: int = 0) -> dict:
    splits = jax.random.split(jax.random.key(seed), 8)
    tokens = bell_draw(splits[0], (CLIPS, FRAMES * POS, D), 1.0, 6.0, ((0, 4), (1, 32)))
    mod_scale = draw_mod_scale(jax.random.fold_in(splits[7], 71), 0)
    mod_shift = bell_draw(splits[2], (CLIPS, D), 0.5, 3.0, ((0, 4),), jnp.float32)
    w_qkv = bell_draw(splits[3], (D, 3 * D), D ** -0.5, 0.15625, ((1, 4),))
    w_out = bell_draw(splits[4], (D, D), D ** -0.5, 0.15625, ((0, 4),))
    neighbors = draw_neighbors(jax.random.fold_in(splits[7], 71), 0)
    counts = draw_counts(jax.random.fold_in(splits[7], 71), 0)
    return dict(tokens=tokens, mod_scale=mod_scale, mod_shift=mod_shift, w_qkv=w_qkv, w_out=w_out, neighbors=neighbors, counts=counts)


def layer_norm(tokens, mod_scale, mod_shift):
    values_f32 = tokens.astype(jnp.float32)
    center = lax.optimization_barrier(jnp.mean(values_f32, axis=-1, keepdims=True))
    spread = lax.optimization_barrier(jnp.mean((values_f32 - center) ** 2, axis=-1, keepdims=True))
    normal = (values_f32 - center) / jnp.sqrt(spread + 1e-06)
    return (normal * (1.0 + mod_scale) + mod_shift).astype(jnp.bfloat16)

def spatial_frame(operands):
    queries, key_proj, values, tile_list, count_here = operands
    scaling = 1.0 / math.sqrt(HD)
    query_f32 = queries.reshape(TILES_F, TILE, HEADS, HD).astype(jnp.float32)
    key_tiles = key_proj.reshape(TILES_F, TILE, HEADS, HD)
    value_tiles = values.reshape(TILES_F, TILE, HEADS, HD)
    key_near = jnp.take(key_tiles, tile_list, axis=0).reshape(TILES_F, NBR * TILE, HEADS, HD).astype(jnp.float32)
    value_near = jnp.take(value_tiles, tile_list, axis=0).reshape(TILES_F, NBR * TILE, HEADS, HD).astype(jnp.float32)
    key_pos = (tile_list[:, :, None] * TILE + jnp.arange(TILE, dtype=jnp.int32)[None, None, :]).reshape(TILES_F, NBR * TILE)
    live_mask = (key_pos < count_here)[:, None, None, :]
    scores = jnp.einsum('tqhd,tkhd->thqk', query_f32, key_near) * scaling
    scores = jnp.where(live_mask, scores, -1e+30)
    row_max = lax.optimization_barrier(jnp.max(scores, axis=-1, keepdims=True))
    exp_terms = jnp.where(live_mask, jnp.exp(scores - row_max), 0.0)
    denominator = lax.optimization_barrier(jnp.sum(exp_terms, axis=-1, keepdims=True))
    weights = exp_terms.astype(jnp.bfloat16)
    summed = jnp.einsum('thqk,tkhd->tqhd', weights.astype(jnp.float32), value_near)
    result = summed / jnp.transpose(denominator, (0, 2, 1, 3))
    return result.astype(jnp.bfloat16).reshape(POS, D)

def temporal_clip(queries, key_proj, spatial, clip_counts):
    scaling = 1.0 / math.sqrt(HD)
    query_f32 = queries.reshape(FRAMES, POS, HEADS, HD).astype(jnp.float32)
    key_f32 = key_proj.reshape(FRAMES, POS, HEADS, HD).astype(jnp.float32)
    spatial_f32 = spatial.reshape(FRAMES, POS, HEADS, HD).astype(jnp.float32)
    live_mask = (jnp.arange(POS, dtype=jnp.int32)[:, None] < clip_counts[None, :])[:, None, None, :]
    scores = jnp.einsum('fphd,gphd->phfg', query_f32, key_f32) * scaling
    scores = jnp.where(live_mask, scores, -1e+30)
    row_max = lax.optimization_barrier(jnp.max(scores, axis=-1, keepdims=True))
    exp_terms = jnp.where(live_mask, jnp.exp(scores - row_max), 0.0)
    denominator = lax.optimization_barrier(jnp.sum(exp_terms, axis=-1, keepdims=True))
    weights = exp_terms.astype(jnp.bfloat16)
    summed = jnp.einsum('phfg,gphd->fphd', weights.astype(jnp.float32), spatial_f32)
    result = summed / jnp.transpose(denominator, (2, 0, 1, 3))
    return result.astype(jnp.bfloat16).reshape(FRAMES, POS, D)

def reference(tokens, mod_scale, mod_shift, w_qkv, w_out, neighbors, counts):
    band_tiles = TILES_F // PIECES

    def one_clip(operands):
        clip_tokens, clip_scale, clip_shift, clip_lists, clip_counts = operands
        ordered = clip_tokens.reshape(PIECES, FRAMES, TOK_DEV, D).transpose(1, 0, 2, 3).reshape(FRAMES * POS, D)
        normed = layer_norm(ordered, clip_scale, clip_shift)
        qkv = jnp.dot(normed, w_qkv, preferred_element_type=jnp.float32)
        qkv = qkv.astype(jnp.bfloat16).reshape(FRAMES, POS, 3 * D)
        queries = qkv[:, :, :D]
        key_proj = qkv[:, :, D:2 * D]
        values = qkv[:, :, 2 * D:]
        frame_lists = clip_lists.reshape(PIECES, FRAMES, band_tiles, NBR).transpose(1, 0, 2, 3).reshape(FRAMES, TILES_F, NBR)
        spatial = lax.map(spatial_frame, (queries, key_proj, values, frame_lists, clip_counts))
        temporal = temporal_clip(queries, key_proj, spatial, clip_counts)
        result = jnp.dot(temporal.reshape(FRAMES * POS, D), w_out, preferred_element_type=jnp.float32)
        result = result.astype(jnp.bfloat16)
        return result.reshape(FRAMES, PIECES, TOK_DEV, D).transpose(1, 0, 2, 3).reshape(FRAMES * POS, D)
    return lax.map(one_clip, (tokens, mod_scale, mod_shift, neighbors, counts))
```

```python
import math

import jax
import jax.numpy as jnp
from jax import lax
from jax.sharding import Mesh
from jax.sharding import PartitionSpec as P

HEADS = 12
HD = 128
TILE = 128
TGW = 5
NBR = 6
PIECES = 4


def passed_along(block, axis, distance):
    devices = range(lax.axis_size(axis))
    route = [(i - distance, i) for i in devices if i - distance in devices]
    return lax.ppermute(block, axis, route)


def layer_norm(tokens, mod_scale, mod_shift):
    values_f32 = tokens.astype(jnp.float32)
    center = jnp.mean(values_f32, axis=-1, keepdims=True)
    spread = jnp.mean((values_f32 - center) ** 2, axis=-1, keepdims=True)
    normal = (values_f32 - center) / jnp.sqrt(spread + 1e-06)
    return (normal * (1.0 + mod_scale) + mod_shift).astype(jnp.bfloat16)


def spatial_rows(queries, key_all, value_all, tile_list, first_tile, count_here):
    scaling = 1.0 / math.sqrt(HD)
    local_tiles = queries.shape[0] // TILE
    buffer_tiles = key_all.shape[0] // TILE
    query_tiles = queries.reshape(local_tiles, TILE, HEADS, HD)
    key_tiles = key_all.reshape(buffer_tiles, TILE, HEADS, HD)
    value_tiles = value_all.reshape(buffer_tiles, TILE, HEADS, HD)
    local_list = tile_list - first_tile
    key_near = jnp.take(key_tiles, local_list, axis=0).reshape(local_tiles, NBR * TILE, HEADS, HD)
    value_near = jnp.take(value_tiles, local_list, axis=0).reshape(
        local_tiles, NBR * TILE, HEADS, HD
    )
    key_pos = (
        tile_list[:, :, None] * TILE + jnp.arange(TILE, dtype=jnp.int32)[None, None, :]
    ).reshape(local_tiles, NBR * TILE)
    live_mask = (key_pos < count_here)[:, None, None, :]
    scores = (
        jnp.einsum("tqhd,tkhd->thqk", query_tiles, key_near, preferred_element_type=jnp.float32)
        * scaling
    )
    scores = jnp.where(live_mask, scores, -1e30)
    row_max = jnp.max(scores, axis=-1, keepdims=True)
    exp_terms = jnp.where(live_mask, jnp.exp(scores - row_max), 0.0)
    denominator = jnp.sum(exp_terms, axis=-1, keepdims=True)
    weights = exp_terms.astype(jnp.bfloat16)
    summed = jnp.einsum("thqk,tkhd->tqhd", weights, value_near, preferred_element_type=jnp.float32)
    result = summed / jnp.transpose(denominator, (0, 2, 1, 3))
    return result.astype(jnp.bfloat16).reshape(queries.shape[0], queries.shape[1])


def temporal_block(query_part, key_part, spatial_part, clip_counts, first_pos):
    n_frames, per_dev = query_part.shape[0], query_part.shape[1]
    scaling = 1.0 / math.sqrt(HD)
    position = first_pos + jnp.arange(per_dev, dtype=jnp.int32)
    live_mask = (position[:, None] < clip_counts[None, :])[:, None, None, :]
    scores = (
        jnp.einsum(
            "fphd,gphd->phfg", query_part, key_part, preferred_element_type=jnp.float32
        )
        * scaling
    )
    scores = jnp.where(live_mask, scores, -1e30)
    row_max = jnp.max(scores, axis=-1, keepdims=True)
    exp_terms = jnp.where(live_mask, jnp.exp(scores - row_max), 0.0)
    denominator = jnp.sum(exp_terms, axis=-1, keepdims=True)
    weights = exp_terms.astype(jnp.bfloat16)
    summed = jnp.einsum(
        "phfg,gphd->fphd", weights, spatial_part, preferred_element_type=jnp.float32
    )
    result = summed / jnp.transpose(denominator, (2, 0, 1, 3))
    return result.astype(jnp.bfloat16)


def local(tokens, mod_scale, mod_shift, w_qkv, w_out, neighbors, counts):
    tok_count = tokens.shape[1]
    feat_count = tokens.shape[2]
    n_frames = lax.axis_size("frame")
    own = tokens[0]
    above = passed_along(own, "piece", 1)
    below = passed_along(own, "piece", -1)
    w_full = lax.all_gather(w_qkv, "fsdp", axis=1, tiled=True)
    w_out_full = lax.all_gather(w_out, "fsdp", axis=0, tiled=True)
    normed = layer_norm(own, mod_scale[0], mod_shift[0])
    normed_rim = layer_norm(jnp.concatenate([above, below], axis=0), mod_scale[0], mod_shift[0])
    qkv = jnp.dot(normed, w_full, preferred_element_type=jnp.float32).astype(jnp.bfloat16)
    kv_rim = jnp.dot(
        normed_rim, w_full[:, feat_count:], preferred_element_type=jnp.float32
    ).astype(jnp.bfloat16)
    queries = qkv[:, :feat_count]
    key_proj = qkv[:, feat_count : 2 * feat_count]
    values = qkv[:, 2 * feat_count :]
    frame_index = lax.axis_index("frame")
    piece_index = lax.axis_index("piece")
    clip_counts = counts[0]
    count_here = lax.dynamic_index_in_dim(clip_counts, frame_index, 0, keepdims=False)
    rows_here = tok_count // (TGW * TILE)
    key_all = jnp.concatenate(
        [kv_rim[:tok_count, :feat_count], key_proj, kv_rim[tok_count:, :feat_count]], axis=0
    )
    value_all = jnp.concatenate(
        [kv_rim[:tok_count, feat_count:], values, kv_rim[tok_count:, feat_count:]], axis=0
    )
    first_tile = (piece_index * rows_here - 1) * TGW
    spatial = spatial_rows(queries, key_all, value_all, neighbors[0], first_tile, count_here)
    head_shape = (1, tok_count, HEADS, HD)
    query_part = lax.all_to_all(
        queries.reshape(head_shape), "frame", split_axis=1, concat_axis=0, tiled=True
    )
    key_part = lax.all_to_all(
        key_proj.reshape(head_shape), "frame", split_axis=1, concat_axis=0, tiled=True
    )
    spatial_part = lax.all_to_all(
        spatial.reshape(head_shape), "frame", split_axis=1, concat_axis=0, tiled=True
    )
    per_dev = tok_count // n_frames
    first_pos = piece_index * tok_count + frame_index * per_dev
    temporal = temporal_block(query_part, key_part, spatial_part, clip_counts, first_pos)
    returned = lax.all_to_all(temporal, "frame", split_axis=0, concat_axis=1, tiled=True)
    flat_temporal = returned.reshape(tok_count, feat_count)
    projected = jnp.dot(flat_temporal, w_out_full, preferred_element_type=jnp.float32)
    return projected.astype(jnp.bfloat16).reshape(1, tok_count, feat_count)


def solution(mesh):
    n_fsdp = mesh.shape["fsdp"]
    n_sp = mesh.shape["sp"]
    split = Mesh(
        mesh.devices.reshape(n_fsdp, PIECES, n_sp // PIECES), ("fsdp", "piece", "frame")
    )
    seq = ("piece", "frame")
    placed = (
        P("fsdp", seq, None),
        P("fsdp", None),
        P("fsdp", None),
        P(None, "fsdp"),
        P("fsdp", None),
        P("fsdp", seq, None),
        P("fsdp", None),
    )
    return jax.shard_map(
        local, mesh=split, in_specs=placed, out_specs=P("fsdp", seq, None), check_vma=False
    )
```

```python
import math

import jax
import jax.numpy as jnp
from jax import lax
from jax.experimental import pallas as pl
from jax.experimental.pallas import tpu as pltpu
from jax.sharding import Mesh
from jax.sharding import PartitionSpec as P

HEADS = 12
HD = 128
TILE = 128
TGW = 5
NBR = 6
PIECES = 4


def passed_along(block, axis, distance):
    devices = range(lax.axis_size(axis))
    route = [(i - distance, i) for i in devices if i - distance in devices]
    return lax.ppermute(block, axis, route)


def layer_norm(tokens, mod_scale, mod_shift):
    values_f32 = tokens.astype(jnp.float32)
    center = jnp.mean(values_f32, axis=-1, keepdims=True)
    spread = jnp.mean((values_f32 - center) ** 2, axis=-1, keepdims=True)
    normal = (values_f32 - center) / jnp.sqrt(spread + 1e-06)
    return (normal * (1.0 + mod_scale) + mod_shift).astype(jnp.bfloat16)


def spatial_kernel(list_ref, scalar_ref, q_ref, k_ref, v_ref, o_ref):
    scaling = 1.0 / math.sqrt(HD)
    first_tile = scalar_ref[0]
    count_here = scalar_ref[1]
    local_tiles = q_ref.shape[0] // TILE
    for t in range(local_tiles):
        query = q_ref[t * TILE : (t + 1) * TILE, :]
        parts = []
        row_max = None
        for n in range(NBR):
            tile_id = list_ref[t * NBR + n]
            start = pl.multiple_of((tile_id - first_tile) * TILE, TILE)
            key = k_ref[pl.ds(start, TILE), :]
            scores = (
                lax.dot_general(
                    query, key, (((1,), (1,)), ((), ())), preferred_element_type=jnp.float32
                )
                * scaling
            )
            key_pos = tile_id * TILE + lax.broadcasted_iota(jnp.int32, scores.shape, 1)
            live = key_pos < count_here
            scores = jnp.where(live, scores, -1e30)
            part_max = jnp.max(scores, axis=-1, keepdims=True)
            row_max = part_max if row_max is None else jnp.maximum(row_max, part_max)
            parts.append((scores, live, start))
        denominator = None
        summed = None
        for scores, live, start in parts:
            exp_terms = jnp.where(live, jnp.exp(scores - row_max), 0.0)
            part_sum = jnp.sum(exp_terms, axis=-1, keepdims=True)
            value = v_ref[pl.ds(start, TILE), :]
            part_out = jnp.dot(
                exp_terms.astype(jnp.bfloat16), value, preferred_element_type=jnp.float32
            )
            denominator = part_sum if denominator is None else denominator + part_sum
            summed = part_out if summed is None else summed + part_out
        o_ref[t * TILE : (t + 1) * TILE, :] = (summed / denominator).astype(o_ref.dtype)


def spatial_rows(queries, kv_all, tile_list, first_tile, count_here):
    rows, feat = queries.shape
    buffer_rows = kv_all.shape[0]
    scalars = jnp.stack([first_tile, count_here]).astype(jnp.int32)
    grid_spec = pltpu.PrefetchScalarGridSpec(
        num_scalar_prefetch=2,
        grid=(HEADS,),
        in_specs=[
            pl.BlockSpec((rows, HD), lambda h, lst, sc: (0, h)),
            pl.BlockSpec((buffer_rows, HD), lambda h, lst, sc: (0, h)),
            pl.BlockSpec((buffer_rows, HD), lambda h, lst, sc: (0, HEADS + h)),
        ],
        out_specs=pl.BlockSpec((rows, HD), lambda h, lst, sc: (0, h)),
    )
    flops = 4 * rows * NBR * TILE * feat
    return pl.pallas_call(
        spatial_kernel,
        grid_spec=grid_spec,
        out_shape=jax.ShapeDtypeStruct((rows, feat), jnp.bfloat16),
        cost_estimate=pl.CostEstimate(
            flops=flops,
            transcendentals=rows * NBR * TILE * HEADS,
            bytes_accessed=2 * (rows * feat * 2 + buffer_rows * feat * 2),
        ),
    )(tile_list.reshape(-1).astype(jnp.int32), scalars, queries, kv_all, kv_all)


def temporal_block(query_part, key_part, spatial_part, clip_counts, first_pos):
    n_frames, per_dev = query_part.shape[0], query_part.shape[1]
    scaling = 1.0 / math.sqrt(HD)
    position = first_pos + jnp.arange(per_dev, dtype=jnp.int32)
    live_mask = (position[:, None] < clip_counts[None, :])[:, None, None, :]
    scores = (
        jnp.einsum(
            "fphd,gphd->phfg", query_part, key_part, preferred_element_type=jnp.float32
        )
        * scaling
    )
    scores = jnp.where(live_mask, scores, -1e30)
    row_max = jnp.max(scores, axis=-1, keepdims=True)
    exp_terms = jnp.where(live_mask, jnp.exp(scores - row_max), 0.0)
    denominator = jnp.sum(exp_terms, axis=-1, keepdims=True)
    weights = exp_terms.astype(jnp.bfloat16)
    summed = jnp.einsum(
        "phfg,gphd->fphd", weights, spatial_part, preferred_element_type=jnp.float32
    )
    result = summed / jnp.transpose(denominator, (2, 0, 1, 3))
    return result.astype(jnp.bfloat16)


def local(tokens, mod_scale, mod_shift, w_qkv, w_out, neighbors, counts):
    tok_count = tokens.shape[1]
    feat_count = tokens.shape[2]
    n_frames = lax.axis_size("frame")
    own = tokens[0]
    above = passed_along(own, "piece", 1)
    below = passed_along(own, "piece", -1)
    w_full = lax.all_gather(w_qkv, "fsdp", axis=1, tiled=True)
    w_out_full = lax.all_gather(w_out, "fsdp", axis=0, tiled=True)
    normed_all = layer_norm(
        jnp.concatenate([above, own, below], axis=0), mod_scale[0], mod_shift[0]
    )
    queries = jnp.dot(
        normed_all[tok_count : 2 * tok_count],
        w_full[:, :feat_count],
        preferred_element_type=jnp.float32,
    ).astype(jnp.bfloat16)
    kv_all = jnp.dot(
        normed_all, w_full[:, feat_count:], preferred_element_type=jnp.float32
    ).astype(jnp.bfloat16)
    key_proj = kv_all[tok_count : 2 * tok_count, :feat_count]
    frame_index = lax.axis_index("frame")
    piece_index = lax.axis_index("piece")
    clip_counts = counts[0]
    count_here = lax.dynamic_index_in_dim(clip_counts, frame_index, 0, keepdims=False)
    rows_here = tok_count // (TGW * TILE)
    first_tile = (piece_index * rows_here - 1) * TGW
    spatial = spatial_rows(queries, kv_all, neighbors[0], first_tile, count_here)
    head_shape = (1, tok_count, HEADS, HD)
    query_part = lax.all_to_all(
        queries.reshape(head_shape), "frame", split_axis=1, concat_axis=0, tiled=True
    )
    key_part = lax.all_to_all(
        key_proj.reshape(head_shape), "frame", split_axis=1, concat_axis=0, tiled=True
    )
    spatial_part = lax.all_to_all(
        spatial.reshape(head_shape), "frame", split_axis=1, concat_axis=0, tiled=True
    )
    per_dev = tok_count // n_frames
    first_pos = piece_index * tok_count + frame_index * per_dev
    temporal = temporal_block(query_part, key_part, spatial_part, clip_counts, first_pos)
    returned = lax.all_to_all(temporal, "frame", split_axis=0, concat_axis=1, tiled=True)
    flat_temporal = returned.reshape(tok_count, feat_count)
    projected = jnp.dot(flat_temporal, w_out_full, preferred_element_type=jnp.float32)
    return projected.astype(jnp.bfloat16).reshape(1, tok_count, feat_count)


def solution(mesh):
    n_fsdp = mesh.shape["fsdp"]
    n_sp = mesh.shape["sp"]
    split = Mesh(
        mesh.devices.reshape(n_fsdp, PIECES, n_sp // PIECES), ("fsdp", "piece", "frame")
    )
    seq = ("piece", "frame")
    placed = (
        P("fsdp", seq, None),
        P("fsdp", None),
        P("fsdp", None),
        P(None, "fsdp"),
        P("fsdp", None),
        P("fsdp", seq, None),
        P("fsdp", None),
    )
    return jax.shard_map(
        local, mesh=split, in_specs=placed, out_specs=P("fsdp", seq, None), check_vma=False
    )
```

```python
import math

import jax
import jax.numpy as jnp
from jax import lax
from jax.experimental import pallas as pl
from jax.experimental.pallas import tpu as pltpu
from jax.sharding import Mesh
from jax.sharding import PartitionSpec as P

HEADS = 12
HD = 128
TILE = 128
TGW = 5
NBR = 6
PIECES = 4


def passed_along(block, axis, distance):
    devices = range(lax.axis_size(axis))
    route = [(i - distance, i) for i in devices if i - distance in devices]
    return lax.ppermute(block, axis, route)


def layer_norm(tokens, mod_scale, mod_shift):
    values_f32 = tokens.astype(jnp.float32)
    center = jnp.mean(values_f32, axis=-1, keepdims=True)
    spread = jnp.mean((values_f32 - center) ** 2, axis=-1, keepdims=True)
    normal = (values_f32 - center) / jnp.sqrt(spread + 1e-06)
    return (normal * (1.0 + mod_scale) + mod_shift).astype(jnp.bfloat16)


def spatial_kernel(list_ref, scalar_ref, q_ref, k_ref, v_ref, o_ref):
    scaling = 1.0 / math.sqrt(HD)
    first_tile = scalar_ref[0]
    count_here = scalar_ref[1]
    local_tiles = q_ref.shape[0] // TILE
    for t in range(local_tiles):
        query = q_ref[t * TILE : (t + 1) * TILE, :]
        parts = []
        row_max = None
        for n in range(NBR):
            tile_id = list_ref[t * NBR + n]
            start = pl.multiple_of((tile_id - first_tile) * TILE, TILE)
            key = k_ref[pl.ds(start, TILE), :]
            scores = (
                lax.dot_general(
                    query, key, (((1,), (1,)), ((), ())), preferred_element_type=jnp.float32
                )
                * scaling
            )
            key_pos = tile_id * TILE + lax.broadcasted_iota(jnp.int32, scores.shape, 1)
            live = key_pos < count_here
            scores = jnp.where(live, scores, -1e30)
            part_max = jnp.max(scores, axis=-1, keepdims=True)
            row_max = part_max if row_max is None else jnp.maximum(row_max, part_max)
            parts.append((scores, live, start))
        denominator = None
        summed = None
        for scores, live, start in parts:
            exp_terms = jnp.where(live, jnp.exp(scores - row_max), 0.0)
            part_sum = jnp.sum(exp_terms, axis=-1, keepdims=True)
            value = v_ref[pl.ds(start, TILE), :]
            part_out = jnp.dot(
                exp_terms.astype(jnp.bfloat16), value, preferred_element_type=jnp.float32
            )
            denominator = part_sum if denominator is None else denominator + part_sum
            summed = part_out if summed is None else summed + part_out
        o_ref[t * TILE : (t + 1) * TILE, :] = (summed / denominator).astype(o_ref.dtype)


def spatial_rows(queries, kv_all, tile_list, first_tile, count_here):
    rows, feat = queries.shape
    buffer_rows = kv_all.shape[0]
    scalars = jnp.stack([first_tile, count_here]).astype(jnp.int32)
    grid_spec = pltpu.PrefetchScalarGridSpec(
        num_scalar_prefetch=2,
        grid=(HEADS,),
        in_specs=[
            pl.BlockSpec((rows, HD), lambda h, lst, sc: (0, h)),
            pl.BlockSpec((buffer_rows, HD), lambda h, lst, sc: (0, h)),
            pl.BlockSpec((buffer_rows, HD), lambda h, lst, sc: (0, HEADS + h)),
        ],
        out_specs=pl.BlockSpec((rows, HD), lambda h, lst, sc: (0, h)),
    )
    flops = 4 * rows * NBR * TILE * feat
    return pl.pallas_call(
        spatial_kernel,
        grid_spec=grid_spec,
        out_shape=jax.ShapeDtypeStruct((rows, feat), jnp.bfloat16),
        cost_estimate=pl.CostEstimate(
            flops=flops,
            transcendentals=rows * NBR * TILE * HEADS,
            bytes_accessed=2 * (rows * feat * 2 + buffer_rows * feat * 2),
        ),
    )(tile_list.reshape(-1).astype(jnp.int32), scalars, queries, kv_all, kv_all)


def temporal_block(query_part, key_part, spatial_part, clip_counts, first_pos):
    n_frames, per_dev = query_part.shape[0], query_part.shape[1]
    scaling = 1.0 / math.sqrt(HD)
    position = first_pos + jnp.arange(per_dev, dtype=jnp.int32)
    live_mask = (position[:, None] < clip_counts[None, :])[:, None, None, :]
    scores = (
        jnp.einsum(
            "fphd,gphd->phfg", query_part, key_part, preferred_element_type=jnp.float32
        )
        * scaling
    )
    scores = jnp.where(live_mask, scores, -1e30)
    row_max = jnp.max(scores, axis=-1, keepdims=True)
    exp_terms = jnp.where(live_mask, jnp.exp(scores - row_max), 0.0)
    denominator = jnp.sum(exp_terms, axis=-1, keepdims=True)
    weights = exp_terms.astype(jnp.bfloat16)
    summed = jnp.einsum(
        "phfg,gphd->fphd", weights, spatial_part, preferred_element_type=jnp.float32
    )
    result = summed / jnp.transpose(denominator, (2, 0, 1, 3))
    return result.astype(jnp.bfloat16)


def local(tokens, mod_scale, mod_shift, w_qkv, w_out, neighbors, counts):
    tok_count = tokens.shape[1]
    feat_count = tokens.shape[2]
    n_frames = lax.axis_size("fy") * lax.axis_size("core")
    own = tokens[0]
    above = passed_along(own, "piece", 1)
    below = passed_along(own, "piece", -1)
    core = lax.axis_index("core")
    half_rows = w_qkv.shape[0] // 2
    w_half = lax.dynamic_slice_in_dim(w_qkv, core * half_rows, half_rows, axis=0)
    w_half = lax.all_gather(w_half, "fsdp", axis=1, tiled=True)
    w_full = lax.all_gather(w_half, "core", axis=0, tiled=True)
    out_rows = w_out.shape[0] // 2
    w_out_half = lax.dynamic_slice_in_dim(w_out, core * out_rows, out_rows, axis=0)
    w_out_half = lax.all_gather(w_out_half, "core", axis=0, tiled=True)
    w_out_full = lax.all_gather(w_out_half, "fsdp", axis=0, tiled=True)
    normed_all = layer_norm(
        jnp.concatenate([above, own, below], axis=0), mod_scale[0], mod_shift[0]
    )
    queries = jnp.dot(
        normed_all[tok_count : 2 * tok_count],
        w_full[:, :feat_count],
        preferred_element_type=jnp.float32,
    ).astype(jnp.bfloat16)
    kv_all = jnp.dot(
        normed_all, w_full[:, feat_count:], preferred_element_type=jnp.float32
    ).astype(jnp.bfloat16)
    key_proj = kv_all[tok_count : 2 * tok_count, :feat_count]
    frame_index = lax.axis_index("fy") * lax.axis_size("core") + lax.axis_index("core")
    piece_index = lax.axis_index("piece")
    clip_counts = counts[0]
    count_here = lax.dynamic_index_in_dim(clip_counts, frame_index, 0, keepdims=False)
    rows_here = tok_count // (TGW * TILE)
    first_tile = (piece_index * rows_here - 1) * TGW
    spatial = spatial_rows(queries, kv_all, neighbors[0], first_tile, count_here)
    head_shape = (1, tok_count, HEADS, HD)
    frame_axes = ("fy", "core")
    qk_part = lax.all_to_all(
        jnp.stack([queries, key_proj]).reshape((2,) + head_shape),
        frame_axes,
        split_axis=2,
        concat_axis=1,
        tiled=True,
    )
    query_part, key_part = qk_part[0], qk_part[1]
    spatial_part = lax.all_to_all(
        spatial.reshape(head_shape), frame_axes, split_axis=1, concat_axis=0, tiled=True
    )
    per_dev = tok_count // n_frames
    first_pos = piece_index * tok_count + frame_index * per_dev
    temporal = temporal_block(query_part, key_part, spatial_part, clip_counts, first_pos)
    returned = lax.all_to_all(temporal, frame_axes, split_axis=0, concat_axis=1, tiled=True)
    flat_temporal = returned.reshape(tok_count, feat_count)
    projected = jnp.dot(flat_temporal, w_out_full, preferred_element_type=jnp.float32)
    return projected.astype(jnp.bfloat16).reshape(1, tok_count, feat_count)


def solution(mesh):
    n_fsdp = mesh.shape["fsdp"]
    n_sp = mesh.shape["sp"]
    split = Mesh(
        mesh.devices.reshape(n_fsdp, PIECES, n_sp // PIECES // 2, 2),
        ("fsdp", "piece", "fy", "core"),
    )
    seq = ("piece", "fy", "core")
    placed = (
        P("fsdp", seq, None),
        P("fsdp", None),
        P("fsdp", None),
        P(None, "fsdp"),
        P("fsdp", None),
        P("fsdp", seq, None),
        P("fsdp", None),
    )
    return jax.shard_map(
        local, mesh=split, in_specs=placed, out_specs=P("fsdp", seq, None), check_vma=False
    )
```

```python
import math

import jax
import jax.numpy as jnp
from jax import lax
from jax.experimental import pallas as pl
from jax.experimental.pallas import tpu as pltpu
from jax.sharding import Mesh
from jax.sharding import PartitionSpec as P

HEADS = 12
HD = 128
TILE = 128
TGW = 5
NBR = 6
PIECES = 4


def passed_along(block, axis, distance):
    devices = range(lax.axis_size(axis))
    route = [(i - distance, i) for i in devices if i - distance in devices]
    return lax.ppermute(block, axis, route)


def layer_norm(tokens, mod_scale, mod_shift):
    values_f32 = tokens.astype(jnp.float32)
    center = jnp.mean(values_f32, axis=-1, keepdims=True)
    spread = jnp.mean((values_f32 - center) ** 2, axis=-1, keepdims=True)
    normal = (values_f32 - center) / jnp.sqrt(spread + 1e-06)
    return (normal * (1.0 + mod_scale) + mod_shift).astype(jnp.bfloat16)


def spatial_kernel(list_ref, scalar_ref, q_ref, k_ref, v_ref, o_ref):
    scaling = 1.0 / math.sqrt(HD)
    first_tile = scalar_ref[0]
    count_here = scalar_ref[1]
    local_tiles = q_ref.shape[0] // TILE
    for t in range(local_tiles):
        query = q_ref[t * TILE : (t + 1) * TILE, :]
        parts = []
        row_max = None
        for n in range(NBR):
            tile_id = list_ref[t * NBR + n]
            start = pl.multiple_of((tile_id - first_tile) * TILE, TILE)
            key = k_ref[pl.ds(start, TILE), :]
            scores = (
                lax.dot_general(
                    query, key, (((1,), (1,)), ((), ())), preferred_element_type=jnp.float32
                )
                * scaling
            )
            key_pos = tile_id * TILE + lax.broadcasted_iota(jnp.int32, scores.shape, 1)
            live = key_pos < count_here
            scores = jnp.where(live, scores, -1e30)
            part_max = jnp.max(scores, axis=-1, keepdims=True)
            row_max = part_max if row_max is None else jnp.maximum(row_max, part_max)
            parts.append((scores, live, start))
        denominator = None
        summed = None
        for scores, live, start in parts:
            exp_terms = jnp.where(live, jnp.exp(scores - row_max), 0.0)
            part_sum = jnp.sum(exp_terms, axis=-1, keepdims=True)
            value = v_ref[pl.ds(start, TILE), :]
            part_out = jnp.dot(
                exp_terms.astype(jnp.bfloat16), value, preferred_element_type=jnp.float32
            )
            denominator = part_sum if denominator is None else denominator + part_sum
            summed = part_out if summed is None else summed + part_out
        o_ref[t * TILE : (t + 1) * TILE, :] = (summed / denominator).astype(o_ref.dtype)


def spatial_rows(qkv_all, tile_list, first_tile, count_here):
    buffer_rows = qkv_all.shape[0]
    rows, feat = buffer_rows // 3, qkv_all.shape[1] // 3
    scalars = jnp.stack([first_tile, count_here]).astype(jnp.int32)
    grid_spec = pltpu.PrefetchScalarGridSpec(
        num_scalar_prefetch=2,
        grid=(HEADS,),
        in_specs=[
            pl.BlockSpec((rows, HD), lambda h, lst, sc: (1, h)),
            pl.BlockSpec((buffer_rows, HD), lambda h, lst, sc: (0, HEADS + h)),
            pl.BlockSpec((buffer_rows, HD), lambda h, lst, sc: (0, 2 * HEADS + h)),
        ],
        out_specs=pl.BlockSpec((rows, HD), lambda h, lst, sc: (0, h)),
    )
    flops = 4 * rows * NBR * TILE * feat
    return pl.pallas_call(
        spatial_kernel,
        grid_spec=grid_spec,
        out_shape=jax.ShapeDtypeStruct((rows, feat), jnp.bfloat16),
        cost_estimate=pl.CostEstimate(
            flops=flops,
            transcendentals=rows * NBR * TILE * HEADS,
            bytes_accessed=2 * (rows * feat * 2 + buffer_rows * feat * 2),
        ),
    )(tile_list.reshape(-1).astype(jnp.int32), scalars, qkv_all, qkv_all, qkv_all)


MESH_IDS = pl.DeviceIdType.MESH


def rim_kernel(tok_ref, rim_ref, send_sem, recv_sem):
    n_piece = lax.axis_size("piece")
    piece = lax.axis_index("piece")
    here = (lax.axis_index("fsdp"), piece, lax.axis_index("fy"), lax.axis_index("core"))
    up = (here[0], piece - 1, here[2], here[3])
    down = (here[0], piece + 1, here[2], here[3])
    has_up = piece > 0
    has_down = piece < n_piece - 1
    barrier = pltpu.get_barrier_semaphore()

    @pl.when(has_up)
    def _():
        pl.semaphore_signal(barrier, inc=1, device_id=up, device_id_type=MESH_IDS)

    @pl.when(has_down)
    def _():
        pl.semaphore_signal(barrier, inc=1, device_id=down, device_id_type=MESH_IDS)

    peers = (piece + n_piece - 1) // n_piece + (2 * n_piece - 2 - piece) // n_piece
    pl.semaphore_wait(barrier, peers)

    to_down = pltpu.make_async_remote_copy(
        src_ref=tok_ref,
        dst_ref=rim_ref.at[0],
        send_sem=send_sem.at[0],
        recv_sem=recv_sem.at[0],
        device_id=down,
        device_id_type=MESH_IDS,
    )
    to_up = pltpu.make_async_remote_copy(
        src_ref=tok_ref,
        dst_ref=rim_ref.at[1],
        send_sem=send_sem.at[1],
        recv_sem=recv_sem.at[1],
        device_id=up,
        device_id_type=MESH_IDS,
    )

    @pl.when(has_down)
    def _():
        to_down.start()

    @pl.when(has_up)
    def _():
        to_up.start()

    @pl.when(has_down)
    def _():
        to_down.wait_send()
        to_up.wait_recv()

    @pl.when(has_up)
    def _():
        to_up.wait_send()
        to_down.wait_recv()


def exchange_rims(own):
    rows, feat = own.shape
    return pl.pallas_call(
        rim_kernel,
        out_shape=jax.ShapeDtypeStruct((2, rows, feat), own.dtype),
        in_specs=[pl.BlockSpec(memory_space=pl.ANY)],
        out_specs=pl.BlockSpec(memory_space=pl.ANY),
        scratch_shapes=[pltpu.SemaphoreType.DMA((2,)), pltpu.SemaphoreType.DMA((2,))],
        compiler_params=pltpu.CompilerParams(collective_id=0, has_side_effects=True),
        cost_estimate=pl.CostEstimate(flops=0, transcendentals=0, bytes_accessed=80 * rows * feat * 2),
    )(own)


def temporal_block(query_part, key_part, spatial_part, clip_counts, first_pos):
    n_frames, per_dev = query_part.shape[0], query_part.shape[1]
    scaling = 1.0 / math.sqrt(HD)
    position = first_pos + jnp.arange(per_dev, dtype=jnp.int32)
    live_mask = (position[:, None] < clip_counts[None, :])[:, None, None, :]
    scores = (
        jnp.einsum(
            "fphd,gphd->phfg", query_part, key_part, preferred_element_type=jnp.float32
        )
        * scaling
    )
    scores = jnp.where(live_mask, scores, -1e30)
    row_max = jnp.max(scores, axis=-1, keepdims=True)
    exp_terms = jnp.where(live_mask, jnp.exp(scores - row_max), 0.0)
    denominator = jnp.sum(exp_terms, axis=-1, keepdims=True)
    weights = exp_terms.astype(jnp.bfloat16)
    summed = jnp.einsum(
        "phfg,gphd->fphd", weights, spatial_part, preferred_element_type=jnp.float32
    )
    result = summed / jnp.transpose(denominator, (2, 0, 1, 3))
    return result.astype(jnp.bfloat16)


def local(tokens, mod_scale, mod_shift, w_qkv, w_out, neighbors, counts):
    tok_count = tokens.shape[1]
    feat_count = tokens.shape[2]
    n_frames = lax.axis_size("fy") * lax.axis_size("core")
    own = tokens[0]
    rims = exchange_rims(own)
    piece_index = lax.axis_index("piece")
    above = jnp.where(piece_index > 0, rims[0], jnp.zeros_like(own))
    below = jnp.where(piece_index < lax.axis_size("piece") - 1, rims[1], jnp.zeros_like(own))
    core = lax.axis_index("core")
    half_rows = w_qkv.shape[0] // 2
    w_half = lax.dynamic_slice_in_dim(w_qkv, core * half_rows, half_rows, axis=0)
    w_pieces = lax.all_gather(w_half, ("fsdp", "core"), axis=0, tiled=False)
    w_full = w_pieces.reshape(lax.axis_size("fsdp"), w_qkv.shape[0], w_qkv.shape[1])
    out_rows = w_out.shape[0] // 2
    w_out_half = lax.dynamic_slice_in_dim(w_out, core * out_rows, out_rows, axis=0)
    w_out_half = lax.all_gather(w_out_half, "core", axis=0, tiled=True)
    w_out_full = lax.all_gather(w_out_half, "fsdp", axis=0, tiled=True)
    normed_all = layer_norm(
        jnp.concatenate([above, own, below], axis=0), mod_scale[0], mod_shift[0]
    )
    qkv_all = jnp.einsum(
        "tk,jkc->tjc", normed_all, w_full, preferred_element_type=jnp.float32
    ).astype(jnp.bfloat16).reshape(normed_all.shape[0], 3 * feat_count)
    queries = qkv_all[tok_count : 2 * tok_count, :feat_count]
    key_proj = qkv_all[tok_count : 2 * tok_count, feat_count : 2 * feat_count]
    frame_index = lax.axis_index("fy") * lax.axis_size("core") + lax.axis_index("core")
    piece_index = lax.axis_index("piece")
    clip_counts = counts[0]
    count_here = lax.dynamic_index_in_dim(clip_counts, frame_index, 0, keepdims=False)
    rows_here = tok_count // (TGW * TILE)
    first_tile = (piece_index * rows_here - 1) * TGW
    spatial = spatial_rows(qkv_all, neighbors[0], first_tile, count_here)
    head_shape = (1, tok_count, HEADS, HD)
    frame_axes = ("fy", "core")
    qk_part = lax.all_to_all(
        jnp.stack([queries, key_proj]).reshape((2,) + head_shape),
        frame_axes,
        split_axis=2,
        concat_axis=1,
        tiled=True,
    )
    query_part, key_part = qk_part[0], qk_part[1]
    spatial_part = lax.all_to_all(
        spatial.reshape(head_shape), frame_axes, split_axis=1, concat_axis=0, tiled=True
    )
    per_dev = tok_count // n_frames
    first_pos = piece_index * tok_count + frame_index * per_dev
    temporal = temporal_block(query_part, key_part, spatial_part, clip_counts, first_pos)
    returned = lax.all_to_all(temporal, frame_axes, split_axis=0, concat_axis=1, tiled=True)
    flat_temporal = returned.reshape(tok_count, feat_count)
    projected = jnp.dot(flat_temporal, w_out_full, preferred_element_type=jnp.float32)
    return projected.astype(jnp.bfloat16).reshape(1, tok_count, feat_count)


def solution(mesh):
    n_fsdp = mesh.shape["fsdp"]
    n_sp = mesh.shape["sp"]
    split = Mesh(
        mesh.devices.reshape(n_fsdp, PIECES, n_sp // PIECES // 2, 2),
        ("fsdp", "piece", "fy", "core"),
    )
    seq = ("piece", "fy", "core")
    placed = (
        P("fsdp", seq, None),
        P("fsdp", None),
        P("fsdp", None),
        P(None, "fsdp"),
        P("fsdp", None),
        P("fsdp", seq, None),
        P("fsdp", None),
    )
    return jax.shard_map(
        local, mesh=split, in_specs=placed, out_specs=P("fsdp", seq, None), check_vma=False
    )
```

```python
import math

import jax
import jax.numpy as jnp
from jax import lax
from jax.experimental import pallas as pl
from jax.experimental.pallas import tpu as pltpu
from jax.sharding import Mesh
from jax.sharding import PartitionSpec as P

HEADS = 12
HD = 128
TILE = 128
TGW = 5
NBR = 6
PIECES = 4


def passed_along(block, axis, distance):
    devices = range(lax.axis_size(axis))
    route = [(i - distance, i) for i in devices if i - distance in devices]
    return lax.ppermute(block, axis, route)


def layer_norm(tokens, mod_scale, mod_shift):
    values_f32 = tokens.astype(jnp.float32)
    center = jnp.mean(values_f32, axis=-1, keepdims=True)
    spread = jnp.mean((values_f32 - center) ** 2, axis=-1, keepdims=True)
    normal = (values_f32 - center) / jnp.sqrt(spread + 1e-06)
    return (normal * (1.0 + mod_scale) + mod_shift).astype(jnp.bfloat16)


def spatial_kernel(list_ref, scalar_ref, q_ref, k_ref, v_ref, o_ref):
    scaling = 1.0 / math.sqrt(HD)
    first_tile = scalar_ref[0]
    count_here = scalar_ref[1]
    local_tiles = q_ref.shape[0] // TILE
    for t in range(local_tiles):
        query = q_ref[t * TILE : (t + 1) * TILE, :]
        parts = []
        row_max = None
        for n in range(NBR):
            tile_id = list_ref[t * NBR + n]
            start = pl.multiple_of((tile_id - first_tile) * TILE, TILE)
            key = k_ref[pl.ds(start, TILE), :]
            scores = (
                lax.dot_general(
                    query, key, (((1,), (1,)), ((), ())), preferred_element_type=jnp.float32
                )
                * scaling
            )
            key_pos = tile_id * TILE + lax.broadcasted_iota(jnp.int32, scores.shape, 1)
            live = key_pos < count_here
            scores = jnp.where(live, scores, -1e30)
            part_max = jnp.max(scores, axis=-1, keepdims=True)
            row_max = part_max if row_max is None else jnp.maximum(row_max, part_max)
            parts.append((scores, live, start))
        denominator = None
        summed = None
        for scores, live, start in parts:
            exp_terms = jnp.where(live, jnp.exp(scores - row_max), 0.0)
            part_sum = jnp.sum(exp_terms, axis=-1, keepdims=True)
            value = v_ref[pl.ds(start, TILE), :]
            part_out = jnp.dot(
                exp_terms.astype(jnp.bfloat16), value, preferred_element_type=jnp.float32
            )
            denominator = part_sum if denominator is None else denominator + part_sum
            summed = part_out if summed is None else summed + part_out
        o_ref[t * TILE : (t + 1) * TILE, :] = (summed / denominator).astype(o_ref.dtype)


def spatial_rows(qkv_all, tile_list, first_tile, count_here):
    buffer_rows = qkv_all.shape[1]
    rows, feat = buffer_rows // 3, qkv_all.shape[0] * qkv_all.shape[2] // 3
    per_shard = qkv_all.shape[2] // HD
    scalars = jnp.stack([first_tile, count_here]).astype(jnp.int32)
    grid_spec = pltpu.PrefetchScalarGridSpec(
        num_scalar_prefetch=2,
        grid=(HEADS,),
        in_specs=[
            pl.BlockSpec(
                (None, rows, HD), lambda h, lst, sc: (h // per_shard, 1, h % per_shard)
            ),
            pl.BlockSpec(
                (None, buffer_rows, HD),
                lambda h, lst, sc: ((HEADS + h) // per_shard, 0, (HEADS + h) % per_shard),
            ),
            pl.BlockSpec(
                (None, buffer_rows, HD),
                lambda h, lst, sc: ((2 * HEADS + h) // per_shard, 0, (2 * HEADS + h) % per_shard),
            ),
        ],
        out_specs=pl.BlockSpec((rows, HD), lambda h, lst, sc: (0, h)),
    )
    flops = 4 * rows * NBR * TILE * feat
    return pl.pallas_call(
        spatial_kernel,
        grid_spec=grid_spec,
        out_shape=jax.ShapeDtypeStruct((rows, feat), jnp.bfloat16),
        cost_estimate=pl.CostEstimate(
            flops=flops,
            transcendentals=rows * NBR * TILE * HEADS,
            bytes_accessed=2 * (rows * feat * 2 + buffer_rows * feat * 2),
        ),
    )(tile_list.reshape(-1).astype(jnp.int32), scalars, qkv_all, qkv_all, qkv_all)


MESH_IDS = pl.DeviceIdType.MESH


def rim_kernel(tok_ref, rim_ref, send_sem, recv_sem):
    n_piece = lax.axis_size("piece")
    piece = lax.axis_index("piece")
    here = (lax.axis_index("fsdp"), piece, lax.axis_index("fy"), lax.axis_index("core"))
    up = (here[0], piece - 1, here[2], here[3])
    down = (here[0], piece + 1, here[2], here[3])
    has_up = piece > 0
    has_down = piece < n_piece - 1
    barrier = pltpu.get_barrier_semaphore()

    @pl.when(has_up)
    def _():
        pl.semaphore_signal(barrier, inc=1, device_id=up, device_id_type=MESH_IDS)

    @pl.when(has_down)
    def _():
        pl.semaphore_signal(barrier, inc=1, device_id=down, device_id_type=MESH_IDS)

    peers = (piece + n_piece - 1) // n_piece + (2 * n_piece - 2 - piece) // n_piece
    pl.semaphore_wait(barrier, peers)

    to_down = pltpu.make_async_remote_copy(
        src_ref=tok_ref,
        dst_ref=rim_ref.at[0],
        send_sem=send_sem.at[0],
        recv_sem=recv_sem.at[0],
        device_id=down,
        device_id_type=MESH_IDS,
    )
    to_up = pltpu.make_async_remote_copy(
        src_ref=tok_ref,
        dst_ref=rim_ref.at[1],
        send_sem=send_sem.at[1],
        recv_sem=recv_sem.at[1],
        device_id=up,
        device_id_type=MESH_IDS,
    )

    @pl.when(has_down)
    def _():
        to_down.start()

    @pl.when(has_up)
    def _():
        to_up.start()

    @pl.when(has_down)
    def _():
        to_down.wait_send()
        to_up.wait_recv()

    @pl.when(has_up)
    def _():
        to_up.wait_send()
        to_down.wait_recv()


def exchange_rims(own):
    rows, feat = own.shape
    return pl.pallas_call(
        rim_kernel,
        out_shape=jax.ShapeDtypeStruct((2, rows, feat), own.dtype),
        in_specs=[pl.BlockSpec(memory_space=pl.ANY)],
        out_specs=pl.BlockSpec(memory_space=pl.ANY),
        scratch_shapes=[pltpu.SemaphoreType.DMA((2,)), pltpu.SemaphoreType.DMA((2,))],
        compiler_params=pltpu.CompilerParams(collective_id=0, has_side_effects=True),
        cost_estimate=pl.CostEstimate(flops=0, transcendentals=0, bytes_accessed=80 * rows * feat * 2),
    )(own)


def temporal_block(query_part, key_part, spatial_part, clip_counts, first_pos):
    n_frames, per_dev = query_part.shape[0], query_part.shape[1]
    scaling = 1.0 / math.sqrt(HD)
    position = first_pos + jnp.arange(per_dev, dtype=jnp.int32)
    live_mask = (position[:, None] < clip_counts[None, :])[:, None, None, :]
    scores = (
        jnp.einsum(
            "fphd,gphd->phfg", query_part, key_part, preferred_element_type=jnp.float32
        )
        * scaling
    )
    scores = jnp.where(live_mask, scores, -1e30)
    row_max = jnp.max(scores, axis=-1, keepdims=True)
    exp_terms = jnp.where(live_mask, jnp.exp(scores - row_max), 0.0)
    denominator = jnp.sum(exp_terms, axis=-1, keepdims=True)
    weights = exp_terms.astype(jnp.bfloat16)
    summed = jnp.einsum(
        "phfg,gphd->fphd", weights, spatial_part, preferred_element_type=jnp.float32
    )
    result = summed / jnp.transpose(denominator, (2, 0, 1, 3))
    return result.astype(jnp.bfloat16)


def local(tokens, mod_scale, mod_shift, w_qkv, w_out, neighbors, counts):
    tok_count = tokens.shape[1]
    feat_count = tokens.shape[2]
    n_frames = lax.axis_size("fy") * lax.axis_size("core")
    own = tokens[0]
    rims = exchange_rims(own)
    piece_index = lax.axis_index("piece")
    above = jnp.where(piece_index > 0, rims[0], jnp.zeros_like(own))
    below = jnp.where(piece_index < lax.axis_size("piece") - 1, rims[1], jnp.zeros_like(own))
    core = lax.axis_index("core")
    half_rows = w_qkv.shape[0] // 2
    w_half = lax.dynamic_slice_in_dim(w_qkv, core * half_rows, half_rows, axis=0)
    w_pieces = lax.all_gather(w_half, ("fsdp", "core"), axis=0, tiled=False)
    w_full = w_pieces.reshape(lax.axis_size("fsdp"), w_qkv.shape[0], w_qkv.shape[1])
    out_rows = w_out.shape[0] // 2
    w_out_half = lax.dynamic_slice_in_dim(w_out, core * out_rows, out_rows, axis=0)
    w_out_half = lax.all_gather(w_out_half, "core", axis=0, tiled=True)
    w_out_full = lax.all_gather(w_out_half, "fsdp", axis=0, tiled=True)
    normed_all = layer_norm(
        jnp.concatenate([above, own, below], axis=0), mod_scale[0], mod_shift[0]
    )
    qkv_all = jnp.einsum(
        "tk,jkc->jtc", normed_all, w_full, preferred_element_type=jnp.float32
    ).astype(jnp.bfloat16)
    qk_own = (
        qkv_all[:, tok_count : 2 * tok_count]
        .transpose(1, 0, 2)
        .reshape(tok_count, 3 * feat_count)[:, : 2 * feat_count]
    )
    queries = qk_own[:, :feat_count]
    key_proj = qk_own[:, feat_count:]
    frame_index = lax.axis_index("fy") * lax.axis_size("core") + lax.axis_index("core")
    piece_index = lax.axis_index("piece")
    clip_counts = counts[0]
    count_here = lax.dynamic_index_in_dim(clip_counts, frame_index, 0, keepdims=False)
    rows_here = tok_count // (TGW * TILE)
    first_tile = (piece_index * rows_here - 1) * TGW
    spatial = spatial_rows(qkv_all, neighbors[0], first_tile, count_here)
    head_shape = (1, tok_count, HEADS, HD)
    frame_axes = ("fy", "core")
    qk_part = lax.all_to_all(
        jnp.stack([queries, key_proj]).reshape((2,) + head_shape),
        frame_axes,
        split_axis=2,
        concat_axis=1,
        tiled=True,
    )
    query_part, key_part = qk_part[0], qk_part[1]
    spatial_part = lax.all_to_all(
        spatial.reshape(head_shape), frame_axes, split_axis=1, concat_axis=0, tiled=True
    )
    per_dev = tok_count // n_frames
    first_pos = piece_index * tok_count + frame_index * per_dev
    temporal = temporal_block(query_part, key_part, spatial_part, clip_counts, first_pos)
    returned = lax.all_to_all(temporal, frame_axes, split_axis=0, concat_axis=1, tiled=True)
    flat_temporal = returned.reshape(tok_count, feat_count)
    projected = jnp.dot(flat_temporal, w_out_full, preferred_element_type=jnp.float32)
    return projected.astype(jnp.bfloat16).reshape(1, tok_count, feat_count)


def solution(mesh):
    n_fsdp = mesh.shape["fsdp"]
    n_sp = mesh.shape["sp"]
    split = Mesh(
        mesh.devices.reshape(n_fsdp, PIECES, n_sp // PIECES // 2, 2),
        ("fsdp", "piece", "fy", "core"),
    )
    seq = ("piece", "fy", "core")
    placed = (
        P("fsdp", seq, None),
        P("fsdp", None),
        P("fsdp", None),
        P(None, "fsdp"),
        P("fsdp", None),
        P("fsdp", seq, None),
        P("fsdp", None),
    )
    return jax.shard_map(
        local, mesh=split, in_specs=placed, out_specs=P("fsdp", seq, None), check_vma=False
    )
```

```python
import math

import jax
import jax.numpy as jnp
from jax import lax
from jax.experimental import pallas as pl
from jax.experimental.pallas import tpu as pltpu
from jax.sharding import Mesh
from jax.sharding import PartitionSpec as P

HEADS = 12
HD = 128
TILE = 128
TGW = 5
NBR = 6
PIECES = 4


def passed_along(block, axis, distance):
    devices = range(lax.axis_size(axis))
    route = [(i - distance, i) for i in devices if i - distance in devices]
    return lax.ppermute(block, axis, route)


def layer_norm(tokens, mod_scale, mod_shift):
    values_f32 = tokens.astype(jnp.float32)
    center = jnp.mean(values_f32, axis=-1, keepdims=True)
    spread = jnp.mean((values_f32 - center) ** 2, axis=-1, keepdims=True)
    normal = (values_f32 - center) / jnp.sqrt(spread + 1e-06)
    return (normal * (1.0 + mod_scale) + mod_shift).astype(jnp.bfloat16)


def spatial_kernel(list_ref, scalar_ref, q_ref, k_ref, v_ref, o_ref):
    scaling = 1.0 / math.sqrt(HD)
    first_tile = scalar_ref[0]
    count_here = scalar_ref[1]
    local_tiles = q_ref.shape[0] // TILE
    for t in range(local_tiles):
        query = q_ref[t * TILE : (t + 1) * TILE, :]
        parts = []
        row_max = None
        for n in range(NBR):
            tile_id = list_ref[t * NBR + n]
            start = pl.multiple_of((tile_id - first_tile) * TILE, TILE)
            key = k_ref[pl.ds(start, TILE), :]
            scores = (
                lax.dot_general(
                    query, key, (((1,), (1,)), ((), ())), preferred_element_type=jnp.float32
                )
                * scaling
            )
            key_pos = tile_id * TILE + lax.broadcasted_iota(jnp.int32, scores.shape, 1)
            live = key_pos < count_here
            scores = jnp.where(live, scores, -1e30)
            part_max = jnp.max(scores, axis=-1, keepdims=True)
            row_max = part_max if row_max is None else jnp.maximum(row_max, part_max)
            parts.append((scores, live, start))
        denominator = None
        summed = None
        for scores, live, start in parts:
            exp_terms = jnp.where(live, jnp.exp(scores - row_max), 0.0)
            part_sum = jnp.sum(exp_terms, axis=-1, keepdims=True)
            value = v_ref[pl.ds(start, TILE), :]
            part_out = jnp.dot(
                exp_terms.astype(jnp.bfloat16), value, preferred_element_type=jnp.float32
            )
            denominator = part_sum if denominator is None else denominator + part_sum
            summed = part_out if summed is None else summed + part_out
        o_ref[t * TILE : (t + 1) * TILE, :] = (summed / denominator).astype(o_ref.dtype)


def spatial_rows(qkv_all, tile_list, first_tile, count_here, h0, nh):
    buffer_rows = qkv_all.shape[1]
    rows, feat = buffer_rows // 3, qkv_all.shape[0] * qkv_all.shape[2] // 3
    per_shard = qkv_all.shape[2] // HD
    scalars = jnp.stack([first_tile, count_here]).astype(jnp.int32)
    grid_spec = pltpu.PrefetchScalarGridSpec(
        num_scalar_prefetch=2,
        grid=(nh,),
        in_specs=[
            pl.BlockSpec(
                (None, rows, HD),
                lambda h, lst, sc: ((h0 + h) // per_shard, 1, (h0 + h) % per_shard),
            ),
            pl.BlockSpec(
                (None, buffer_rows, HD),
                lambda h, lst, sc: (
                    (HEADS + h0 + h) // per_shard,
                    0,
                    (HEADS + h0 + h) % per_shard,
                ),
            ),
            pl.BlockSpec(
                (None, buffer_rows, HD),
                lambda h, lst, sc: (
                    (2 * HEADS + h0 + h) // per_shard,
                    0,
                    (2 * HEADS + h0 + h) % per_shard,
                ),
            ),
        ],
        out_specs=pl.BlockSpec((rows, HD), lambda h, lst, sc: (0, h)),
    )
    flops = 4 * rows * NBR * TILE * nh * HD
    return pl.pallas_call(
        spatial_kernel,
        grid_spec=grid_spec,
        out_shape=jax.ShapeDtypeStruct((rows, nh * HD), jnp.bfloat16),
        cost_estimate=pl.CostEstimate(
            flops=flops,
            transcendentals=rows * NBR * TILE * nh,
            bytes_accessed=2 * (rows * nh * HD * 2 + buffer_rows * nh * HD * 2),
        ),
    )(tile_list.reshape(-1).astype(jnp.int32), scalars, qkv_all, qkv_all, qkv_all)


MESH_IDS = pl.DeviceIdType.MESH


def rim_kernel(tok_ref, rim_ref, send_sem, recv_sem):
    n_piece = lax.axis_size("piece")
    piece = lax.axis_index("piece")
    here = (lax.axis_index("fsdp"), piece, lax.axis_index("fy"), lax.axis_index("core"))
    up = (here[0], piece - 1, here[2], here[3])
    down = (here[0], piece + 1, here[2], here[3])
    has_up = piece > 0
    has_down = piece < n_piece - 1
    barrier = pltpu.get_barrier_semaphore()

    @pl.when(has_up)
    def _():
        pl.semaphore_signal(barrier, inc=1, device_id=up, device_id_type=MESH_IDS)

    @pl.when(has_down)
    def _():
        pl.semaphore_signal(barrier, inc=1, device_id=down, device_id_type=MESH_IDS)

    peers = (piece + n_piece - 1) // n_piece + (2 * n_piece - 2 - piece) // n_piece
    pl.semaphore_wait(barrier, peers)

    to_down = pltpu.make_async_remote_copy(
        src_ref=tok_ref,
        dst_ref=rim_ref.at[0],
        send_sem=send_sem.at[0],
        recv_sem=recv_sem.at[0],
        device_id=down,
        device_id_type=MESH_IDS,
    )
    to_up = pltpu.make_async_remote_copy(
        src_ref=tok_ref,
        dst_ref=rim_ref.at[1],
        send_sem=send_sem.at[1],
        recv_sem=recv_sem.at[1],
        device_id=up,
        device_id_type=MESH_IDS,
    )

    @pl.when(has_down)
    def _():
        to_down.start()

    @pl.when(has_up)
    def _():
        to_up.start()

    @pl.when(has_down)
    def _():
        to_down.wait_send()
        to_up.wait_recv()

    @pl.when(has_up)
    def _():
        to_up.wait_send()
        to_down.wait_recv()


def exchange_rims(own):
    rows, feat = own.shape
    return pl.pallas_call(
        rim_kernel,
        out_shape=jax.ShapeDtypeStruct((2, rows, feat), own.dtype),
        in_specs=[pl.BlockSpec(memory_space=pl.ANY)],
        out_specs=pl.BlockSpec(memory_space=pl.ANY),
        scratch_shapes=[pltpu.SemaphoreType.DMA((2,)), pltpu.SemaphoreType.DMA((2,))],
        compiler_params=pltpu.CompilerParams(collective_id=0, has_side_effects=True),
        cost_estimate=pl.CostEstimate(flops=0, transcendentals=0, bytes_accessed=80 * rows * feat * 2),
    )(own)


def temporal_block(query_part, key_part, spatial_part, clip_counts, first_pos):
    n_frames, per_dev = query_part.shape[0], query_part.shape[1]
    scaling = 1.0 / math.sqrt(HD)
    position = first_pos + jnp.arange(per_dev, dtype=jnp.int32)
    live_mask = (position[:, None] < clip_counts[None, :])[:, None, None, :]
    scores = (
        jnp.einsum(
            "fphd,gphd->phfg", query_part, key_part, preferred_element_type=jnp.float32
        )
        * scaling
    )
    scores = jnp.where(live_mask, scores, -1e30)
    row_max = jnp.max(scores, axis=-1, keepdims=True)
    exp_terms = jnp.where(live_mask, jnp.exp(scores - row_max), 0.0)
    denominator = jnp.sum(exp_terms, axis=-1, keepdims=True)
    weights = exp_terms.astype(jnp.bfloat16)
    summed = jnp.einsum(
        "phfg,gphd->fphd", weights, spatial_part, preferred_element_type=jnp.float32
    )
    result = summed / jnp.transpose(denominator, (2, 0, 1, 3))
    return result.astype(jnp.bfloat16)


def local(tokens, mod_scale, mod_shift, w_qkv, w_out, neighbors, counts):
    tok_count = tokens.shape[1]
    feat_count = tokens.shape[2]
    n_frames = lax.axis_size("fy") * lax.axis_size("core")
    own = tokens[0]
    rims = exchange_rims(own)
    piece_index = lax.axis_index("piece")
    above = jnp.where(piece_index > 0, rims[0], jnp.zeros_like(own))
    below = jnp.where(piece_index < lax.axis_size("piece") - 1, rims[1], jnp.zeros_like(own))
    core = lax.axis_index("core")
    half_rows = w_qkv.shape[0] // 2
    w_half = lax.dynamic_slice_in_dim(w_qkv, core * half_rows, half_rows, axis=0)
    w_pieces = lax.all_gather(w_half, ("fsdp", "core"), axis=0, tiled=False)
    w_full = w_pieces.reshape(lax.axis_size("fsdp"), w_qkv.shape[0], w_qkv.shape[1])
    out_rows = w_out.shape[0] // 2
    w_out_half = lax.dynamic_slice_in_dim(w_out, core * out_rows, out_rows, axis=0)
    w_out_half = lax.all_gather(w_out_half, "core", axis=0, tiled=True)
    w_out_full = lax.all_gather(w_out_half, "fsdp", axis=0, tiled=True)
    normed_all = layer_norm(
        jnp.concatenate([above, own, below], axis=0), mod_scale[0], mod_shift[0]
    )
    qkv_all = jnp.einsum(
        "tk,jkc->jtc", normed_all, w_full, preferred_element_type=jnp.float32
    ).astype(jnp.bfloat16)
    frame_index = lax.axis_index("fy") * lax.axis_size("core") + lax.axis_index("core")
    piece_index = lax.axis_index("piece")
    clip_counts = counts[0]
    count_here = lax.dynamic_index_in_dim(clip_counts, frame_index, 0, keepdims=False)
    rows_here = tok_count // (TGW * TILE)
    first_tile = (piece_index * rows_here - 1) * TGW
    per_shard = qkv_all.shape[2] // HD
    own_rows = qkv_all[:, tok_count : 2 * tok_count]

    def head_columns(block0, nh):
        pieces = []
        for b in range(block0, block0 + nh):
            pieces.append(own_rows[b // per_shard, :, (b % per_shard) * HD : (b % per_shard + 1) * HD])
        return jnp.concatenate(pieces, axis=1)

    frame_axes = ("fy", "core")
    per_dev = tok_count // n_frames
    first_pos = piece_index * tok_count + frame_index * per_dev
    group = 4
    projected = None
    for h0 in range(0, HEADS, group):
        qk_in = jnp.concatenate(
            [head_columns(h0, group), head_columns(HEADS + h0, group)], axis=1
        )
        qk_part = lax.all_to_all(qk_in, frame_axes, split_axis=0, concat_axis=0, tiled=True)
        spatial = spatial_rows(qkv_all, neighbors[0], first_tile, count_here, h0, group)
        spatial_part = lax.all_to_all(spatial, frame_axes, split_axis=0, concat_axis=0, tiled=True)
        part_shape = (n_frames, per_dev, group, HD)
        query_part = qk_part[:, : group * HD].reshape(part_shape)
        key_part = qk_part[:, group * HD :].reshape(part_shape)
        temporal = temporal_block(
            query_part, key_part, spatial_part.reshape(part_shape), clip_counts, first_pos
        )
        returned = lax.all_to_all(
            temporal.reshape(tok_count, group * HD),
            frame_axes,
            split_axis=0,
            concat_axis=0,
            tiled=True,
        )
        partial = jnp.dot(
            returned,
            w_out_full[h0 * HD : (h0 + group) * HD],
            preferred_element_type=jnp.float32,
        )
        projected = partial if projected is None else projected + partial
    return projected.astype(jnp.bfloat16).reshape(1, tok_count, feat_count)


def solution(mesh):
    n_fsdp = mesh.shape["fsdp"]
    n_sp = mesh.shape["sp"]
    split = Mesh(
        mesh.devices.reshape(n_fsdp, PIECES, n_sp // PIECES // 2, 2),
        ("fsdp", "piece", "fy", "core"),
    )
    seq = ("piece", "fy", "core")
    placed = (
        P("fsdp", seq, None),
        P("fsdp", None),
        P("fsdp", None),
        P(None, "fsdp"),
        P("fsdp", None),
        P("fsdp", seq, None),
        P("fsdp", None),
    )
    return jax.shard_map(
        local, mesh=split, in_specs=placed, out_specs=P("fsdp", seq, None), check_vma=False
    )
```

```python
import math

import jax
import jax.numpy as jnp
from jax import lax
from jax.experimental import pallas as pl
from jax.experimental.pallas import tpu as pltpu
from jax.sharding import Mesh
from jax.sharding import PartitionSpec as P

HEADS = 12
HD = 128
TILE = 128
TGW = 5
NBR = 6
PIECES = 4


def passed_along(block, axis, distance):
    devices = range(lax.axis_size(axis))
    route = [(i - distance, i) for i in devices if i - distance in devices]
    return lax.ppermute(block, axis, route)


def layer_norm(tokens, mod_scale, mod_shift):
    values_f32 = tokens.astype(jnp.float32)
    center = jnp.mean(values_f32, axis=-1, keepdims=True)
    spread = jnp.mean((values_f32 - center) ** 2, axis=-1, keepdims=True)
    normal = (values_f32 - center) / jnp.sqrt(spread + 1e-06)
    return (normal * (1.0 + mod_scale) + mod_shift).astype(jnp.bfloat16)


def spatial_kernel(list_ref, scalar_ref, q_ref, k_ref, v_ref, o_ref):
    scaling = 1.0 / math.sqrt(HD)
    first_tile = scalar_ref[0]
    count_here = scalar_ref[1]
    local_tiles = q_ref.shape[0] // TILE
    for t in range(local_tiles):
        query = q_ref[t * TILE : (t + 1) * TILE, :]
        parts = []
        row_max = None
        for n in range(NBR):
            tile_id = list_ref[t * NBR + n]
            start = pl.multiple_of((tile_id - first_tile) * TILE, TILE)
            key = k_ref[pl.ds(start, TILE), :]
            scores = (
                lax.dot_general(
                    query, key, (((1,), (1,)), ((), ())), preferred_element_type=jnp.float32
                )
                * scaling
            )
            key_pos = tile_id * TILE + lax.broadcasted_iota(jnp.int32, scores.shape, 1)
            live = key_pos < count_here
            scores = jnp.where(live, scores, -1e30)
            part_max = jnp.max(scores, axis=-1, keepdims=True)
            row_max = part_max if row_max is None else jnp.maximum(row_max, part_max)
            parts.append((scores, live, start))
        denominator = None
        summed = None
        for scores, live, start in parts:
            exp_terms = jnp.where(live, jnp.exp(scores - row_max), 0.0)
            part_sum = jnp.sum(exp_terms, axis=-1, keepdims=True)
            value = v_ref[pl.ds(start, TILE), :]
            part_out = jnp.dot(
                exp_terms.astype(jnp.bfloat16), value, preferred_element_type=jnp.float32
            )
            denominator = part_sum if denominator is None else denominator + part_sum
            summed = part_out if summed is None else summed + part_out
        o_ref[t * TILE : (t + 1) * TILE, :] = (summed / denominator).astype(o_ref.dtype)


def spatial_rows(queries, kv_all, tile_list, first_tile, count_here):
    buffer_rows = kv_all.shape[1]
    rows, feat = queries.shape
    per_shard = kv_all.shape[2] // HD
    scalars = jnp.stack([first_tile, count_here]).astype(jnp.int32)
    grid_spec = pltpu.PrefetchScalarGridSpec(
        num_scalar_prefetch=2,
        grid=(HEADS,),
        in_specs=[
            pl.BlockSpec((rows, HD), lambda h, lst, sc: (0, h)),
            pl.BlockSpec(
                (None, buffer_rows, HD),
                lambda h, lst, sc: ((HEADS + h) // per_shard - 1, 0, (HEADS + h) % per_shard),
            ),
            pl.BlockSpec(
                (None, buffer_rows, HD),
                lambda h, lst, sc: (
                    (2 * HEADS + h) // per_shard - 1,
                    0,
                    (2 * HEADS + h) % per_shard,
                ),
            ),
        ],
        out_specs=pl.BlockSpec((rows, HD), lambda h, lst, sc: (0, h)),
    )
    flops = 4 * rows * NBR * TILE * feat
    return pl.pallas_call(
        spatial_kernel,
        grid_spec=grid_spec,
        out_shape=jax.ShapeDtypeStruct((rows, feat), jnp.bfloat16),
        cost_estimate=pl.CostEstimate(
            flops=flops,
            transcendentals=rows * NBR * TILE * HEADS,
            bytes_accessed=2 * (rows * feat * 2 + buffer_rows * feat * 2),
        ),
    )(tile_list.reshape(-1).astype(jnp.int32), scalars, queries, kv_all, kv_all)


MESH_IDS = pl.DeviceIdType.MESH


def rim_kernel(tok_ref, rim_ref, send_sem, recv_sem):
    n_piece = lax.axis_size("piece")
    piece = lax.axis_index("piece")
    here = (lax.axis_index("fsdp"), piece, lax.axis_index("fy"), lax.axis_index("core"))
    up = (here[0], piece - 1, here[2], here[3])
    down = (here[0], piece + 1, here[2], here[3])
    has_up = piece > 0
    has_down = piece < n_piece - 1
    barrier = pltpu.get_barrier_semaphore()

    @pl.when(has_up)
    def _():
        pl.semaphore_signal(barrier, inc=1, device_id=up, device_id_type=MESH_IDS)

    @pl.when(has_down)
    def _():
        pl.semaphore_signal(barrier, inc=1, device_id=down, device_id_type=MESH_IDS)

    peers = (piece + n_piece - 1) // n_piece + (2 * n_piece - 2 - piece) // n_piece
    pl.semaphore_wait(barrier, peers)

    to_down = pltpu.make_async_remote_copy(
        src_ref=tok_ref,
        dst_ref=rim_ref.at[0],
        send_sem=send_sem.at[0],
        recv_sem=recv_sem.at[0],
        device_id=down,
        device_id_type=MESH_IDS,
    )
    to_up = pltpu.make_async_remote_copy(
        src_ref=tok_ref,
        dst_ref=rim_ref.at[1],
        send_sem=send_sem.at[1],
        recv_sem=recv_sem.at[1],
        device_id=up,
        device_id_type=MESH_IDS,
    )

    @pl.when(has_down)
    def _():
        to_down.start()

    @pl.when(has_up)
    def _():
        to_up.start()

    @pl.when(has_down)
    def _():
        to_down.wait_send()
        to_up.wait_recv()

    @pl.when(has_up)
    def _():
        to_up.wait_send()
        to_down.wait_recv()


def exchange_rims(own):
    rows, feat = own.shape
    return pl.pallas_call(
        rim_kernel,
        out_shape=jax.ShapeDtypeStruct((2, rows, feat), own.dtype),
        in_specs=[pl.BlockSpec(memory_space=pl.ANY)],
        out_specs=pl.BlockSpec(memory_space=pl.ANY),
        scratch_shapes=[pltpu.SemaphoreType.DMA((2,)), pltpu.SemaphoreType.DMA((2,))],
        compiler_params=pltpu.CompilerParams(collective_id=0, has_side_effects=True),
        cost_estimate=pl.CostEstimate(flops=0, transcendentals=0, bytes_accessed=80 * rows * feat * 2),
    )(own)


def temporal_block(query_part, key_part, spatial_part, clip_counts, first_pos):
    n_frames, per_dev = query_part.shape[0], query_part.shape[1]
    scaling = 1.0 / math.sqrt(HD)
    position = first_pos + jnp.arange(per_dev, dtype=jnp.int32)
    live_mask = (position[:, None] < clip_counts[None, :])[:, None, None, :]
    scores = (
        jnp.einsum(
            "fphd,gphd->phfg", query_part, key_part, preferred_element_type=jnp.float32
        )
        * scaling
    )
    scores = jnp.where(live_mask, scores, -1e30)
    row_max = jnp.max(scores, axis=-1, keepdims=True)
    exp_terms = jnp.where(live_mask, jnp.exp(scores - row_max), 0.0)
    denominator = jnp.sum(exp_terms, axis=-1, keepdims=True)
    weights = exp_terms.astype(jnp.bfloat16)
    summed = jnp.einsum(
        "phfg,gphd->fphd", weights, spatial_part, preferred_element_type=jnp.float32
    )
    result = summed / jnp.transpose(denominator, (2, 0, 1, 3))
    return result.astype(jnp.bfloat16)


def local(tokens, mod_scale, mod_shift, w_qkv, w_out, neighbors, counts):
    tok_count = tokens.shape[1]
    feat_count = tokens.shape[2]
    n_frames = lax.axis_size("fy") * lax.axis_size("core")
    own = tokens[0]
    rims = exchange_rims(own)
    piece_index = lax.axis_index("piece")
    above = jnp.where(piece_index > 0, rims[0], jnp.zeros_like(own))
    below = jnp.where(piece_index < lax.axis_size("piece") - 1, rims[1], jnp.zeros_like(own))
    core = lax.axis_index("core")
    half_rows = w_qkv.shape[0] // 2
    w_half = lax.dynamic_slice_in_dim(w_qkv, core * half_rows, half_rows, axis=0)
    w_pieces = lax.all_gather(w_half, ("fsdp", "core"), axis=0, tiled=False)
    w_full = w_pieces.reshape(lax.axis_size("fsdp"), w_qkv.shape[0], w_qkv.shape[1])
    out_rows = w_out.shape[0] // 2
    w_out_half = lax.dynamic_slice_in_dim(w_out, core * out_rows, out_rows, axis=0)
    w_out_half = lax.all_gather(w_out_half, "core", axis=0, tiled=True)
    w_out_full = lax.all_gather(w_out_half, "fsdp", axis=0, tiled=True)
    normed_all = layer_norm(
        jnp.concatenate([above, own, below], axis=0), mod_scale[0], mod_shift[0]
    )
    shard_cols = w_full.shape[2]
    w_query = jnp.concatenate(
        [w_full[0], w_full[1, :, : feat_count - shard_cols]], axis=1
    )
    queries = jnp.dot(
        normed_all[tok_count : 2 * tok_count], w_query, preferred_element_type=jnp.float32
    ).astype(jnp.bfloat16)
    kv_all = jnp.einsum(
        "tk,jkc->jtc", normed_all, w_full[1:], preferred_element_type=jnp.float32
    ).astype(jnp.bfloat16)
    key_cut = feat_count - shard_cols
    own_kv = kv_all[:, tok_count : 2 * tok_count]
    key_proj = jnp.concatenate(
        [own_kv[0, :, key_cut:], own_kv[1, :, : feat_count - shard_cols + key_cut]], axis=1
    )
    frame_index = lax.axis_index("fy") * lax.axis_size("core") + lax.axis_index("core")
    piece_index = lax.axis_index("piece")
    clip_counts = counts[0]
    count_here = lax.dynamic_index_in_dim(clip_counts, frame_index, 0, keepdims=False)
    rows_here = tok_count // (TGW * TILE)
    first_tile = (piece_index * rows_here - 1) * TGW
    spatial = spatial_rows(queries, kv_all, neighbors[0], first_tile, count_here)
    frame_axes = ("fy", "core")
    qk_part = lax.all_to_all(
        jnp.concatenate([queries, key_proj], axis=1),
        frame_axes,
        split_axis=0,
        concat_axis=0,
        tiled=True,
    )
    spatial_part = lax.all_to_all(spatial, frame_axes, split_axis=0, concat_axis=0, tiled=True)
    per_dev = tok_count // n_frames
    first_pos = piece_index * tok_count + frame_index * per_dev
    part_shape = (n_frames, per_dev, HEADS, HD)
    temporal = temporal_block(
        qk_part[:, :feat_count].reshape(part_shape),
        qk_part[:, feat_count:].reshape(part_shape),
        spatial_part.reshape(part_shape),
        clip_counts,
        first_pos,
    )
    flat_temporal = lax.all_to_all(
        temporal.reshape(tok_count, feat_count), frame_axes, split_axis=0, concat_axis=0, tiled=True
    )
    projected = jnp.dot(flat_temporal, w_out_full, preferred_element_type=jnp.float32)
    return projected.astype(jnp.bfloat16).reshape(1, tok_count, feat_count)


def solution(mesh):
    n_fsdp = mesh.shape["fsdp"]
    n_sp = mesh.shape["sp"]
    split = Mesh(
        mesh.devices.reshape(n_fsdp, PIECES, n_sp // PIECES // 2, 2),
        ("fsdp", "piece", "fy", "core"),
    )
    seq = ("piece", "fy", "core")
    placed = (
        P("fsdp", seq, None),
        P("fsdp", None),
        P("fsdp", None),
        P(None, "fsdp"),
        P("fsdp", None),
        P("fsdp", seq, None),
        P("fsdp", None),
    )
    return jax.shard_map(
        local, mesh=split, in_specs=placed, out_specs=P("fsdp", seq, None), check_vma=False
    )
```

```python
import math

import jax
import jax.numpy as jnp
from jax import lax
from jax.experimental import pallas as pl
from jax.experimental.pallas import tpu as pltpu
from jax.sharding import Mesh
from jax.sharding import PartitionSpec as P

HEADS = 12
HD = 128
TILE = 128
TGW = 5
NBR = 6
PIECES = 4


def passed_along(block, axis, distance):
    devices = range(lax.axis_size(axis))
    route = [(i - distance, i) for i in devices if i - distance in devices]
    return lax.ppermute(block, axis, route)


def layer_norm(tokens, mod_scale, mod_shift):
    values_f32 = tokens.astype(jnp.float32)
    center = jnp.mean(values_f32, axis=-1, keepdims=True)
    spread = jnp.mean((values_f32 - center) ** 2, axis=-1, keepdims=True)
    normal = (values_f32 - center) / jnp.sqrt(spread + 1e-06)
    return (normal * (1.0 + mod_scale) + mod_shift).astype(jnp.bfloat16)


def spatial_kernel(list_ref, scalar_ref, q_ref, k_ref, v_ref, o_ref):
    scaling = 1.0 / math.sqrt(HD)
    first_tile = scalar_ref[0]
    count_here = scalar_ref[1]
    local_tiles = q_ref.shape[0] // TILE
    for t in range(local_tiles):
        query = q_ref[t * TILE : (t + 1) * TILE, :]
        parts = []
        row_max = None
        for n in range(NBR):
            tile_id = list_ref[t * NBR + n]
            start = pl.multiple_of((tile_id - first_tile) * TILE, TILE)
            key = k_ref[pl.ds(start, TILE), :]
            scores = (
                lax.dot_general(
                    query, key, (((1,), (1,)), ((), ())), preferred_element_type=jnp.float32
                )
                * scaling
            )
            key_pos = tile_id * TILE + lax.broadcasted_iota(jnp.int32, scores.shape, 1)
            live = key_pos < count_here
            scores = jnp.where(live, scores, -1e30)
            part_max = jnp.max(scores, axis=-1, keepdims=True)
            row_max = part_max if row_max is None else jnp.maximum(row_max, part_max)
            parts.append((scores, live, start))
        denominator = None
        summed = None
        for scores, live, start in parts:
            exp_terms = jnp.where(live, jnp.exp(scores - row_max), 0.0)
            part_sum = jnp.sum(exp_terms, axis=-1, keepdims=True)
            value = v_ref[pl.ds(start, TILE), :]
            part_out = jnp.dot(
                exp_terms.astype(jnp.bfloat16), value, preferred_element_type=jnp.float32
            )
            denominator = part_sum if denominator is None else denominator + part_sum
            summed = part_out if summed is None else summed + part_out
        o_ref[t * TILE : (t + 1) * TILE, :] = (summed / denominator).astype(o_ref.dtype)


def spatial_rows(queries, kv_all, tile_list, first_tile, count_here):
    buffer_rows = kv_all.shape[1]
    rows, feat = queries.shape
    per_shard = kv_all.shape[2] // HD
    scalars = jnp.stack([first_tile, count_here]).astype(jnp.int32)
    grid_spec = pltpu.PrefetchScalarGridSpec(
        num_scalar_prefetch=2,
        grid=(HEADS,),
        in_specs=[
            pl.BlockSpec((rows, HD), lambda h, lst, sc: (0, h)),
            pl.BlockSpec(
                (None, buffer_rows, HD),
                lambda h, lst, sc: ((HEADS + h) // per_shard - 1, 0, (HEADS + h) % per_shard),
            ),
            pl.BlockSpec(
                (None, buffer_rows, HD),
                lambda h, lst, sc: (
                    (2 * HEADS + h) // per_shard - 1,
                    0,
                    (2 * HEADS + h) % per_shard,
                ),
            ),
        ],
        out_specs=pl.BlockSpec((rows, HD), lambda h, lst, sc: (0, h)),
    )
    flops = 4 * rows * NBR * TILE * feat
    return pl.pallas_call(
        spatial_kernel,
        grid_spec=grid_spec,
        out_shape=jax.ShapeDtypeStruct((rows, feat), jnp.bfloat16),
        cost_estimate=pl.CostEstimate(
            flops=flops,
            transcendentals=rows * NBR * TILE * HEADS,
            bytes_accessed=2 * (rows * feat * 2 + buffer_rows * feat * 2),
        ),
    )(tile_list.reshape(-1).astype(jnp.int32), scalars, queries, kv_all, kv_all)


MESH_IDS = pl.DeviceIdType.MESH


def exchange_kernel(tok_ref, rim_ref, cross_ref, send_sem, recv_sem, cross_send, cross_recv, own_sem):
    n_piece = lax.axis_size("piece")
    n_core = lax.axis_size("core")
    n_frames = lax.axis_size("fy") * n_core
    piece = lax.axis_index("piece")
    frame = lax.axis_index("fy") * n_core + lax.axis_index("core")
    fsdp = lax.axis_index("fsdp")
    here = (fsdp, piece, lax.axis_index("fy"), lax.axis_index("core"))
    up = (fsdp, piece - 1, here[2], here[3])
    down = (fsdp, piece + 1, here[2], here[3])
    has_up = piece > 0
    has_down = piece < n_piece - 1
    per = tok_ref.shape[0] // n_frames
    peers = [(frame + k) % n_frames for k in range(1, n_frames)]
    barrier = pltpu.get_barrier_semaphore()

    @pl.when(has_up)
    def _():
        pl.semaphore_signal(barrier, inc=1, device_id=up, device_id_type=MESH_IDS)

    @pl.when(has_down)
    def _():
        pl.semaphore_signal(barrier, inc=1, device_id=down, device_id_type=MESH_IDS)

    for d in peers:
        pl.semaphore_signal(
            barrier, inc=1, device_id=(fsdp, piece, d // n_core, d % n_core), device_id_type=MESH_IDS
        )
    rim_peers = (piece + n_piece - 1) // n_piece + (2 * n_piece - 2 - piece) // n_piece
    pl.semaphore_wait(barrier, rim_peers + n_frames - 1)

    to_down = pltpu.make_async_remote_copy(
        src_ref=tok_ref,
        dst_ref=rim_ref.at[0],
        send_sem=send_sem.at[0],
        recv_sem=recv_sem.at[0],
        device_id=down,
        device_id_type=MESH_IDS,
    )
    to_up = pltpu.make_async_remote_copy(
        src_ref=tok_ref,
        dst_ref=rim_ref.at[1],
        send_sem=send_sem.at[1],
        recv_sem=recv_sem.at[1],
        device_id=up,
        device_id_type=MESH_IDS,
    )

    @pl.when(has_down)
    def _():
        to_down.start()

    @pl.when(has_up)
    def _():
        to_up.start()

    crosses = []
    for k, d in enumerate(peers):
        copy = pltpu.make_async_remote_copy(
            src_ref=tok_ref.at[pl.ds(pl.multiple_of(d * per, 16), per)],
            dst_ref=cross_ref.at[pl.ds(pl.multiple_of(frame * per, 16), per)],
            send_sem=cross_send.at[k],
            recv_sem=cross_recv.at[k],
            device_id=(fsdp, piece, d // n_core, d % n_core),
            device_id_type=MESH_IDS,
        )
        copy.start()
        crosses.append(copy)
    own_rows = pl.ds(pl.multiple_of(frame * per, 16), per)
    own_copy = pltpu.make_async_copy(tok_ref.at[own_rows], cross_ref.at[own_rows], own_sem)
    own_copy.start()

    @pl.when(has_down)
    def _():
        to_down.wait_send()
        to_up.wait_recv()

    @pl.when(has_up)
    def _():
        to_up.wait_send()
        to_down.wait_recv()

    for copy in crosses:
        copy.wait()
    own_copy.wait()


def exchange_tokens(own):
    rows, feat = own.shape
    return pl.pallas_call(
        exchange_kernel,
        out_shape=(
            jax.ShapeDtypeStruct((2, rows, feat), own.dtype),
            jax.ShapeDtypeStruct((rows, feat), own.dtype),
        ),
        in_specs=[pl.BlockSpec(memory_space=pl.ANY)],
        out_specs=(pl.BlockSpec(memory_space=pl.ANY), pl.BlockSpec(memory_space=pl.ANY)),
        scratch_shapes=[
            pltpu.SemaphoreType.DMA((2,)),
            pltpu.SemaphoreType.DMA((2,)),
            pltpu.SemaphoreType.DMA((8,)),
            pltpu.SemaphoreType.DMA((8,)),
            pltpu.SemaphoreType.DMA(()),
        ],
        compiler_params=pltpu.CompilerParams(collective_id=0, has_side_effects=True),
        cost_estimate=pl.CostEstimate(flops=0, transcendentals=0, bytes_accessed=80 * rows * feat * 2),
    )(own)


def temporal_block(query_part, key_part, spatial_part, clip_counts, first_pos):
    n_frames, per_dev = query_part.shape[0], query_part.shape[1]
    scaling = 1.0 / math.sqrt(HD)
    position = first_pos + jnp.arange(per_dev, dtype=jnp.int32)
    live_mask = (position[:, None] < clip_counts[None, :])[:, None, None, :]
    scores = (
        jnp.einsum(
            "fphd,gphd->phfg", query_part, key_part, preferred_element_type=jnp.float32
        )
        * scaling
    )
    scores = jnp.where(live_mask, scores, -1e30)
    row_max = jnp.max(scores, axis=-1, keepdims=True)
    exp_terms = jnp.where(live_mask, jnp.exp(scores - row_max), 0.0)
    denominator = jnp.sum(exp_terms, axis=-1, keepdims=True)
    weights = exp_terms.astype(jnp.bfloat16)
    summed = jnp.einsum(
        "phfg,gphd->fphd", weights, spatial_part, preferred_element_type=jnp.float32
    )
    result = summed / jnp.transpose(denominator, (2, 0, 1, 3))
    return result.astype(jnp.bfloat16)


def local(tokens, mod_scale, mod_shift, w_qkv, w_out, neighbors, counts):
    tok_count = tokens.shape[1]
    feat_count = tokens.shape[2]
    n_frames = lax.axis_size("fy") * lax.axis_size("core")
    own = tokens[0]
    rims, crossed = exchange_tokens(own)
    piece_index = lax.axis_index("piece")
    above = jnp.where(piece_index > 0, rims[0], jnp.zeros_like(own))
    below = jnp.where(piece_index < lax.axis_size("piece") - 1, rims[1], jnp.zeros_like(own))
    core = lax.axis_index("core")
    half_rows = w_qkv.shape[0] // 2
    w_half = lax.dynamic_slice_in_dim(w_qkv, core * half_rows, half_rows, axis=0)
    w_pieces = lax.all_gather(w_half, ("fsdp", "core"), axis=0, tiled=False)
    w_full = w_pieces.reshape(lax.axis_size("fsdp"), w_qkv.shape[0], w_qkv.shape[1])
    out_rows = w_out.shape[0] // 2
    w_out_half = lax.dynamic_slice_in_dim(w_out, core * out_rows, out_rows, axis=0)
    w_out_half = lax.all_gather(w_out_half, "core", axis=0, tiled=True)
    w_out_full = lax.all_gather(w_out_half, "fsdp", axis=0, tiled=True)
    normed_all = layer_norm(
        jnp.concatenate([above, own, below], axis=0), mod_scale[0], mod_shift[0]
    )
    shard_cols = w_full.shape[2]
    w_query = jnp.concatenate(
        [w_full[0], w_full[1, :, : feat_count - shard_cols]], axis=1
    )
    normed_cross = layer_norm(crossed, mod_scale[0], mod_shift[0])
    w_key = jnp.concatenate(
        [w_full[1, :, feat_count - shard_cols :], w_full[2, :, : 2 * shard_cols - feat_count]], axis=1
    )
    q_both = jnp.dot(
        jnp.concatenate([normed_all[tok_count : 2 * tok_count], normed_cross], axis=0),
        w_query,
        preferred_element_type=jnp.float32,
    ).astype(jnp.bfloat16)
    queries = q_both[:tok_count]
    key_cross = jnp.dot(normed_cross, w_key, preferred_element_type=jnp.float32).astype(jnp.bfloat16)
    kv_all = jnp.einsum(
        "tk,jkc->jtc", normed_all, w_full[1:], preferred_element_type=jnp.float32
    ).astype(jnp.bfloat16)
    frame_index = lax.axis_index("fy") * lax.axis_size("core") + lax.axis_index("core")
    piece_index = lax.axis_index("piece")
    clip_counts = counts[0]
    count_here = lax.dynamic_index_in_dim(clip_counts, frame_index, 0, keepdims=False)
    rows_here = tok_count // (TGW * TILE)
    first_tile = (piece_index * rows_here - 1) * TGW
    spatial = spatial_rows(queries, kv_all, neighbors[0], first_tile, count_here)
    frame_axes = ("fy", "core")
    spatial_part = lax.all_to_all(spatial, frame_axes, split_axis=0, concat_axis=0, tiled=True)
    per_dev = tok_count // n_frames
    first_pos = piece_index * tok_count + frame_index * per_dev
    part_shape = (n_frames, per_dev, HEADS, HD)
    temporal = temporal_block(
        q_both[tok_count:].reshape(part_shape),
        key_cross.reshape(part_shape),
        spatial_part.reshape(part_shape),
        clip_counts,
        first_pos,
    )
    flat_temporal = lax.all_to_all(
        temporal.reshape(tok_count, feat_count), frame_axes, split_axis=0, concat_axis=0, tiled=True
    )
    projected = jnp.dot(flat_temporal, w_out_full, preferred_element_type=jnp.float32)
    return projected.astype(jnp.bfloat16).reshape(1, tok_count, feat_count)


def solution(mesh):
    n_fsdp = mesh.shape["fsdp"]
    n_sp = mesh.shape["sp"]
    split = Mesh(
        mesh.devices.reshape(n_fsdp, PIECES, n_sp // PIECES // 2, 2),
        ("fsdp", "piece", "fy", "core"),
    )
    seq = ("piece", "fy", "core")
    placed = (
        P("fsdp", seq, None),
        P("fsdp", None),
        P("fsdp", None),
        P(None, "fsdp"),
        P("fsdp", None),
        P("fsdp", seq, None),
        P("fsdp", None),
    )
    return jax.shard_map(
        local, mesh=split, in_specs=placed, out_specs=P("fsdp", seq, None), check_vma=False
    )
```

```python
import math

import jax
import jax.numpy as jnp
from jax import lax
from jax.experimental import pallas as pl
from jax.experimental.pallas import tpu as pltpu
from jax.sharding import Mesh
from jax.sharding import PartitionSpec as P

HEADS = 12
HD = 128
TILE = 128
TGW = 5
NBR = 6
PIECES = 4


def passed_along(block, axis, distance):
    devices = range(lax.axis_size(axis))
    route = [(i - distance, i) for i in devices if i - distance in devices]
    return lax.ppermute(block, axis, route)


def layer_norm(tokens, mod_scale, mod_shift):
    values_f32 = tokens.astype(jnp.float32)
    center = jnp.mean(values_f32, axis=-1, keepdims=True)
    spread = jnp.mean((values_f32 - center) ** 2, axis=-1, keepdims=True)
    normal = (values_f32 - center) / jnp.sqrt(spread + 1e-06)
    return (normal * (1.0 + mod_scale) + mod_shift).astype(jnp.bfloat16)


def spatial_kernel(list_ref, scalar_ref, q_ref, k_ref, v_ref, o_ref):
    scaling = 1.0 / math.sqrt(HD)
    first_tile = scalar_ref[0]
    count_here = scalar_ref[1]
    local_tiles = q_ref.shape[0] // TILE
    for t in range(local_tiles):
        query = q_ref[t * TILE : (t + 1) * TILE, :]
        parts = []
        row_max = None
        for n in range(NBR):
            tile_id = list_ref[t * NBR + n]
            start = pl.multiple_of((tile_id - first_tile) * TILE, TILE)
            key = k_ref[pl.ds(start, TILE), :]
            scores = (
                lax.dot_general(
                    query, key, (((1,), (1,)), ((), ())), preferred_element_type=jnp.float32
                )
                * scaling
            )
            key_pos = tile_id * TILE + lax.broadcasted_iota(jnp.int32, scores.shape, 1)
            live = key_pos < count_here
            scores = jnp.where(live, scores, -1e30)
            part_max = jnp.max(scores, axis=-1, keepdims=True)
            row_max = part_max if row_max is None else jnp.maximum(row_max, part_max)
            parts.append((scores, live, start))
        denominator = None
        summed = None
        for scores, live, start in parts:
            exp_terms = jnp.where(live, jnp.exp(scores - row_max), 0.0)
            part_sum = jnp.sum(exp_terms, axis=-1, keepdims=True)
            value = v_ref[pl.ds(start, TILE), :]
            part_out = jnp.dot(
                exp_terms.astype(jnp.bfloat16), value, preferred_element_type=jnp.float32
            )
            denominator = part_sum if denominator is None else denominator + part_sum
            summed = part_out if summed is None else summed + part_out
        o_ref[t * TILE : (t + 1) * TILE, :] = (summed / denominator).astype(o_ref.dtype)


def spatial_rows(queries, kv_all, tile_list, first_tile, count_here):
    buffer_rows = kv_all.shape[1]
    rows, feat = queries.shape
    per_shard = kv_all.shape[2] // HD
    scalars = jnp.stack([first_tile, count_here]).astype(jnp.int32)
    grid_spec = pltpu.PrefetchScalarGridSpec(
        num_scalar_prefetch=2,
        grid=(HEADS,),
        in_specs=[
            pl.BlockSpec((rows, HD), lambda h, lst, sc: (0, h)),
            pl.BlockSpec(
                (None, buffer_rows, HD),
                lambda h, lst, sc: ((HEADS + h) // per_shard - 1, 0, (HEADS + h) % per_shard),
            ),
            pl.BlockSpec(
                (None, buffer_rows, HD),
                lambda h, lst, sc: (
                    (2 * HEADS + h) // per_shard - 1,
                    0,
                    (2 * HEADS + h) % per_shard,
                ),
            ),
        ],
        out_specs=pl.BlockSpec((rows, HD), lambda h, lst, sc: (0, h)),
    )
    flops = 4 * rows * NBR * TILE * feat
    return pl.pallas_call(
        spatial_kernel,
        grid_spec=grid_spec,
        out_shape=jax.ShapeDtypeStruct((rows, feat), jnp.bfloat16),
        cost_estimate=pl.CostEstimate(
            flops=flops,
            transcendentals=rows * NBR * TILE * HEADS,
            bytes_accessed=2 * (rows * feat * 2 + buffer_rows * feat * 2),
        ),
    )(tile_list.reshape(-1).astype(jnp.int32), scalars, queries, kv_all, kv_all)


MESH_IDS = pl.DeviceIdType.MESH


def exchange_kernel(tok_ref, rim_ref, cross_ref, send_sem, recv_sem, cross_send, cross_recv, own_sem):
    n_piece = lax.axis_size("piece")
    n_core = lax.axis_size("core")
    n_frames = lax.axis_size("fy") * n_core
    piece = lax.axis_index("piece")
    frame = lax.axis_index("fy") * n_core + lax.axis_index("core")
    fsdp = lax.axis_index("fsdp")
    here = (fsdp, piece, lax.axis_index("fy"), lax.axis_index("core"))
    up = (fsdp, piece - 1, here[2], here[3])
    down = (fsdp, piece + 1, here[2], here[3])
    has_up = piece > 0
    has_down = piece < n_piece - 1
    per = tok_ref.shape[0] // n_frames
    peers = [(frame + k) % n_frames for k in range(1, n_frames)]
    barrier = pltpu.get_barrier_semaphore()

    @pl.when(has_up)
    def _():
        pl.semaphore_signal(barrier, inc=1, device_id=up, device_id_type=MESH_IDS)

    @pl.when(has_down)
    def _():
        pl.semaphore_signal(barrier, inc=1, device_id=down, device_id_type=MESH_IDS)

    for d in peers:
        pl.semaphore_signal(
            barrier, inc=1, device_id=(fsdp, piece, d // n_core, d % n_core), device_id_type=MESH_IDS
        )
    rim_peers = (piece + n_piece - 1) // n_piece + (2 * n_piece - 2 - piece) // n_piece
    pl.semaphore_wait(barrier, rim_peers + n_frames - 1)

    to_down = pltpu.make_async_remote_copy(
        src_ref=tok_ref,
        dst_ref=rim_ref.at[0],
        send_sem=send_sem.at[0],
        recv_sem=recv_sem.at[0],
        device_id=down,
        device_id_type=MESH_IDS,
    )
    to_up = pltpu.make_async_remote_copy(
        src_ref=tok_ref,
        dst_ref=rim_ref.at[1],
        send_sem=send_sem.at[1],
        recv_sem=recv_sem.at[1],
        device_id=up,
        device_id_type=MESH_IDS,
    )

    @pl.when(has_down)
    def _():
        to_down.start()

    @pl.when(has_up)
    def _():
        to_up.start()

    crosses = []
    for k, d in enumerate(peers):
        copy = pltpu.make_async_remote_copy(
            src_ref=tok_ref.at[pl.ds(pl.multiple_of(d * per, 16), per)],
            dst_ref=cross_ref.at[pl.ds(pl.multiple_of(frame * per, 16), per)],
            send_sem=cross_send.at[k],
            recv_sem=cross_recv.at[k],
            device_id=(fsdp, piece, d // n_core, d % n_core),
            device_id_type=MESH_IDS,
        )
        copy.start()
        crosses.append(copy)
    own_rows = pl.ds(pl.multiple_of(frame * per, 16), per)
    own_copy = pltpu.make_async_copy(tok_ref.at[own_rows], cross_ref.at[own_rows], own_sem)
    own_copy.start()

    @pl.when(has_down)
    def _():
        to_down.wait_send()
        to_up.wait_recv()

    @pl.when(has_up)
    def _():
        to_up.wait_send()
        to_down.wait_recv()

    for copy in crosses:
        copy.wait()
    own_copy.wait()


def exchange_tokens(own):
    rows, feat = own.shape
    return pl.pallas_call(
        exchange_kernel,
        out_shape=(
            jax.ShapeDtypeStruct((2, rows, feat), own.dtype),
            jax.ShapeDtypeStruct((rows, feat), own.dtype),
        ),
        in_specs=[pl.BlockSpec(memory_space=pl.ANY)],
        out_specs=(pl.BlockSpec(memory_space=pl.ANY), pl.BlockSpec(memory_space=pl.ANY)),
        scratch_shapes=[
            pltpu.SemaphoreType.DMA((2,)),
            pltpu.SemaphoreType.DMA((2,)),
            pltpu.SemaphoreType.DMA((8,)),
            pltpu.SemaphoreType.DMA((8,)),
            pltpu.SemaphoreType.DMA(()),
        ],
        compiler_params=pltpu.CompilerParams(collective_id=0, has_side_effects=True),
        cost_estimate=pl.CostEstimate(flops=0, transcendentals=0, bytes_accessed=80 * rows * feat * 2),
    )(own)


def temporal_kernel(scalar_ref, q_ref, k_ref, s_ref, o_ref):
    scaling = 1.0 / math.sqrt(HD)
    n_frames = scalar_ref.shape[0] - 1
    per = q_ref.shape[0] // n_frames
    position = scalar_ref[0] + lax.broadcasted_iota(jnp.int32, (per, 1), 0)
    live = [position < scalar_ref[1 + g] for g in range(n_frames)]
    keys = [k_ref[g * per : (g + 1) * per, :].astype(jnp.float32) for g in range(n_frames)]
    for f in range(n_frames):
        query = q_ref[f * per : (f + 1) * per, :].astype(jnp.float32)
        scores = []
        row_max = None
        for g in range(n_frames):
            score = jnp.sum(query * keys[g], axis=-1, keepdims=True) * scaling
            score = jnp.where(live[g], score, -1e30)
            row_max = score if row_max is None else jnp.maximum(row_max, score)
            scores.append(score)
        denominator = None
        summed = None
        for g in range(n_frames):
            exp_term = jnp.where(live[g], jnp.exp(scores[g] - row_max), 0.0)
            denominator = exp_term if denominator is None else denominator + exp_term
            weight = exp_term.astype(jnp.bfloat16).astype(jnp.float32)
            term = weight * s_ref[g * per : (g + 1) * per, :].astype(jnp.float32)
            summed = term if summed is None else summed + term
        o_ref[f * per : (f + 1) * per, :] = (summed / denominator).astype(o_ref.dtype)


def temporal_rows(q_src, q_block, keys, spatial_part, clip_counts, first_pos):
    rows, feat = keys.shape
    n_frames = clip_counts.shape[0]
    scalars = jnp.concatenate([first_pos.reshape(1), clip_counts]).astype(jnp.int32)
    grid_spec = pltpu.PrefetchScalarGridSpec(
        num_scalar_prefetch=1,
        grid=(feat // HD,),
        in_specs=[
            pl.BlockSpec((rows, HD), lambda h, sc: (q_block, h)),
            pl.BlockSpec((rows, HD), lambda h, sc: (0, h)),
            pl.BlockSpec((rows, HD), lambda h, sc: (0, h)),
        ],
        out_specs=pl.BlockSpec((rows, HD), lambda h, sc: (0, h)),
    )
    return pl.pallas_call(
        temporal_kernel,
        grid_spec=grid_spec,
        out_shape=jax.ShapeDtypeStruct((rows, feat), jnp.bfloat16),
        cost_estimate=pl.CostEstimate(
            flops=4 * rows * n_frames * feat,
            transcendentals=rows * n_frames * feat // HD,
            bytes_accessed=4 * rows * feat * 2,
        ),
    )(scalars, q_src, keys, spatial_part)


def local(tokens, mod_scale, mod_shift, w_qkv, w_out, neighbors, counts):
    tok_count = tokens.shape[1]
    feat_count = tokens.shape[2]
    n_frames = lax.axis_size("fy") * lax.axis_size("core")
    own = tokens[0]
    rims, crossed = exchange_tokens(own)
    piece_index = lax.axis_index("piece")
    above = jnp.where(piece_index > 0, rims[0], jnp.zeros_like(own))
    below = jnp.where(piece_index < lax.axis_size("piece") - 1, rims[1], jnp.zeros_like(own))
    core = lax.axis_index("core")
    half_rows = w_qkv.shape[0] // 2
    w_half = lax.dynamic_slice_in_dim(w_qkv, core * half_rows, half_rows, axis=0)
    w_pieces = lax.all_gather(w_half, ("fsdp", "core"), axis=0, tiled=False)
    w_full = w_pieces.reshape(lax.axis_size("fsdp"), w_qkv.shape[0], w_qkv.shape[1])
    out_rows = w_out.shape[0] // 2
    w_out_half = lax.dynamic_slice_in_dim(w_out, core * out_rows, out_rows, axis=0)
    w_out_half = lax.all_gather(w_out_half, "core", axis=0, tiled=True)
    w_out_full = lax.all_gather(w_out_half, "fsdp", axis=0, tiled=True)
    normed_all = layer_norm(
        jnp.concatenate([above, own, below], axis=0), mod_scale[0], mod_shift[0]
    )
    shard_cols = w_full.shape[2]
    w_query = jnp.concatenate(
        [w_full[0], w_full[1, :, : feat_count - shard_cols]], axis=1
    )
    normed_cross = layer_norm(crossed, mod_scale[0], mod_shift[0])
    w_key = jnp.concatenate(
        [w_full[1, :, feat_count - shard_cols :], w_full[2, :, : 2 * shard_cols - feat_count]], axis=1
    )
    q_both = jnp.dot(
        jnp.concatenate([normed_all[tok_count : 2 * tok_count], normed_cross], axis=0),
        w_query,
        preferred_element_type=jnp.float32,
    ).astype(jnp.bfloat16)
    queries = q_both[:tok_count]
    key_cross = jnp.dot(normed_cross, w_key, preferred_element_type=jnp.float32).astype(jnp.bfloat16)
    kv_all = jnp.einsum(
        "tk,jkc->jtc", normed_all, w_full[1:], preferred_element_type=jnp.float32
    ).astype(jnp.bfloat16)
    frame_index = lax.axis_index("fy") * lax.axis_size("core") + lax.axis_index("core")
    piece_index = lax.axis_index("piece")
    clip_counts = counts[0]
    count_here = lax.dynamic_index_in_dim(clip_counts, frame_index, 0, keepdims=False)
    rows_here = tok_count // (TGW * TILE)
    first_tile = (piece_index * rows_here - 1) * TGW
    spatial = spatial_rows(queries, kv_all, neighbors[0], first_tile, count_here)
    frame_axes = ("fy", "core")
    spatial_part = lax.all_to_all(spatial, frame_axes, split_axis=0, concat_axis=0, tiled=True)
    per_dev = tok_count // n_frames
    first_pos = piece_index * tok_count + frame_index * per_dev
    temporal = temporal_rows(q_both, 1, key_cross, spatial_part, clip_counts, first_pos)
    flat_temporal = lax.all_to_all(temporal, frame_axes, split_axis=0, concat_axis=0, tiled=True)
    projected = jnp.dot(flat_temporal, w_out_full, preferred_element_type=jnp.float32)
    return projected.astype(jnp.bfloat16).reshape(1, tok_count, feat_count)


def solution(mesh):
    n_fsdp = mesh.shape["fsdp"]
    n_sp = mesh.shape["sp"]
    split = Mesh(
        mesh.devices.reshape(n_fsdp, PIECES, n_sp // PIECES // 2, 2),
        ("fsdp", "piece", "fy", "core"),
    )
    seq = ("piece", "fy", "core")
    placed = (
        P("fsdp", seq, None),
        P("fsdp", None),
        P("fsdp", None),
        P(None, "fsdp"),
        P("fsdp", None),
        P("fsdp", seq, None),
        P("fsdp", None),
    )
    return jax.shard_map(
        local, mesh=split, in_specs=placed, out_specs=P("fsdp", seq, None), check_vma=False
    )
```

```python
import math

import jax
import jax.numpy as jnp
from jax import lax
from jax.experimental import pallas as pl
from jax.experimental.pallas import tpu as pltpu
from jax.sharding import Mesh
from jax.sharding import PartitionSpec as P

HEADS = 12
HD = 128
TILE = 128
TGW = 5
NBR = 6
PIECES = 4


def passed_along(block, axis, distance):
    devices = range(lax.axis_size(axis))
    route = [(i - distance, i) for i in devices if i - distance in devices]
    return lax.ppermute(block, axis, route)


def layer_norm(tokens, mod_scale, mod_shift):
    values_f32 = tokens.astype(jnp.float32)
    center = jnp.mean(values_f32, axis=-1, keepdims=True)
    spread = jnp.mean((values_f32 - center) ** 2, axis=-1, keepdims=True)
    normal = (values_f32 - center) / jnp.sqrt(spread + 1e-06)
    return (normal * (1.0 + mod_scale) + mod_shift).astype(jnp.bfloat16)


def spatial_kernel(list_ref, scalar_ref, q_ref, k_ref, v_ref, o_ref):
    scaling = 1.0 / math.sqrt(HD)
    first_tile = scalar_ref[0]
    count_here = scalar_ref[1]
    local_tiles = q_ref.shape[0] // TILE
    for t in range(local_tiles):
        query = q_ref[t * TILE : (t + 1) * TILE, :]
        parts = []
        row_max = None
        for n in range(NBR):
            tile_id = list_ref[t * NBR + n]
            start = pl.multiple_of((tile_id - first_tile) * TILE, TILE)
            key = k_ref[pl.ds(start, TILE), :]
            scores = (
                lax.dot_general(
                    query, key, (((1,), (1,)), ((), ())), preferred_element_type=jnp.float32
                )
                * scaling
            )
            key_pos = tile_id * TILE + lax.broadcasted_iota(jnp.int32, scores.shape, 1)
            live = key_pos < count_here
            scores = jnp.where(live, scores, -1e30)
            part_max = jnp.max(scores, axis=-1, keepdims=True)
            row_max = part_max if row_max is None else jnp.maximum(row_max, part_max)
            parts.append((scores, live, start))
        denominator = None
        summed = None
        for scores, live, start in parts:
            exp_terms = jnp.where(live, jnp.exp(scores - row_max), 0.0)
            part_sum = jnp.sum(exp_terms, axis=-1, keepdims=True)
            value = v_ref[pl.ds(start, TILE), :]
            part_out = jnp.dot(
                exp_terms.astype(jnp.bfloat16), value, preferred_element_type=jnp.float32
            )
            denominator = part_sum if denominator is None else denominator + part_sum
            summed = part_out if summed is None else summed + part_out
        o_ref[t * TILE : (t + 1) * TILE, :] = (summed / denominator).astype(o_ref.dtype)


def spatial_rows(queries, kv_all, tile_list, first_tile, count_here):
    buffer_rows = kv_all.shape[1]
    rows, feat = queries.shape
    per_shard = kv_all.shape[2] // HD
    scalars = jnp.stack([first_tile, count_here]).astype(jnp.int32)
    grid_spec = pltpu.PrefetchScalarGridSpec(
        num_scalar_prefetch=2,
        grid=(HEADS,),
        in_specs=[
            pl.BlockSpec((rows, HD), lambda h, lst, sc: (0, h)),
            pl.BlockSpec(
                (None, buffer_rows, HD),
                lambda h, lst, sc: ((HEADS + h) // per_shard - 1, 0, (HEADS + h) % per_shard),
            ),
            pl.BlockSpec(
                (None, buffer_rows, HD),
                lambda h, lst, sc: (
                    (2 * HEADS + h) // per_shard - 1,
                    0,
                    (2 * HEADS + h) % per_shard,
                ),
            ),
        ],
        out_specs=pl.BlockSpec((rows, HD), lambda h, lst, sc: (0, h)),
    )
    flops = 4 * rows * NBR * TILE * feat
    return pl.pallas_call(
        spatial_kernel,
        grid_spec=grid_spec,
        out_shape=jax.ShapeDtypeStruct((rows, feat), jnp.bfloat16),
        cost_estimate=pl.CostEstimate(
            flops=flops,
            transcendentals=rows * NBR * TILE * HEADS,
            bytes_accessed=2 * (rows * feat * 2 + buffer_rows * feat * 2),
        ),
    )(tile_list.reshape(-1).astype(jnp.int32), scalars, queries, kv_all, kv_all)


MESH_IDS = pl.DeviceIdType.MESH


def exchange_kernel(tok_ref, rim_ref, cross_ref, send_sem, recv_sem, cross_send, cross_recv, own_sem):
    n_piece = lax.axis_size("piece")
    n_core = lax.axis_size("core")
    n_frames = lax.axis_size("fy") * n_core
    piece = lax.axis_index("piece")
    frame = lax.axis_index("fy") * n_core + lax.axis_index("core")
    fsdp = lax.axis_index("fsdp")
    here = (fsdp, piece, lax.axis_index("fy"), lax.axis_index("core"))
    up = (fsdp, piece - 1, here[2], here[3])
    down = (fsdp, piece + 1, here[2], here[3])
    has_up = piece > 0
    has_down = piece < n_piece - 1
    per = tok_ref.shape[0] // n_frames
    peers = [(frame + k) % n_frames for k in range(1, n_frames)]
    barrier = pltpu.get_barrier_semaphore()

    @pl.when(has_up)
    def _():
        pl.semaphore_signal(barrier, inc=1, device_id=up, device_id_type=MESH_IDS)

    @pl.when(has_down)
    def _():
        pl.semaphore_signal(barrier, inc=1, device_id=down, device_id_type=MESH_IDS)

    for d in peers:
        pl.semaphore_signal(
            barrier, inc=1, device_id=(fsdp, piece, d // n_core, d % n_core), device_id_type=MESH_IDS
        )
    rim_peers = (piece + n_piece - 1) // n_piece + (2 * n_piece - 2 - piece) // n_piece
    pl.semaphore_wait(barrier, rim_peers + n_frames - 1)

    to_down = pltpu.make_async_remote_copy(
        src_ref=tok_ref,
        dst_ref=rim_ref.at[0],
        send_sem=send_sem.at[0],
        recv_sem=recv_sem.at[0],
        device_id=down,
        device_id_type=MESH_IDS,
    )
    to_up = pltpu.make_async_remote_copy(
        src_ref=tok_ref,
        dst_ref=rim_ref.at[1],
        send_sem=send_sem.at[1],
        recv_sem=recv_sem.at[1],
        device_id=up,
        device_id_type=MESH_IDS,
    )

    @pl.when(has_down)
    def _():
        to_down.start()

    @pl.when(has_up)
    def _():
        to_up.start()

    crosses = []
    for k, d in enumerate(peers):
        copy = pltpu.make_async_remote_copy(
            src_ref=tok_ref.at[pl.ds(pl.multiple_of(d * per, 16), per)],
            dst_ref=cross_ref.at[pl.ds(pl.multiple_of(frame * per, 16), per)],
            send_sem=cross_send.at[k],
            recv_sem=cross_recv.at[k],
            device_id=(fsdp, piece, d // n_core, d % n_core),
            device_id_type=MESH_IDS,
        )
        copy.start()
        crosses.append(copy)
    own_rows = pl.ds(pl.multiple_of(frame * per, 16), per)
    own_copy = pltpu.make_async_copy(tok_ref.at[own_rows], cross_ref.at[own_rows], own_sem)
    own_copy.start()

    @pl.when(has_down)
    def _():
        to_down.wait_send()
        to_up.wait_recv()

    @pl.when(has_up)
    def _():
        to_up.wait_send()
        to_down.wait_recv()

    for copy in crosses:
        copy.wait()
    own_copy.wait()


def exchange_tokens(own):
    rows, feat = own.shape
    return pl.pallas_call(
        exchange_kernel,
        out_shape=(
            jax.ShapeDtypeStruct((2, rows, feat), own.dtype),
            jax.ShapeDtypeStruct((rows, feat), own.dtype),
        ),
        in_specs=[pl.BlockSpec(memory_space=pl.ANY)],
        out_specs=(pl.BlockSpec(memory_space=pl.ANY), pl.BlockSpec(memory_space=pl.ANY)),
        scratch_shapes=[
            pltpu.SemaphoreType.DMA((2,)),
            pltpu.SemaphoreType.DMA((2,)),
            pltpu.SemaphoreType.DMA((8,)),
            pltpu.SemaphoreType.DMA((8,)),
            pltpu.SemaphoreType.DMA(()),
        ],
        compiler_params=pltpu.CompilerParams(collective_id=0, has_side_effects=True),
        cost_estimate=pl.CostEstimate(flops=0, transcendentals=0, bytes_accessed=80 * rows * feat * 2),
    )(own)


def temporal_weight_kernel(scalar_ref, q_ref, k_ref, w_ref):
    scaling = 1.0 / math.sqrt(HD)
    n_frames = scalar_ref.shape[0] - 1
    per = q_ref.shape[0] // n_frames
    position = scalar_ref[0] + lax.broadcasted_iota(jnp.int32, (per, 1), 0)
    live = [position < scalar_ref[1 + g] for g in range(n_frames)]
    keys = k_ref[...].astype(jnp.float32)
    ones = jnp.ones((HD, HD), jnp.bfloat16)
    lane = lax.broadcasted_iota(jnp.int32, (per, HD), 1)
    for f in range(n_frames):
        query = q_ref[f * per : (f + 1) * per, :].astype(jnp.float32)
        prod = jnp.concatenate([query] * n_frames, axis=0) * keys
        high = prod.astype(jnp.bfloat16)
        low = (prod - high.astype(jnp.float32)).astype(jnp.bfloat16)
        sums = jnp.dot(high, ones, preferred_element_type=jnp.float32) + jnp.dot(
            low, ones, preferred_element_type=jnp.float32
        )
        scores = []
        row_max = None
        for g in range(n_frames):
            score = jnp.where(live[g], sums[g * per : (g + 1) * per] * scaling, -1e30)
            row_max = score if row_max is None else jnp.maximum(row_max, score)
            scores.append(score)
        denominator = None
        packed = None
        for g in range(n_frames):
            exp_term = jnp.where(live[g], jnp.exp(scores[g] - row_max), 0.0)
            denominator = exp_term if denominator is None else denominator + exp_term
            weight = exp_term.astype(jnp.bfloat16).astype(jnp.float32)
            picked = jnp.where(lane == g, weight, 0.0)
            packed = picked if packed is None else packed + picked
        packed = packed + jnp.where(lane == n_frames, denominator, 0.0)
        w_ref[f * per : (f + 1) * per, :] = packed


def temporal_sum_kernel(w_ref, s_ref, o_ref):
    n_frames = 8
    per = s_ref.shape[0] // n_frames
    spatial = [s_ref[g * per : (g + 1) * per, :].astype(jnp.float32) for g in range(n_frames)]
    for f in range(n_frames):
        packed = w_ref[f * per : (f + 1) * per, :]
        summed = None
        for g in range(n_frames):
            term = packed[:, g : g + 1] * spatial[g]
            summed = term if summed is None else summed + term
        o_ref[f * per : (f + 1) * per, :] = (summed / packed[:, n_frames : n_frames + 1]).astype(
            o_ref.dtype
        )


def temporal_weights(q_src, q_block, keys, clip_counts, first_pos):
    rows, feat = keys.shape
    n_frames = clip_counts.shape[0]
    scalars = jnp.concatenate([first_pos.reshape(1), clip_counts]).astype(jnp.int32)
    grid_spec = pltpu.PrefetchScalarGridSpec(
        num_scalar_prefetch=1,
        grid=(feat // HD,),
        in_specs=[
            pl.BlockSpec((rows, HD), lambda h, sc: (q_block, h)),
            pl.BlockSpec((rows, HD), lambda h, sc: (0, h)),
        ],
        out_specs=pl.BlockSpec((None, rows, HD), lambda h, sc: (h, 0, 0)),
    )
    return pl.pallas_call(
        temporal_weight_kernel,
        grid_spec=grid_spec,
        out_shape=jax.ShapeDtypeStruct((feat // HD, rows, HD), jnp.float32),
        cost_estimate=pl.CostEstimate(
            flops=4 * rows * n_frames * feat * HD,
            transcendentals=rows * n_frames * feat,
            bytes_accessed=2 * rows * feat * 2 + rows * feat * 4,
        ),
    )(scalars, q_src, keys)


def temporal_sum(packed, spatial_part):
    rows, feat = spatial_part.shape
    return pl.pallas_call(
        temporal_sum_kernel,
        grid=(feat // HD,),
        in_specs=[
            pl.BlockSpec((None, rows, HD), lambda h: (h, 0, 0)),
            pl.BlockSpec((rows, HD), lambda h: (0, h)),
        ],
        out_specs=pl.BlockSpec((rows, HD), lambda h: (0, h)),
        out_shape=jax.ShapeDtypeStruct((rows, feat), jnp.bfloat16),
        cost_estimate=pl.CostEstimate(
            flops=2 * rows * 8 * feat, transcendentals=0, bytes_accessed=rows * feat * 8
        ),
    )(packed, spatial_part)


def local(tokens, mod_scale, mod_shift, w_qkv, w_out, neighbors, counts):
    tok_count = tokens.shape[1]
    feat_count = tokens.shape[2]
    n_frames = lax.axis_size("fy") * lax.axis_size("core")
    own = tokens[0]
    rims, crossed = exchange_tokens(own)
    piece_index = lax.axis_index("piece")
    above = jnp.where(piece_index > 0, rims[0], jnp.zeros_like(own))
    below = jnp.where(piece_index < lax.axis_size("piece") - 1, rims[1], jnp.zeros_like(own))
    core = lax.axis_index("core")
    half_rows = w_qkv.shape[0] // 2
    w_half = lax.dynamic_slice_in_dim(w_qkv, core * half_rows, half_rows, axis=0)
    w_pieces = lax.all_gather(w_half, ("fsdp", "core"), axis=0, tiled=False)
    w_full = w_pieces.reshape(lax.axis_size("fsdp"), w_qkv.shape[0], w_qkv.shape[1])
    out_rows = w_out.shape[0] // 2
    w_out_half = lax.dynamic_slice_in_dim(w_out, core * out_rows, out_rows, axis=0)
    w_out_half = lax.all_gather(w_out_half, "core", axis=0, tiled=True)
    w_out_full = lax.all_gather(w_out_half, "fsdp", axis=0, tiled=True)
    normed_all = layer_norm(
        jnp.concatenate([above, own, below], axis=0), mod_scale[0], mod_shift[0]
    )
    shard_cols = w_full.shape[2]
    w_query = jnp.concatenate(
        [w_full[0], w_full[1, :, : feat_count - shard_cols]], axis=1
    )
    normed_cross = layer_norm(crossed, mod_scale[0], mod_shift[0])
    w_key = jnp.concatenate(
        [w_full[1, :, feat_count - shard_cols :], w_full[2, :, : 2 * shard_cols - feat_count]], axis=1
    )
    q_both = jnp.dot(
        jnp.concatenate([normed_all[tok_count : 2 * tok_count], normed_cross], axis=0),
        w_query,
        preferred_element_type=jnp.float32,
    ).astype(jnp.bfloat16)
    queries = q_both[:tok_count]
    key_cross = jnp.dot(normed_cross, w_key, preferred_element_type=jnp.float32).astype(jnp.bfloat16)
    kv_all = jnp.einsum(
        "tk,jkc->jtc", normed_all, w_full[1:], preferred_element_type=jnp.float32
    ).astype(jnp.bfloat16)
    frame_index = lax.axis_index("fy") * lax.axis_size("core") + lax.axis_index("core")
    piece_index = lax.axis_index("piece")
    clip_counts = counts[0]
    count_here = lax.dynamic_index_in_dim(clip_counts, frame_index, 0, keepdims=False)
    rows_here = tok_count // (TGW * TILE)
    first_tile = (piece_index * rows_here - 1) * TGW
    spatial = spatial_rows(queries, kv_all, neighbors[0], first_tile, count_here)
    frame_axes = ("fy", "core")
    spatial_part = lax.all_to_all(spatial, frame_axes, split_axis=0, concat_axis=0, tiled=True)
    per_dev = tok_count // n_frames
    first_pos = piece_index * tok_count + frame_index * per_dev
    packed = temporal_weights(q_both, 1, key_cross, clip_counts, first_pos)
    temporal = temporal_sum(packed, spatial_part)
    flat_temporal = lax.all_to_all(temporal, frame_axes, split_axis=0, concat_axis=0, tiled=True)
    projected = jnp.dot(flat_temporal, w_out_full, preferred_element_type=jnp.float32)
    return projected.astype(jnp.bfloat16).reshape(1, tok_count, feat_count)


def solution(mesh):
    n_fsdp = mesh.shape["fsdp"]
    n_sp = mesh.shape["sp"]
    split = Mesh(
        mesh.devices.reshape(n_fsdp, PIECES, n_sp // PIECES // 2, 2),
        ("fsdp", "piece", "fy", "core"),
    )
    seq = ("piece", "fy", "core")
    placed = (
        P("fsdp", seq, None),
        P("fsdp", None),
        P("fsdp", None),
        P(None, "fsdp"),
        P("fsdp", None),
        P("fsdp", seq, None),
        P("fsdp", None),
    )
    return jax.shard_map(
        local, mesh=split, in_specs=placed, out_specs=P("fsdp", seq, None), check_vma=False
    )
```

```python
import math

import jax
import jax.numpy as jnp
from jax import lax
from jax.experimental import pallas as pl
from jax.experimental.pallas import tpu as pltpu
from jax.sharding import Mesh
from jax.sharding import PartitionSpec as P

HEADS = 12
HD = 128
TILE = 128
TGW = 5
NBR = 6
PIECES = 4


def passed_along(block, axis, distance):
    devices = range(lax.axis_size(axis))
    route = [(i - distance, i) for i in devices if i - distance in devices]
    return lax.ppermute(block, axis, route)


def layer_norm(tokens, mod_scale, mod_shift):
    values_f32 = tokens.astype(jnp.float32)
    center = jnp.mean(values_f32, axis=-1, keepdims=True)
    spread = jnp.mean((values_f32 - center) ** 2, axis=-1, keepdims=True)
    normal = (values_f32 - center) / jnp.sqrt(spread + 1e-06)
    return (normal * (1.0 + mod_scale) + mod_shift).astype(jnp.bfloat16)


def spatial_kernel(list_ref, scalar_ref, q_ref, k_ref, v_ref, o_ref):
    scaling = 1.0 / math.sqrt(HD)
    first_tile = scalar_ref[0]
    count_here = scalar_ref[1]
    local_tiles = q_ref.shape[0] // TILE
    for t in range(local_tiles):
        query = q_ref[t * TILE : (t + 1) * TILE, :]
        parts = []
        block_max = None
        for n in range(NBR):
            tile_id = list_ref[t * NBR + n]
            start = pl.multiple_of((tile_id - first_tile) * TILE, TILE)
            key = k_ref[pl.ds(start, TILE), :]
            scores = (
                lax.dot_general(
                    query, key, (((1,), (1,)), ((), ())), preferred_element_type=jnp.float32
                )
                * scaling
            )
            key_pos = tile_id * TILE + lax.broadcasted_iota(jnp.int32, scores.shape, 1)
            live = key_pos < count_here
            scores = jnp.where(live, scores, -1e30)
            block_max = scores if block_max is None else jnp.maximum(block_max, scores)
            parts.append((scores, live, start))
        row_max = jnp.max(block_max, axis=-1, keepdims=True)
        exp_total = None
        summed = None
        for scores, live, start in parts:
            exp_terms = jnp.where(live, jnp.exp(scores - row_max), 0.0)
            value = v_ref[pl.ds(start, TILE), :]
            part_out = jnp.dot(
                exp_terms.astype(jnp.bfloat16), value, preferred_element_type=jnp.float32
            )
            exp_total = exp_terms if exp_total is None else exp_total + exp_terms
            summed = part_out if summed is None else summed + part_out
        denominator = jnp.sum(exp_total, axis=-1, keepdims=True)
        o_ref[t * TILE : (t + 1) * TILE, :] = (summed / denominator).astype(o_ref.dtype)


def spatial_rows(queries, kv_all, tile_list, first_tile, count_here):
    buffer_rows = kv_all.shape[1]
    rows, feat = queries.shape
    per_shard = kv_all.shape[2] // HD
    scalars = jnp.stack([first_tile, count_here]).astype(jnp.int32)
    grid_spec = pltpu.PrefetchScalarGridSpec(
        num_scalar_prefetch=2,
        grid=(HEADS,),
        in_specs=[
            pl.BlockSpec((rows, HD), lambda h, lst, sc: (0, h)),
            pl.BlockSpec(
                (None, buffer_rows, HD),
                lambda h, lst, sc: ((HEADS + h) // per_shard - 1, 0, (HEADS + h) % per_shard),
            ),
            pl.BlockSpec(
                (None, buffer_rows, HD),
                lambda h, lst, sc: (
                    (2 * HEADS + h) // per_shard - 1,
                    0,
                    (2 * HEADS + h) % per_shard,
                ),
            ),
        ],
        out_specs=pl.BlockSpec((rows, HD), lambda h, lst, sc: (0, h)),
    )
    flops = 4 * rows * NBR * TILE * feat
    return pl.pallas_call(
        spatial_kernel,
        grid_spec=grid_spec,
        out_shape=jax.ShapeDtypeStruct((rows, feat), jnp.bfloat16),
        cost_estimate=pl.CostEstimate(
            flops=flops,
            transcendentals=rows * NBR * TILE * HEADS,
            bytes_accessed=2 * (rows * feat * 2 + buffer_rows * feat * 2),
        ),
    )(tile_list.reshape(-1).astype(jnp.int32), scalars, queries, kv_all, kv_all)


MESH_IDS = pl.DeviceIdType.MESH


def exchange_kernel(tok_ref, rim_ref, cross_ref, send_sem, recv_sem, cross_send, cross_recv, own_sem):
    n_piece = lax.axis_size("piece")
    n_core = lax.axis_size("core")
    n_frames = lax.axis_size("fy") * n_core
    piece = lax.axis_index("piece")
    frame = lax.axis_index("fy") * n_core + lax.axis_index("core")
    fsdp = lax.axis_index("fsdp")
    here = (fsdp, piece, lax.axis_index("fy"), lax.axis_index("core"))
    up = (fsdp, piece - 1, here[2], here[3])
    down = (fsdp, piece + 1, here[2], here[3])
    has_up = piece > 0
    has_down = piece < n_piece - 1
    per = tok_ref.shape[0] // n_frames
    peers = [(frame + k) % n_frames for k in range(1, n_frames)]
    barrier = pltpu.get_barrier_semaphore()

    @pl.when(has_up)
    def _():
        pl.semaphore_signal(barrier, inc=1, device_id=up, device_id_type=MESH_IDS)

    @pl.when(has_down)
    def _():
        pl.semaphore_signal(barrier, inc=1, device_id=down, device_id_type=MESH_IDS)

    for d in peers:
        pl.semaphore_signal(
            barrier, inc=1, device_id=(fsdp, piece, d // n_core, d % n_core), device_id_type=MESH_IDS
        )
    rim_peers = (piece + n_piece - 1) // n_piece + (2 * n_piece - 2 - piece) // n_piece
    pl.semaphore_wait(barrier, rim_peers + n_frames - 1)

    to_down = pltpu.make_async_remote_copy(
        src_ref=tok_ref,
        dst_ref=rim_ref.at[0],
        send_sem=send_sem.at[0],
        recv_sem=recv_sem.at[0],
        device_id=down,
        device_id_type=MESH_IDS,
    )
    to_up = pltpu.make_async_remote_copy(
        src_ref=tok_ref,
        dst_ref=rim_ref.at[1],
        send_sem=send_sem.at[1],
        recv_sem=recv_sem.at[1],
        device_id=up,
        device_id_type=MESH_IDS,
    )

    @pl.when(has_down)
    def _():
        to_down.start()

    @pl.when(has_up)
    def _():
        to_up.start()

    crosses = []
    for k, d in enumerate(peers):
        copy = pltpu.make_async_remote_copy(
            src_ref=tok_ref.at[pl.ds(pl.multiple_of(d * per, 16), per)],
            dst_ref=cross_ref.at[pl.ds(pl.multiple_of(frame * per, 16), per)],
            send_sem=cross_send.at[k],
            recv_sem=cross_recv.at[k],
            device_id=(fsdp, piece, d // n_core, d % n_core),
            device_id_type=MESH_IDS,
        )
        copy.start()
        crosses.append(copy)
    own_rows = pl.ds(pl.multiple_of(frame * per, 16), per)
    own_copy = pltpu.make_async_copy(tok_ref.at[own_rows], cross_ref.at[own_rows], own_sem)
    own_copy.start()

    @pl.when(has_down)
    def _():
        to_down.wait_send()
        to_up.wait_recv()

    @pl.when(has_up)
    def _():
        to_up.wait_send()
        to_down.wait_recv()

    for copy in crosses:
        copy.wait()
    own_copy.wait()


def exchange_tokens(own):
    rows, feat = own.shape
    return pl.pallas_call(
        exchange_kernel,
        out_shape=(
            jax.ShapeDtypeStruct((2, rows, feat), own.dtype),
            jax.ShapeDtypeStruct((rows, feat), own.dtype),
        ),
        in_specs=[pl.BlockSpec(memory_space=pl.ANY)],
        out_specs=(pl.BlockSpec(memory_space=pl.ANY), pl.BlockSpec(memory_space=pl.ANY)),
        scratch_shapes=[
            pltpu.SemaphoreType.DMA((2,)),
            pltpu.SemaphoreType.DMA((2,)),
            pltpu.SemaphoreType.DMA((8,)),
            pltpu.SemaphoreType.DMA((8,)),
            pltpu.SemaphoreType.DMA(()),
        ],
        compiler_params=pltpu.CompilerParams(collective_id=0, has_side_effects=True),
        cost_estimate=pl.CostEstimate(flops=0, transcendentals=0, bytes_accessed=80 * rows * feat * 2),
    )(own)


def temporal_block(query_part, key_part, spatial_part, clip_counts, first_pos):
    n_frames, per_dev = query_part.shape[0], query_part.shape[1]
    scaling = 1.0 / math.sqrt(HD)
    position = first_pos + jnp.arange(per_dev, dtype=jnp.int32)
    live_mask = (position[:, None] < clip_counts[None, :])[:, None, None, :]
    scores = (
        jnp.einsum(
            "fphd,gphd->phfg", query_part, key_part, preferred_element_type=jnp.float32
        )
        * scaling
    )
    scores = jnp.where(live_mask, scores, -1e30)
    row_max = jnp.max(scores, axis=-1, keepdims=True)
    exp_terms = jnp.where(live_mask, jnp.exp(scores - row_max), 0.0)
    denominator = jnp.sum(exp_terms, axis=-1, keepdims=True)
    weights = exp_terms.astype(jnp.bfloat16)
    summed = jnp.einsum(
        "phfg,gphd->fphd", weights, spatial_part, preferred_element_type=jnp.float32
    )
    result = summed / jnp.transpose(denominator, (2, 0, 1, 3))
    return result.astype(jnp.bfloat16)


def local(tokens, mod_scale, mod_shift, w_qkv, w_out, neighbors, counts):
    tok_count = tokens.shape[1]
    feat_count = tokens.shape[2]
    n_frames = lax.axis_size("fy") * lax.axis_size("core")
    own = tokens[0]
    rims, crossed = exchange_tokens(own)
    piece_index = lax.axis_index("piece")
    above = jnp.where(piece_index > 0, rims[0], jnp.zeros_like(own))
    below = jnp.where(piece_index < lax.axis_size("piece") - 1, rims[1], jnp.zeros_like(own))
    core = lax.axis_index("core")
    half_rows = w_qkv.shape[0] // 2
    w_half = lax.dynamic_slice_in_dim(w_qkv, core * half_rows, half_rows, axis=0)
    w_pieces = lax.all_gather(w_half, ("fsdp", "core"), axis=0, tiled=False)
    w_full = w_pieces.reshape(lax.axis_size("fsdp"), w_qkv.shape[0], w_qkv.shape[1])
    out_rows = w_out.shape[0] // 2
    w_out_half = lax.dynamic_slice_in_dim(w_out, core * out_rows, out_rows, axis=0)
    w_out_half = lax.all_gather(w_out_half, "core", axis=0, tiled=True)
    w_out_full = lax.all_gather(w_out_half, "fsdp", axis=0, tiled=True)
    normed_all = layer_norm(
        jnp.concatenate([above, own, below], axis=0), mod_scale[0], mod_shift[0]
    )
    shard_cols = w_full.shape[2]
    w_query = jnp.concatenate(
        [w_full[0], w_full[1, :, : feat_count - shard_cols]], axis=1
    )
    normed_cross = layer_norm(crossed, mod_scale[0], mod_shift[0])
    w_key = jnp.concatenate(
        [w_full[1, :, feat_count - shard_cols :], w_full[2, :, : 2 * shard_cols - feat_count]], axis=1
    )
    q_both = jnp.dot(
        jnp.concatenate([normed_all[tok_count : 2 * tok_count], normed_cross], axis=0),
        w_query,
        preferred_element_type=jnp.float32,
    ).astype(jnp.bfloat16)
    queries = q_both[:tok_count]
    key_cross = jnp.dot(normed_cross, w_key, preferred_element_type=jnp.float32).astype(jnp.bfloat16)
    kv_all = jnp.einsum(
        "tk,jkc->jtc", normed_all, w_full[1:], preferred_element_type=jnp.float32
    ).astype(jnp.bfloat16)
    frame_index = lax.axis_index("fy") * lax.axis_size("core") + lax.axis_index("core")
    piece_index = lax.axis_index("piece")
    clip_counts = counts[0]
    count_here = lax.dynamic_index_in_dim(clip_counts, frame_index, 0, keepdims=False)
    rows_here = tok_count // (TGW * TILE)
    first_tile = (piece_index * rows_here - 1) * TGW
    spatial = spatial_rows(queries, kv_all, neighbors[0], first_tile, count_here)
    frame_axes = ("fy", "core")
    spatial_part = lax.all_to_all(spatial, frame_axes, split_axis=0, concat_axis=0, tiled=True)
    per_dev = tok_count // n_frames
    first_pos = piece_index * tok_count + frame_index * per_dev
    part_shape = (n_frames, per_dev, HEADS, HD)
    temporal = temporal_block(
        q_both[tok_count:].reshape(part_shape),
        key_cross.reshape(part_shape),
        spatial_part.reshape(part_shape),
        clip_counts,
        first_pos,
    )
    flat_temporal = lax.all_to_all(
        temporal.reshape(tok_count, feat_count), frame_axes, split_axis=0, concat_axis=0, tiled=True
    )
    projected = jnp.dot(flat_temporal, w_out_full, preferred_element_type=jnp.float32)
    return projected.astype(jnp.bfloat16).reshape(1, tok_count, feat_count)


def solution(mesh):
    n_fsdp = mesh.shape["fsdp"]
    n_sp = mesh.shape["sp"]
    split = Mesh(
        mesh.devices.reshape(n_fsdp, PIECES, n_sp // PIECES // 2, 2),
        ("fsdp", "piece", "fy", "core"),
    )
    seq = ("piece", "fy", "core")
    placed = (
        P("fsdp", seq, None),
        P("fsdp", None),
        P("fsdp", None),
        P(None, "fsdp"),
        P("fsdp", None),
        P("fsdp", seq, None),
        P("fsdp", None),
    )
    return jax.shard_map(
        local, mesh=split, in_specs=placed, out_specs=P("fsdp", seq, None), check_vma=False
    )
```

```python
import math

import jax
import jax.numpy as jnp
from jax import lax
from jax.experimental import pallas as pl
from jax.experimental.pallas import tpu as pltpu
from jax.sharding import Mesh
from jax.sharding import PartitionSpec as P

HEADS = 12
HD = 128
TILE = 128
TGW = 5
NBR = 6
PIECES = 4


def passed_along(block, axis, distance):
    devices = range(lax.axis_size(axis))
    route = [(i - distance, i) for i in devices if i - distance in devices]
    return lax.ppermute(block, axis, route)


def layer_norm(tokens, mod_scale, mod_shift):
    values_f32 = tokens.astype(jnp.float32)
    center = jnp.mean(values_f32, axis=-1, keepdims=True)
    spread = jnp.mean((values_f32 - center) ** 2, axis=-1, keepdims=True)
    normal = (values_f32 - center) / jnp.sqrt(spread + 1e-06)
    return (normal * (1.0 + mod_scale) + mod_shift).astype(jnp.bfloat16)


def spatial_kernel(list_ref, scalar_ref, q_ref, k_ref, v_ref, o_ref):
    scaling = 1.0 / math.sqrt(HD)
    first_tile = scalar_ref[0]
    count_here = scalar_ref[1]
    local_tiles = q_ref.shape[0] // TILE
    for t in range(local_tiles):
        query = q_ref[t * TILE : (t + 1) * TILE, :]
        parts = []
        block_max = None
        for n in range(NBR):
            tile_id = list_ref[t * NBR + n]
            start = pl.multiple_of((tile_id - first_tile) * TILE, TILE)
            key = k_ref[pl.ds(start, TILE), :]
            scores = (
                lax.dot_general(
                    query, key, (((1,), (1,)), ((), ())), preferred_element_type=jnp.float32
                )
                * scaling
            )
            key_pos = tile_id * TILE + lax.broadcasted_iota(jnp.int32, (1, TILE), 1)
            scores = scores + jnp.where(key_pos < count_here, 0.0, -1e30)
            block_max = scores if block_max is None else jnp.maximum(block_max, scores)
            parts.append((scores, start))
        row_max = jnp.max(block_max, axis=-1, keepdims=True)
        exp_total = None
        summed = None
        for scores, start in parts:
            exp_terms = jnp.exp(scores - row_max)
            value = v_ref[pl.ds(start, TILE), :]
            part_out = jnp.dot(
                exp_terms.astype(jnp.bfloat16), value, preferred_element_type=jnp.float32
            )
            exp_total = exp_terms if exp_total is None else exp_total + exp_terms
            summed = part_out if summed is None else summed + part_out
        denominator = jnp.sum(exp_total, axis=-1, keepdims=True)
        o_ref[t * TILE : (t + 1) * TILE, :] = (summed / denominator).astype(o_ref.dtype)


def spatial_rows(queries, kv_all, tile_list, first_tile, count_here):
    buffer_rows = kv_all.shape[1]
    rows, feat = queries.shape
    per_shard = kv_all.shape[2] // HD
    scalars = jnp.stack([first_tile, count_here]).astype(jnp.int32)
    grid_spec = pltpu.PrefetchScalarGridSpec(
        num_scalar_prefetch=2,
        grid=(HEADS,),
        in_specs=[
            pl.BlockSpec((rows, HD), lambda h, lst, sc: (0, h)),
            pl.BlockSpec(
                (None, buffer_rows, HD),
                lambda h, lst, sc: ((HEADS + h) // per_shard - 1, 0, (HEADS + h) % per_shard),
            ),
            pl.BlockSpec(
                (None, buffer_rows, HD),
                lambda h, lst, sc: (
                    (2 * HEADS + h) // per_shard - 1,
                    0,
                    (2 * HEADS + h) % per_shard,
                ),
            ),
        ],
        out_specs=pl.BlockSpec((rows, HD), lambda h, lst, sc: (0, h)),
    )
    flops = 4 * rows * NBR * TILE * feat
    return pl.pallas_call(
        spatial_kernel,
        grid_spec=grid_spec,
        out_shape=jax.ShapeDtypeStruct((rows, feat), jnp.bfloat16),
        cost_estimate=pl.CostEstimate(
            flops=flops,
            transcendentals=rows * NBR * TILE * HEADS,
            bytes_accessed=2 * (rows * feat * 2 + buffer_rows * feat * 2),
        ),
    )(tile_list.reshape(-1).astype(jnp.int32), scalars, queries, kv_all, kv_all)


MESH_IDS = pl.DeviceIdType.MESH


def exchange_kernel(tok_ref, rim_ref, cross_ref, send_sem, recv_sem, cross_send, cross_recv, own_sem):
    n_piece = lax.axis_size("piece")
    n_core = lax.axis_size("core")
    n_frames = lax.axis_size("fy") * n_core
    piece = lax.axis_index("piece")
    frame = lax.axis_index("fy") * n_core + lax.axis_index("core")
    fsdp = lax.axis_index("fsdp")
    here = (fsdp, piece, lax.axis_index("fy"), lax.axis_index("core"))
    up = (fsdp, piece - 1, here[2], here[3])
    down = (fsdp, piece + 1, here[2], here[3])
    has_up = piece > 0
    has_down = piece < n_piece - 1
    per = tok_ref.shape[0] // n_frames
    peers = [(frame + k) % n_frames for k in range(1, n_frames)]
    barrier = pltpu.get_barrier_semaphore()

    @pl.when(has_up)
    def _():
        pl.semaphore_signal(barrier, inc=1, device_id=up, device_id_type=MESH_IDS)

    @pl.when(has_down)
    def _():
        pl.semaphore_signal(barrier, inc=1, device_id=down, device_id_type=MESH_IDS)

    for d in peers:
        pl.semaphore_signal(
            barrier, inc=1, device_id=(fsdp, piece, d // n_core, d % n_core), device_id_type=MESH_IDS
        )
    rim_peers = (piece + n_piece - 1) // n_piece + (2 * n_piece - 2 - piece) // n_piece
    pl.semaphore_wait(barrier, rim_peers + n_frames - 1)

    to_down = pltpu.make_async_remote_copy(
        src_ref=tok_ref,
        dst_ref=rim_ref.at[0],
        send_sem=send_sem.at[0],
        recv_sem=recv_sem.at[0],
        device_id=down,
        device_id_type=MESH_IDS,
    )
    to_up = pltpu.make_async_remote_copy(
        src_ref=tok_ref,
        dst_ref=rim_ref.at[1],
        send_sem=send_sem.at[1],
        recv_sem=recv_sem.at[1],
        device_id=up,
        device_id_type=MESH_IDS,
    )

    @pl.when(has_down)
    def _():
        to_down.start()

    @pl.when(has_up)
    def _():
        to_up.start()

    crosses = []
    for k, d in enumerate(peers):
        copy = pltpu.make_async_remote_copy(
            src_ref=tok_ref.at[pl.ds(pl.multiple_of(d * per, 16), per)],
            dst_ref=cross_ref.at[pl.ds(pl.multiple_of(frame * per, 16), per)],
            send_sem=cross_send.at[k],
            recv_sem=cross_recv.at[k],
            device_id=(fsdp, piece, d // n_core, d % n_core),
            device_id_type=MESH_IDS,
        )
        copy.start()
        crosses.append(copy)
    own_rows = pl.ds(pl.multiple_of(frame * per, 16), per)
    own_copy = pltpu.make_async_copy(tok_ref.at[own_rows], cross_ref.at[own_rows], own_sem)
    own_copy.start()

    @pl.when(has_down)
    def _():
        to_down.wait_send()
        to_up.wait_recv()

    @pl.when(has_up)
    def _():
        to_up.wait_send()
        to_down.wait_recv()

    for copy in crosses:
        copy.wait()
    own_copy.wait()


def exchange_tokens(own):
    rows, feat = own.shape
    return pl.pallas_call(
        exchange_kernel,
        out_shape=(
            jax.ShapeDtypeStruct((2, rows, feat), own.dtype),
            jax.ShapeDtypeStruct((rows, feat), own.dtype),
        ),
        in_specs=[pl.BlockSpec(memory_space=pl.ANY)],
        out_specs=(pl.BlockSpec(memory_space=pl.ANY), pl.BlockSpec(memory_space=pl.ANY)),
        scratch_shapes=[
            pltpu.SemaphoreType.DMA((2,)),
            pltpu.SemaphoreType.DMA((2,)),
            pltpu.SemaphoreType.DMA((8,)),
            pltpu.SemaphoreType.DMA((8,)),
            pltpu.SemaphoreType.DMA(()),
        ],
        compiler_params=pltpu.CompilerParams(collective_id=0, has_side_effects=True),
        cost_estimate=pl.CostEstimate(flops=0, transcendentals=0, bytes_accessed=80 * rows * feat * 2),
    )(own)


def temporal_block(query_part, key_part, spatial_part, clip_counts, first_pos):
    n_frames, per_dev = query_part.shape[0], query_part.shape[1]
    scaling = 1.0 / math.sqrt(HD)
    position = first_pos + jnp.arange(per_dev, dtype=jnp.int32)
    live_mask = (position[:, None] < clip_counts[None, :])[:, None, None, :]
    scores = (
        jnp.einsum(
            "fphd,gphd->phfg", query_part, key_part, preferred_element_type=jnp.float32
        )
        * scaling
    )
    scores = jnp.where(live_mask, scores, -1e30)
    row_max = jnp.max(scores, axis=-1, keepdims=True)
    exp_terms = jnp.where(live_mask, jnp.exp(scores - row_max), 0.0)
    denominator = jnp.sum(exp_terms, axis=-1, keepdims=True)
    weights = exp_terms.astype(jnp.bfloat16)
    summed = jnp.einsum(
        "phfg,gphd->fphd", weights, spatial_part, preferred_element_type=jnp.float32
    )
    result = summed / jnp.transpose(denominator, (2, 0, 1, 3))
    return result.astype(jnp.bfloat16)


def local(tokens, mod_scale, mod_shift, w_qkv, w_out, neighbors, counts):
    tok_count = tokens.shape[1]
    feat_count = tokens.shape[2]
    n_frames = lax.axis_size("fy") * lax.axis_size("core")
    own = tokens[0]
    rims, crossed = exchange_tokens(own)
    piece_index = lax.axis_index("piece")
    above = jnp.where(piece_index > 0, rims[0], jnp.zeros_like(own))
    below = jnp.where(piece_index < lax.axis_size("piece") - 1, rims[1], jnp.zeros_like(own))
    core = lax.axis_index("core")
    half_rows = w_qkv.shape[0] // 2
    w_half = lax.dynamic_slice_in_dim(w_qkv, core * half_rows, half_rows, axis=0)
    w_pieces = lax.all_gather(w_half, ("fsdp", "core"), axis=0, tiled=False)
    w_full = w_pieces.reshape(lax.axis_size("fsdp"), w_qkv.shape[0], w_qkv.shape[1])
    out_rows = w_out.shape[0] // 2
    w_out_half = lax.dynamic_slice_in_dim(w_out, core * out_rows, out_rows, axis=0)
    w_out_half = lax.all_gather(w_out_half, "core", axis=0, tiled=True)
    w_out_full = lax.all_gather(w_out_half, "fsdp", axis=0, tiled=True)
    normed_all = layer_norm(
        jnp.concatenate([above, own, below], axis=0), mod_scale[0], mod_shift[0]
    )
    shard_cols = w_full.shape[2]
    w_query = jnp.concatenate(
        [w_full[0], w_full[1, :, : feat_count - shard_cols]], axis=1
    )
    normed_cross = layer_norm(crossed, mod_scale[0], mod_shift[0])
    w_key = jnp.concatenate(
        [w_full[1, :, feat_count - shard_cols :], w_full[2, :, : 2 * shard_cols - feat_count]], axis=1
    )
    q_both = jnp.dot(
        jnp.concatenate([normed_all[tok_count : 2 * tok_count], normed_cross], axis=0),
        w_query,
        preferred_element_type=jnp.float32,
    ).astype(jnp.bfloat16)
    queries = q_both[:tok_count]
    key_cross = jnp.dot(normed_cross, w_key, preferred_element_type=jnp.float32).astype(jnp.bfloat16)
    kv_all = jnp.einsum(
        "tk,jkc->jtc", normed_all, w_full[1:], preferred_element_type=jnp.float32
    ).astype(jnp.bfloat16)
    frame_index = lax.axis_index("fy") * lax.axis_size("core") + lax.axis_index("core")
    piece_index = lax.axis_index("piece")
    clip_counts = counts[0]
    count_here = lax.dynamic_index_in_dim(clip_counts, frame_index, 0, keepdims=False)
    rows_here = tok_count // (TGW * TILE)
    first_tile = (piece_index * rows_here - 1) * TGW
    spatial = spatial_rows(queries, kv_all, neighbors[0], first_tile, count_here)
    frame_axes = ("fy", "core")
    spatial_part = lax.all_to_all(spatial, frame_axes, split_axis=0, concat_axis=0, tiled=True)
    per_dev = tok_count // n_frames
    first_pos = piece_index * tok_count + frame_index * per_dev
    part_shape = (n_frames, per_dev, HEADS, HD)
    temporal = temporal_block(
        q_both[tok_count:].reshape(part_shape),
        key_cross.reshape(part_shape),
        spatial_part.reshape(part_shape),
        clip_counts,
        first_pos,
    )
    flat_temporal = lax.all_to_all(
        temporal.reshape(tok_count, feat_count), frame_axes, split_axis=0, concat_axis=0, tiled=True
    )
    projected = jnp.dot(flat_temporal, w_out_full, preferred_element_type=jnp.float32)
    return projected.astype(jnp.bfloat16).reshape(1, tok_count, feat_count)


def solution(mesh):
    n_fsdp = mesh.shape["fsdp"]
    n_sp = mesh.shape["sp"]
    split = Mesh(
        mesh.devices.reshape(n_fsdp, PIECES, n_sp // PIECES // 2, 2),
        ("fsdp", "piece", "fy", "core"),
    )
    seq = ("piece", "fy", "core")
    placed = (
        P("fsdp", seq, None),
        P("fsdp", None),
        P("fsdp", None),
        P(None, "fsdp"),
        P("fsdp", None),
        P("fsdp", seq, None),
        P("fsdp", None),
    )
    return jax.shard_map(
        local, mesh=split, in_specs=placed, out_specs=P("fsdp", seq, None), check_vma=False
    )
```

```python
import math

import jax
import jax.numpy as jnp
from jax import lax
from jax.experimental import pallas as pl
from jax.experimental.pallas import tpu as pltpu
from jax.sharding import Mesh
from jax.sharding import PartitionSpec as P

HEADS = 12
HD = 128
TILE = 128
TGW = 5
NBR = 6
PIECES = 4


def passed_along(block, axis, distance):
    devices = range(lax.axis_size(axis))
    route = [(i - distance, i) for i in devices if i - distance in devices]
    return lax.ppermute(block, axis, route)


def layer_norm(tokens, mod_scale, mod_shift):
    values_f32 = tokens.astype(jnp.float32)
    center = jnp.mean(values_f32, axis=-1, keepdims=True)
    spread = jnp.mean((values_f32 - center) ** 2, axis=-1, keepdims=True)
    normal = (values_f32 - center) / jnp.sqrt(spread + 1e-06)
    return (normal * (1.0 + mod_scale) + mod_shift).astype(jnp.bfloat16)


def spatial_kernel(list_ref, scalar_ref, q_ref, k_ref, v_ref, o_ref):
    scaling = 1.0 / math.sqrt(HD)
    first_tile = scalar_ref[0]
    count_here = scalar_ref[1]
    local_tiles = q_ref.shape[0] // TILE
    for t, c in [(t, c) for c in range(q_ref.shape[1] // HD) for t in range(local_tiles)]:
        cols = slice(c * HD, (c + 1) * HD)
        query = q_ref[t * TILE : (t + 1) * TILE, cols]
        parts = []
        block_max = None
        for n in range(NBR):
            tile_id = list_ref[t * NBR + n]
            start = pl.multiple_of((tile_id - first_tile) * TILE, TILE)
            key = k_ref[pl.ds(start, TILE), cols]
            scores = (
                lax.dot_general(
                    query, key, (((1,), (1,)), ((), ())), preferred_element_type=jnp.float32
                )
                * scaling
            )
            key_pos = tile_id * TILE + lax.broadcasted_iota(jnp.int32, (1, TILE), 1)
            scores = scores + jnp.where(key_pos < count_here, 0.0, -1e30)
            block_max = scores if block_max is None else jnp.maximum(block_max, scores)
            parts.append((scores, start))
        row_max = jnp.max(block_max, axis=-1, keepdims=True)
        exp_total = None
        summed = None
        for scores, start in parts:
            exp_terms = jnp.exp(scores - row_max)
            value = v_ref[pl.ds(start, TILE), cols]
            part_out = jnp.dot(
                exp_terms.astype(jnp.bfloat16), value, preferred_element_type=jnp.float32
            )
            exp_total = exp_terms if exp_total is None else exp_total + exp_terms
            summed = part_out if summed is None else summed + part_out
        denominator = jnp.sum(exp_total, axis=-1, keepdims=True)
        o_ref[t * TILE : (t + 1) * TILE, cols] = (summed / denominator).astype(o_ref.dtype)


def spatial_rows(queries, kv_all, tile_list, first_tile, count_here):
    buffer_rows = kv_all.shape[1]
    rows, feat = queries.shape
    scalars = jnp.stack([first_tile, count_here]).astype(jnp.int32)
    width = 3 * HD
    per_shard = kv_all.shape[2] // width
    k0 = feat // width
    grid_spec = pltpu.PrefetchScalarGridSpec(
        num_scalar_prefetch=2,
        grid=(feat // width,),
        in_specs=[
            pl.BlockSpec((rows, width), lambda g, lst, sc: (0, g)),
            pl.BlockSpec(
                (None, buffer_rows, width),
                lambda g, lst, sc: ((k0 + g) // per_shard - 1, 0, (k0 + g) % per_shard),
            ),
            pl.BlockSpec(
                (None, buffer_rows, width),
                lambda g, lst, sc: ((2 * k0 + g) // per_shard - 1, 0, (2 * k0 + g) % per_shard),
            ),
        ],
        out_specs=pl.BlockSpec((rows, width), lambda g, lst, sc: (0, g)),
    )
    flops = 4 * rows * NBR * TILE * feat
    return pl.pallas_call(
        spatial_kernel,
        grid_spec=grid_spec,
        out_shape=jax.ShapeDtypeStruct((rows, feat), jnp.bfloat16),
        cost_estimate=pl.CostEstimate(
            flops=flops,
            transcendentals=rows * NBR * TILE * HEADS,
            bytes_accessed=2 * (rows * feat * 2 + buffer_rows * feat * 2),
        ),
    )(tile_list.reshape(-1).astype(jnp.int32), scalars, queries, kv_all, kv_all)


MESH_IDS = pl.DeviceIdType.MESH


def exchange_kernel(tok_ref, rim_ref, cross_ref, send_sem, recv_sem, cross_send, cross_recv, own_sem):
    n_piece = lax.axis_size("piece")
    n_core = lax.axis_size("core")
    n_frames = lax.axis_size("fy") * n_core
    piece = lax.axis_index("piece")
    frame = lax.axis_index("fy") * n_core + lax.axis_index("core")
    fsdp = lax.axis_index("fsdp")
    here = (fsdp, piece, lax.axis_index("fy"), lax.axis_index("core"))
    up = (fsdp, piece - 1, here[2], here[3])
    down = (fsdp, piece + 1, here[2], here[3])
    has_up = piece > 0
    has_down = piece < n_piece - 1
    per = tok_ref.shape[0] // n_frames
    peers = [(frame + k) % n_frames for k in range(1, n_frames)]
    barrier = pltpu.get_barrier_semaphore()

    @pl.when(has_up)
    def _():
        pl.semaphore_signal(barrier, inc=1, device_id=up, device_id_type=MESH_IDS)

    @pl.when(has_down)
    def _():
        pl.semaphore_signal(barrier, inc=1, device_id=down, device_id_type=MESH_IDS)

    for d in peers:
        pl.semaphore_signal(
            barrier, inc=1, device_id=(fsdp, piece, d // n_core, d % n_core), device_id_type=MESH_IDS
        )
    rim_peers = (piece + n_piece - 1) // n_piece + (2 * n_piece - 2 - piece) // n_piece
    pl.semaphore_wait(barrier, rim_peers + n_frames - 1)

    to_down = pltpu.make_async_remote_copy(
        src_ref=tok_ref,
        dst_ref=rim_ref.at[0],
        send_sem=send_sem.at[0],
        recv_sem=recv_sem.at[0],
        device_id=down,
        device_id_type=MESH_IDS,
    )
    to_up = pltpu.make_async_remote_copy(
        src_ref=tok_ref,
        dst_ref=rim_ref.at[1],
        send_sem=send_sem.at[1],
        recv_sem=recv_sem.at[1],
        device_id=up,
        device_id_type=MESH_IDS,
    )

    @pl.when(has_down)
    def _():
        to_down.start()

    @pl.when(has_up)
    def _():
        to_up.start()

    crosses = []
    for k, d in enumerate(peers):
        copy = pltpu.make_async_remote_copy(
            src_ref=tok_ref.at[pl.ds(pl.multiple_of(d * per, 16), per)],
            dst_ref=cross_ref.at[pl.ds(pl.multiple_of(frame * per, 16), per)],
            send_sem=cross_send.at[k],
            recv_sem=cross_recv.at[k],
            device_id=(fsdp, piece, d // n_core, d % n_core),
            device_id_type=MESH_IDS,
        )
        copy.start()
        crosses.append(copy)
    own_rows = pl.ds(pl.multiple_of(frame * per, 16), per)
    own_copy = pltpu.make_async_copy(tok_ref.at[own_rows], cross_ref.at[own_rows], own_sem)
    own_copy.start()

    @pl.when(has_down)
    def _():
        to_down.wait_send()
        to_up.wait_recv()

    @pl.when(has_up)
    def _():
        to_up.wait_send()
        to_down.wait_recv()

    for copy in crosses:
        copy.wait()
    own_copy.wait()


def exchange_tokens(own):
    rows, feat = own.shape
    return pl.pallas_call(
        exchange_kernel,
        out_shape=(
            jax.ShapeDtypeStruct((2, rows, feat), own.dtype),
            jax.ShapeDtypeStruct((rows, feat), own.dtype),
        ),
        in_specs=[pl.BlockSpec(memory_space=pl.ANY)],
        out_specs=(pl.BlockSpec(memory_space=pl.ANY), pl.BlockSpec(memory_space=pl.ANY)),
        scratch_shapes=[
            pltpu.SemaphoreType.DMA((2,)),
            pltpu.SemaphoreType.DMA((2,)),
            pltpu.SemaphoreType.DMA((8,)),
            pltpu.SemaphoreType.DMA((8,)),
            pltpu.SemaphoreType.DMA(()),
        ],
        compiler_params=pltpu.CompilerParams(collective_id=0, has_side_effects=True),
        cost_estimate=pl.CostEstimate(flops=0, transcendentals=0, bytes_accessed=80 * rows * feat * 2),
    )(own)


def temporal_block(query_part, key_part, spatial_part, clip_counts, first_pos):
    n_frames, per_dev = query_part.shape[0], query_part.shape[1]
    scaling = 1.0 / math.sqrt(HD)
    position = first_pos + jnp.arange(per_dev, dtype=jnp.int32)
    live_mask = (position[:, None] < clip_counts[None, :])[:, None, None, :]
    scores = (
        jnp.einsum(
            "fphd,gphd->phfg", query_part, key_part, preferred_element_type=jnp.float32
        )
        * scaling
    )
    scores = jnp.where(live_mask, scores, -1e30)
    row_max = jnp.max(scores, axis=-1, keepdims=True)
    exp_terms = jnp.where(live_mask, jnp.exp(scores - row_max), 0.0)
    denominator = jnp.sum(exp_terms, axis=-1, keepdims=True)
    weights = exp_terms.astype(jnp.bfloat16)
    summed = jnp.einsum(
        "phfg,gphd->fphd", weights, spatial_part, preferred_element_type=jnp.float32
    )
    result = summed / jnp.transpose(denominator, (2, 0, 1, 3))
    return result.astype(jnp.bfloat16)


def local(tokens, mod_scale, mod_shift, w_qkv, w_out, neighbors, counts):
    tok_count = tokens.shape[1]
    feat_count = tokens.shape[2]
    n_frames = lax.axis_size("fy") * lax.axis_size("core")
    own = tokens[0]
    rims, crossed = exchange_tokens(own)
    piece_index = lax.axis_index("piece")
    above = jnp.where(piece_index > 0, rims[0], jnp.zeros_like(own))
    below = jnp.where(piece_index < lax.axis_size("piece") - 1, rims[1], jnp.zeros_like(own))
    core = lax.axis_index("core")
    half_rows = w_qkv.shape[0] // 2
    w_half = lax.dynamic_slice_in_dim(w_qkv, core * half_rows, half_rows, axis=0)
    w_pieces = lax.all_gather(w_half, ("fsdp", "core"), axis=0, tiled=False)
    w_full = w_pieces.reshape(lax.axis_size("fsdp"), w_qkv.shape[0], w_qkv.shape[1])
    out_rows = w_out.shape[0] // 2
    w_out_half = lax.dynamic_slice_in_dim(w_out, core * out_rows, out_rows, axis=0)
    w_out_half = lax.all_gather(w_out_half, "core", axis=0, tiled=True)
    w_out_full = lax.all_gather(w_out_half, "fsdp", axis=0, tiled=True)
    normed_all = layer_norm(
        jnp.concatenate([above, own, below], axis=0), mod_scale[0], mod_shift[0]
    )
    shard_cols = w_full.shape[2]
    w_query = jnp.concatenate(
        [w_full[0], w_full[1, :, : feat_count - shard_cols]], axis=1
    )
    normed_cross = layer_norm(crossed, mod_scale[0], mod_shift[0])
    w_key = jnp.concatenate(
        [w_full[1, :, feat_count - shard_cols :], w_full[2, :, : 2 * shard_cols - feat_count]], axis=1
    )
    q_both = jnp.dot(
        jnp.concatenate([normed_all[tok_count : 2 * tok_count], normed_cross], axis=0),
        w_query,
        preferred_element_type=jnp.float32,
    ).astype(jnp.bfloat16)
    queries = q_both[:tok_count]
    key_cross = jnp.dot(normed_cross, w_key, preferred_element_type=jnp.float32).astype(jnp.bfloat16)
    kv_all = jnp.einsum(
        "tk,jkc->jtc", normed_all, w_full[1:], preferred_element_type=jnp.float32
    ).astype(jnp.bfloat16)
    frame_index = lax.axis_index("fy") * lax.axis_size("core") + lax.axis_index("core")
    piece_index = lax.axis_index("piece")
    clip_counts = counts[0]
    count_here = lax.dynamic_index_in_dim(clip_counts, frame_index, 0, keepdims=False)
    rows_here = tok_count // (TGW * TILE)
    first_tile = (piece_index * rows_here - 1) * TGW
    spatial = spatial_rows(queries, kv_all, neighbors[0], first_tile, count_here)
    frame_axes = ("fy", "core")
    spatial_part = lax.all_to_all(spatial, frame_axes, split_axis=0, concat_axis=0, tiled=True)
    per_dev = tok_count // n_frames
    first_pos = piece_index * tok_count + frame_index * per_dev
    part_shape = (n_frames, per_dev, HEADS, HD)
    temporal = temporal_block(
        q_both[tok_count:].reshape(part_shape),
        key_cross.reshape(part_shape),
        spatial_part.reshape(part_shape),
        clip_counts,
        first_pos,
    )
    flat_temporal = lax.all_to_all(
        temporal.reshape(tok_count, feat_count), frame_axes, split_axis=0, concat_axis=0, tiled=True
    )
    projected = jnp.dot(flat_temporal, w_out_full, preferred_element_type=jnp.float32)
    return projected.astype(jnp.bfloat16).reshape(1, tok_count, feat_count)


def solution(mesh):
    n_fsdp = mesh.shape["fsdp"]
    n_sp = mesh.shape["sp"]
    split = Mesh(
        mesh.devices.reshape(n_fsdp, PIECES, n_sp // PIECES // 2, 2),
        ("fsdp", "piece", "fy", "core"),
    )
    seq = ("piece", "fy", "core")
    placed = (
        P("fsdp", seq, None),
        P("fsdp", None),
        P("fsdp", None),
        P(None, "fsdp"),
        P("fsdp", None),
        P("fsdp", seq, None),
        P("fsdp", None),
    )
    return jax.shard_map(
        local, mesh=split, in_specs=placed, out_specs=P("fsdp", seq, None), check_vma=False
    )
```

```python
import math

import jax
import jax.numpy as jnp
from jax import lax
from jax.experimental import pallas as pl
from jax.experimental.pallas import tpu as pltpu
from jax.sharding import Mesh
from jax.sharding import PartitionSpec as P

HEADS = 12
HD = 128
TILE = 128
TGW = 5
NBR = 6
PIECES = 4


def passed_along(block, axis, distance):
    devices = range(lax.axis_size(axis))
    route = [(i - distance, i) for i in devices if i - distance in devices]
    return lax.ppermute(block, axis, route)


def layer_norm(tokens, mod_scale, mod_shift):
    values_f32 = tokens.astype(jnp.float32)
    center = jnp.mean(values_f32, axis=-1, keepdims=True)
    spread = jnp.mean((values_f32 - center) ** 2, axis=-1, keepdims=True)
    normal = (values_f32 - center) / jnp.sqrt(spread + 1e-06)
    return (normal * (1.0 + mod_scale) + mod_shift).astype(jnp.bfloat16)


def spatial_kernel(list_ref, scalar_ref, q_ref, k_ref, v_ref, o_ref):
    scaling = 1.0 / math.sqrt(HD)
    first_tile = scalar_ref[0]
    count_here = scalar_ref[1]
    local_tiles = q_ref.shape[0] // TILE
    for t, c in [(t, c) for c in range(q_ref.shape[1] // HD) for t in range(local_tiles)]:
        cols = slice(c * HD, (c + 1) * HD)
        query = q_ref[t * TILE : (t + 1) * TILE, cols]
        parts = []
        block_max = None
        for n in range(NBR):
            tile_id = list_ref[t * NBR + n]
            start = pl.multiple_of((tile_id - first_tile) * TILE, TILE)
            key = k_ref[pl.ds(start, TILE), cols]
            scores = (
                lax.dot_general(
                    query, key, (((1,), (1,)), ((), ())), preferred_element_type=jnp.float32
                )
                * scaling
            )
            key_pos = tile_id * TILE + lax.broadcasted_iota(jnp.int32, (1, TILE), 1)
            scores = scores + jnp.where(key_pos < count_here, 0.0, -1e30)
            block_max = scores if block_max is None else jnp.maximum(block_max, scores)
            parts.append((scores, start))
        row_max = jnp.max(block_max, axis=-1, keepdims=True)
        exp_total = None
        summed = None
        for scores, start in parts:
            exp_terms = jnp.exp(scores - row_max)
            value = v_ref[pl.ds(start, TILE), cols]
            part_out = jnp.dot(
                exp_terms.astype(jnp.bfloat16), value, preferred_element_type=jnp.float32
            )
            exp_total = exp_terms if exp_total is None else exp_total + exp_terms
            summed = part_out if summed is None else summed + part_out
        denominator = jnp.sum(exp_total, axis=-1, keepdims=True)
        o_ref[t * TILE : (t + 1) * TILE, cols] = (summed / denominator).astype(o_ref.dtype)


def spatial_rows(queries, kv_all, tile_list, first_tile, count_here):
    buffer_rows = kv_all.shape[1]
    rows, feat = queries.shape
    scalars = jnp.stack([first_tile, count_here]).astype(jnp.int32)
    width = 3 * HD
    per_shard = kv_all.shape[2] // width
    k0 = feat // width
    grid_spec = pltpu.PrefetchScalarGridSpec(
        num_scalar_prefetch=2,
        grid=(feat // width,),
        in_specs=[
            pl.BlockSpec((rows, width), lambda g, lst, sc: (0, g)),
            pl.BlockSpec(
                (None, buffer_rows, width),
                lambda g, lst, sc: ((k0 + g) // per_shard - 1, 0, (k0 + g) % per_shard),
            ),
            pl.BlockSpec(
                (None, buffer_rows, width),
                lambda g, lst, sc: ((2 * k0 + g) // per_shard - 1, 0, (2 * k0 + g) % per_shard),
            ),
        ],
        out_specs=pl.BlockSpec((rows, width), lambda g, lst, sc: (0, g)),
    )
    flops = 4 * rows * NBR * TILE * feat
    return pl.pallas_call(
        spatial_kernel,
        grid_spec=grid_spec,
        out_shape=jax.ShapeDtypeStruct((rows, feat), jnp.bfloat16),
        cost_estimate=pl.CostEstimate(
            flops=flops,
            transcendentals=rows * NBR * TILE * HEADS,
            bytes_accessed=2 * (rows * feat * 2 + buffer_rows * feat * 2),
        ),
    )(tile_list.reshape(-1).astype(jnp.int32), scalars, queries, kv_all, kv_all)


MESH_IDS = pl.DeviceIdType.MESH


def exchange_kernel(tok_ref, rim_ref, cross_ref, send_sem, recv_sem, cross_send, cross_recv, own_sem):
    n_piece = lax.axis_size("piece")
    n_core = lax.axis_size("core")
    n_frames = lax.axis_size("fy") * n_core
    piece = lax.axis_index("piece")
    frame = lax.axis_index("fy") * n_core + lax.axis_index("core")
    fsdp = lax.axis_index("fsdp")
    here = (fsdp, piece, lax.axis_index("fy"), lax.axis_index("core"))
    up = (fsdp, piece - 1, here[2], here[3])
    down = (fsdp, piece + 1, here[2], here[3])
    has_up = piece > 0
    has_down = piece < n_piece - 1
    per = tok_ref.shape[0] // n_frames
    peers = [(frame + k) % n_frames for k in range(1, n_frames)]
    barrier = pltpu.get_barrier_semaphore()

    @pl.when(has_up)
    def _():
        pl.semaphore_signal(barrier, inc=1, device_id=up, device_id_type=MESH_IDS)

    @pl.when(has_down)
    def _():
        pl.semaphore_signal(barrier, inc=1, device_id=down, device_id_type=MESH_IDS)

    for d in peers:
        pl.semaphore_signal(
            barrier, inc=1, device_id=(fsdp, piece, d // n_core, d % n_core), device_id_type=MESH_IDS
        )
    rim_peers = (piece + n_piece - 1) // n_piece + (2 * n_piece - 2 - piece) // n_piece
    pl.semaphore_wait(barrier, rim_peers + n_frames - 1)

    to_down = pltpu.make_async_remote_copy(
        src_ref=tok_ref,
        dst_ref=rim_ref.at[0],
        send_sem=send_sem.at[0],
        recv_sem=recv_sem.at[0],
        device_id=down,
        device_id_type=MESH_IDS,
    )
    to_up = pltpu.make_async_remote_copy(
        src_ref=tok_ref,
        dst_ref=rim_ref.at[1],
        send_sem=send_sem.at[1],
        recv_sem=recv_sem.at[1],
        device_id=up,
        device_id_type=MESH_IDS,
    )

    @pl.when(has_down)
    def _():
        to_down.start()

    @pl.when(has_up)
    def _():
        to_up.start()

    crosses = []
    for k, d in enumerate(peers):
        copy = pltpu.make_async_remote_copy(
            src_ref=tok_ref.at[pl.ds(pl.multiple_of(d * per, 16), per)],
            dst_ref=cross_ref.at[pl.ds(pl.multiple_of(frame * per, 16), per)],
            send_sem=cross_send.at[k],
            recv_sem=cross_recv.at[k],
            device_id=(fsdp, piece, d // n_core, d % n_core),
            device_id_type=MESH_IDS,
        )
        copy.start()
        crosses.append(copy)
    own_rows = pl.ds(pl.multiple_of(frame * per, 16), per)
    own_copy = pltpu.make_async_copy(tok_ref.at[own_rows], cross_ref.at[own_rows], own_sem)
    own_copy.start()

    @pl.when(has_down)
    def _():
        to_down.wait_send()
        to_up.wait_recv()

    @pl.when(has_up)
    def _():
        to_up.wait_send()
        to_down.wait_recv()

    for copy in crosses:
        copy.wait()
    own_copy.wait()


def exchange_tokens(own):
    rows, feat = own.shape
    return pl.pallas_call(
        exchange_kernel,
        out_shape=(
            jax.ShapeDtypeStruct((2, rows, feat), own.dtype),
            jax.ShapeDtypeStruct((rows, feat), own.dtype),
        ),
        in_specs=[pl.BlockSpec(memory_space=pl.ANY)],
        out_specs=(pl.BlockSpec(memory_space=pl.ANY), pl.BlockSpec(memory_space=pl.ANY)),
        scratch_shapes=[
            pltpu.SemaphoreType.DMA((2,)),
            pltpu.SemaphoreType.DMA((2,)),
            pltpu.SemaphoreType.DMA((8,)),
            pltpu.SemaphoreType.DMA((8,)),
            pltpu.SemaphoreType.DMA(()),
        ],
        compiler_params=pltpu.CompilerParams(collective_id=0, has_side_effects=True),
        cost_estimate=pl.CostEstimate(flops=0, transcendentals=0, bytes_accessed=80 * rows * feat * 2),
    )(own)


def temporal_block(query_part, key_part, spatial_part, clip_counts, first_pos):
    n_frames, per_dev = query_part.shape[0], query_part.shape[1]
    scaling = 1.0 / math.sqrt(HD)
    position = first_pos + jnp.arange(per_dev, dtype=jnp.int32)
    live_mask = (position[:, None] < clip_counts[None, :])[:, None, None, :]
    scores = (
        jnp.einsum(
            "fphd,gphd->phfg", query_part, key_part, preferred_element_type=jnp.float32
        )
        * scaling
    )
    scores = jnp.where(live_mask, scores, -1e30)
    row_max = jnp.max(scores, axis=-1, keepdims=True)
    exp_terms = jnp.where(live_mask, jnp.exp(scores - row_max), 0.0)
    denominator = jnp.sum(exp_terms, axis=-1, keepdims=True)
    weights = exp_terms.astype(jnp.bfloat16)
    summed = jnp.einsum(
        "phfg,gphd->fphd", weights, spatial_part, preferred_element_type=jnp.float32
    )
    result = summed / jnp.transpose(denominator, (2, 0, 1, 3))
    return result.astype(jnp.bfloat16)


def local(tokens, mod_scale, mod_shift, w_qkv, w_out, neighbors, counts):
    tok_count = tokens.shape[1]
    feat_count = tokens.shape[2]
    n_frames = lax.axis_size("fy") * lax.axis_size("core")
    own = tokens[0]
    rims, crossed = exchange_tokens(own)
    piece_index = lax.axis_index("piece")
    above = jnp.where(piece_index > 0, rims[0], jnp.zeros_like(own))
    below = jnp.where(piece_index < lax.axis_size("piece") - 1, rims[1], jnp.zeros_like(own))
    core = lax.axis_index("core")
    half_rows = w_qkv.shape[0] // 2
    w_half = lax.dynamic_slice_in_dim(w_qkv, core * half_rows, half_rows, axis=0)
    w_pieces = lax.all_gather(w_half, ("fsdp", "core"), axis=0, tiled=False)
    w_full = w_pieces.reshape(lax.axis_size("fsdp"), w_qkv.shape[0], w_qkv.shape[1])
    w_out, w_full = lax.optimization_barrier((w_out, w_full))
    out_rows = w_out.shape[0] // 2
    w_out_half = lax.dynamic_slice_in_dim(w_out, core * out_rows, out_rows, axis=0)
    w_out_half = lax.all_gather(w_out_half, "core", axis=0, tiled=True)
    w_out_full = lax.all_gather(w_out_half, "fsdp", axis=0, tiled=True)
    normed_all = layer_norm(
        jnp.concatenate([above, own, below], axis=0), mod_scale[0], mod_shift[0]
    )
    shard_cols = w_full.shape[2]
    w_query = jnp.concatenate(
        [w_full[0], w_full[1, :, : feat_count - shard_cols]], axis=1
    )
    normed_cross = layer_norm(crossed, mod_scale[0], mod_shift[0])
    w_key = jnp.concatenate(
        [w_full[1, :, feat_count - shard_cols :], w_full[2, :, : 2 * shard_cols - feat_count]], axis=1
    )
    q_both = jnp.dot(
        jnp.concatenate([normed_all[tok_count : 2 * tok_count], normed_cross], axis=0),
        w_query,
        preferred_element_type=jnp.float32,
    ).astype(jnp.bfloat16)
    queries = q_both[:tok_count]
    key_cross = jnp.dot(normed_cross, w_key, preferred_element_type=jnp.float32).astype(jnp.bfloat16)
    kv_all = jnp.einsum(
        "tk,jkc->jtc", normed_all, w_full[1:], preferred_element_type=jnp.float32
    ).astype(jnp.bfloat16)
    frame_index = lax.axis_index("fy") * lax.axis_size("core") + lax.axis_index("core")
    piece_index = lax.axis_index("piece")
    clip_counts = counts[0]
    count_here = lax.dynamic_index_in_dim(clip_counts, frame_index, 0, keepdims=False)
    rows_here = tok_count // (TGW * TILE)
    first_tile = (piece_index * rows_here - 1) * TGW
    spatial = spatial_rows(queries, kv_all, neighbors[0], first_tile, count_here)
    frame_axes = ("fy", "core")
    spatial_part = lax.all_to_all(spatial, frame_axes, split_axis=0, concat_axis=0, tiled=True)
    per_dev = tok_count // n_frames
    first_pos = piece_index * tok_count + frame_index * per_dev
    part_shape = (n_frames, per_dev, HEADS, HD)
    temporal = temporal_block(
        q_both[tok_count:].reshape(part_shape),
        key_cross.reshape(part_shape),
        spatial_part.reshape(part_shape),
        clip_counts,
        first_pos,
    )
    flat_temporal = lax.all_to_all(
        temporal.reshape(tok_count, feat_count), frame_axes, split_axis=0, concat_axis=0, tiled=True
    )
    projected = jnp.dot(flat_temporal, w_out_full, preferred_element_type=jnp.float32)
    return projected.astype(jnp.bfloat16).reshape(1, tok_count, feat_count)


def solution(mesh):
    n_fsdp = mesh.shape["fsdp"]
    n_sp = mesh.shape["sp"]
    split = Mesh(
        mesh.devices.reshape(n_fsdp, PIECES, n_sp // PIECES // 2, 2),
        ("fsdp", "piece", "fy", "core"),
    )
    seq = ("piece", "fy", "core")
    placed = (
        P("fsdp", seq, None),
        P("fsdp", None),
        P("fsdp", None),
        P(None, "fsdp"),
        P("fsdp", None),
        P("fsdp", seq, None),
        P("fsdp", None),
    )
    return jax.shard_map(
        local, mesh=split, in_specs=placed, out_specs=P("fsdp", seq, None), check_vma=False
    )
```

```python
import math

import jax
import jax.numpy as jnp
from jax import lax
from jax.experimental import pallas as pl
from jax.experimental.pallas import tpu as pltpu
from jax.sharding import Mesh
from jax.sharding import PartitionSpec as P

HEADS = 12
HD = 128
TILE = 128
TGW = 5
NBR = 6
PIECES = 4


def passed_along(block, axis, distance):
    devices = range(lax.axis_size(axis))
    route = [(i - distance, i) for i in devices if i - distance in devices]
    return lax.ppermute(block, axis, route)


def layer_norm(tokens, mod_scale, mod_shift):
    values_f32 = tokens.astype(jnp.float32)
    center = jnp.mean(values_f32, axis=-1, keepdims=True)
    spread = jnp.mean((values_f32 - center) ** 2, axis=-1, keepdims=True)
    normal = (values_f32 - center) / jnp.sqrt(spread + 1e-06)
    return (normal * (1.0 + mod_scale) + mod_shift).astype(jnp.bfloat16)


def spatial_kernel(list_ref, scalar_ref, q_ref, k_ref, v_ref, o_ref):
    scaling = 1.0 / math.sqrt(HD)
    first_tile = scalar_ref[0]
    count_here = scalar_ref[1]
    local_tiles = q_ref.shape[0] // TILE
    for t, c in [(t, c) for c in range(q_ref.shape[1] // HD) for t in range(local_tiles)]:
        cols = slice(c * HD, (c + 1) * HD)
        query = q_ref[t * TILE : (t + 1) * TILE, cols]
        parts = []
        block_max = None
        for n in range(NBR):
            tile_id = list_ref[t * NBR + n]
            start = pl.multiple_of((tile_id - first_tile) * TILE, TILE)
            key = k_ref[pl.ds(start, TILE), cols]
            scores = (
                lax.dot_general(
                    query, key, (((1,), (1,)), ((), ())), preferred_element_type=jnp.float32
                )
                * scaling
            )
            key_pos = tile_id * TILE + lax.broadcasted_iota(jnp.int32, (1, TILE), 1)
            scores = scores + jnp.where(key_pos < count_here, 0.0, -1e30)
            block_max = scores if block_max is None else jnp.maximum(block_max, scores)
            parts.append((scores, start))
        row_max = jnp.max(block_max, axis=-1, keepdims=True)
        exp_total = None
        summed = None
        for scores, start in parts:
            exp_terms = jnp.exp(scores - row_max)
            value = v_ref[pl.ds(start, TILE), cols]
            part_out = jnp.dot(
                exp_terms.astype(jnp.bfloat16), value, preferred_element_type=jnp.float32
            )
            exp_total = exp_terms if exp_total is None else exp_total + exp_terms
            summed = part_out if summed is None else summed + part_out
        denominator = jnp.sum(exp_total, axis=-1, keepdims=True)
        o_ref[t * TILE : (t + 1) * TILE, cols] = (summed / denominator).astype(o_ref.dtype)


def spatial_rows(queries, kv_all, tile_list, first_tile, count_here):
    buffer_rows = kv_all.shape[1]
    rows, feat = queries.shape
    scalars = jnp.stack([first_tile, count_here]).astype(jnp.int32)
    width = 3 * HD
    per_shard = kv_all.shape[2] // width
    k0 = feat // width
    grid_spec = pltpu.PrefetchScalarGridSpec(
        num_scalar_prefetch=2,
        grid=(feat // width,),
        in_specs=[
            pl.BlockSpec((rows, width), lambda g, lst, sc: (0, g)),
            pl.BlockSpec(
                (None, buffer_rows, width),
                lambda g, lst, sc: ((k0 + g) // per_shard - 1, 0, (k0 + g) % per_shard),
            ),
            pl.BlockSpec(
                (None, buffer_rows, width),
                lambda g, lst, sc: ((2 * k0 + g) // per_shard - 1, 0, (2 * k0 + g) % per_shard),
            ),
        ],
        out_specs=pl.BlockSpec((rows, width), lambda g, lst, sc: (0, g)),
    )
    flops = 4 * rows * NBR * TILE * feat
    return pl.pallas_call(
        spatial_kernel,
        grid_spec=grid_spec,
        out_shape=jax.ShapeDtypeStruct((rows, feat), jnp.bfloat16),
        cost_estimate=pl.CostEstimate(
            flops=flops,
            transcendentals=rows * NBR * TILE * HEADS,
            bytes_accessed=2 * (rows * feat * 2 + buffer_rows * feat * 2),
        ),
    )(tile_list.reshape(-1).astype(jnp.int32), scalars, queries, kv_all, kv_all)


MESH_IDS = pl.DeviceIdType.MESH


def exchange_kernel(tok_ref, rim_ref, cross_ref, send_sem, recv_sem, cross_send, cross_recv, own_sem):
    n_piece = lax.axis_size("piece")
    n_core = lax.axis_size("core")
    n_frames = lax.axis_size("fy") * n_core
    piece = lax.axis_index("piece")
    frame = lax.axis_index("fy") * n_core + lax.axis_index("core")
    fsdp = lax.axis_index("fsdp")
    here = (fsdp, piece, lax.axis_index("fy"), lax.axis_index("core"))
    up = (fsdp, piece - 1, here[2], here[3])
    down = (fsdp, piece + 1, here[2], here[3])
    has_up = piece > 0
    has_down = piece < n_piece - 1
    per = tok_ref.shape[0] // n_frames
    peers = [(frame + k) % n_frames for k in range(1, n_frames)]
    barrier = pltpu.get_barrier_semaphore()

    @pl.when(has_up)
    def _():
        pl.semaphore_signal(barrier, inc=1, device_id=up, device_id_type=MESH_IDS)

    @pl.when(has_down)
    def _():
        pl.semaphore_signal(barrier, inc=1, device_id=down, device_id_type=MESH_IDS)

    for d in peers:
        pl.semaphore_signal(
            barrier, inc=1, device_id=(fsdp, piece, d // n_core, d % n_core), device_id_type=MESH_IDS
        )
    rim_peers = (piece + n_piece - 1) // n_piece + (2 * n_piece - 2 - piece) // n_piece
    pl.semaphore_wait(barrier, rim_peers + n_frames - 1)

    to_down = pltpu.make_async_remote_copy(
        src_ref=tok_ref,
        dst_ref=rim_ref.at[0],
        send_sem=send_sem.at[0],
        recv_sem=recv_sem.at[0],
        device_id=down,
        device_id_type=MESH_IDS,
    )
    to_up = pltpu.make_async_remote_copy(
        src_ref=tok_ref,
        dst_ref=rim_ref.at[1],
        send_sem=send_sem.at[1],
        recv_sem=recv_sem.at[1],
        device_id=up,
        device_id_type=MESH_IDS,
    )

    @pl.when(has_down)
    def _():
        to_down.start()

    @pl.when(has_up)
    def _():
        to_up.start()

    crosses = []
    for k, d in enumerate(peers):
        copy = pltpu.make_async_remote_copy(
            src_ref=tok_ref.at[pl.ds(pl.multiple_of(d * per, 16), per)],
            dst_ref=cross_ref.at[pl.ds(pl.multiple_of(frame * per, 16), per)],
            send_sem=cross_send.at[k],
            recv_sem=cross_recv.at[k],
            device_id=(fsdp, piece, d // n_core, d % n_core),
            device_id_type=MESH_IDS,
        )
        copy.start()
        crosses.append(copy)
    own_rows = pl.ds(pl.multiple_of(frame * per, 16), per)
    own_copy = pltpu.make_async_copy(tok_ref.at[own_rows], cross_ref.at[own_rows], own_sem)
    own_copy.start()

    @pl.when(has_down)
    def _():
        to_down.wait_send()
        to_up.wait_recv()

    @pl.when(has_up)
    def _():
        to_up.wait_send()
        to_down.wait_recv()

    for copy in crosses:
        copy.wait()
    own_copy.wait()


def exchange_tokens(own):
    rows, feat = own.shape
    return pl.pallas_call(
        exchange_kernel,
        out_shape=(
            jax.ShapeDtypeStruct((2, rows, feat), own.dtype),
            jax.ShapeDtypeStruct((rows, feat), own.dtype),
        ),
        in_specs=[pl.BlockSpec(memory_space=pl.ANY)],
        out_specs=(pl.BlockSpec(memory_space=pl.ANY), pl.BlockSpec(memory_space=pl.ANY)),
        scratch_shapes=[
            pltpu.SemaphoreType.DMA((2,)),
            pltpu.SemaphoreType.DMA((2,)),
            pltpu.SemaphoreType.DMA((8,)),
            pltpu.SemaphoreType.DMA((8,)),
            pltpu.SemaphoreType.DMA(()),
        ],
        compiler_params=pltpu.CompilerParams(collective_id=0, has_side_effects=True),
        cost_estimate=pl.CostEstimate(flops=0, transcendentals=0, bytes_accessed=80 * rows * feat * 2),
    )(own)


def temporal_block(query_part, key_part, spatial_part, clip_counts, first_pos):
    n_frames, per_dev = query_part.shape[0], query_part.shape[1]
    scaling = 1.0 / math.sqrt(HD)
    position = first_pos + jnp.arange(per_dev, dtype=jnp.int32)
    live_mask = (position[:, None] < clip_counts[None, :])[:, None, None, :]
    scores = (
        jnp.einsum(
            "fphd,gphd->phfg", query_part, key_part, preferred_element_type=jnp.float32
        )
        * scaling
    )
    scores = jnp.where(live_mask, scores, -1e30)
    row_max = jnp.max(scores, axis=-1, keepdims=True)
    exp_terms = jnp.where(live_mask, jnp.exp(scores - row_max), 0.0)
    denominator = jnp.sum(exp_terms, axis=-1, keepdims=True)
    weights = exp_terms.astype(jnp.bfloat16)
    summed = jnp.einsum(
        "phfg,gphd->fphd", weights, spatial_part, preferred_element_type=jnp.float32
    )
    result = summed / jnp.transpose(denominator, (2, 0, 1, 3))
    return result.astype(jnp.bfloat16)


def local(tokens, mod_scale, mod_shift, w_qkv, w_out, neighbors, counts):
    tok_count = tokens.shape[1]
    feat_count = tokens.shape[2]
    n_frames = lax.axis_size("fy") * lax.axis_size("core")
    own = tokens[0]
    rims, crossed = exchange_tokens(own)
    piece_index = lax.axis_index("piece")
    above = jnp.where(piece_index > 0, rims[0], jnp.zeros_like(own))
    below = jnp.where(piece_index < lax.axis_size("piece") - 1, rims[1], jnp.zeros_like(own))
    core = lax.axis_index("core")
    half_rows = w_qkv.shape[0] // 2
    w_half = lax.dynamic_slice_in_dim(w_qkv, core * half_rows, half_rows, axis=0)
    w_pieces = lax.all_gather(w_half, ("fsdp", "core"), axis=0, tiled=False)
    w_full = w_pieces.reshape(lax.axis_size("fsdp"), w_qkv.shape[0], w_qkv.shape[1])
    normed_all = layer_norm(
        jnp.concatenate([above, own, below], axis=0), mod_scale[0], mod_shift[0]
    )
    shard_cols = w_full.shape[2]
    w_query = jnp.concatenate(
        [w_full[0], w_full[1, :, : feat_count - shard_cols]], axis=1
    )
    normed_cross = layer_norm(crossed, mod_scale[0], mod_shift[0])
    w_key = jnp.concatenate(
        [w_full[1, :, feat_count - shard_cols :], w_full[2, :, : 2 * shard_cols - feat_count]], axis=1
    )
    q_both = jnp.dot(
        jnp.concatenate([normed_all[tok_count : 2 * tok_count], normed_cross], axis=0),
        w_query,
        preferred_element_type=jnp.float32,
    ).astype(jnp.bfloat16)
    queries = q_both[:tok_count]
    key_cross = jnp.dot(normed_cross, w_key, preferred_element_type=jnp.float32).astype(jnp.bfloat16)
    kv_all = jnp.einsum(
        "tk,jkc->jtc", normed_all, w_full[1:], preferred_element_type=jnp.float32
    ).astype(jnp.bfloat16)
    frame_index = lax.axis_index("fy") * lax.axis_size("core") + lax.axis_index("core")
    piece_index = lax.axis_index("piece")
    clip_counts = counts[0]
    count_here = lax.dynamic_index_in_dim(clip_counts, frame_index, 0, keepdims=False)
    rows_here = tok_count // (TGW * TILE)
    first_tile = (piece_index * rows_here - 1) * TGW
    spatial = spatial_rows(queries, kv_all, neighbors[0], first_tile, count_here)
    w_out, spatial = lax.optimization_barrier((w_out, spatial))
    out_rows = w_out.shape[0] // 2
    w_out_half = lax.dynamic_slice_in_dim(w_out, core * out_rows, out_rows, axis=0)
    w_out_half = lax.all_gather(w_out_half, "core", axis=0, tiled=True)
    w_out_full = lax.all_gather(w_out_half, "fsdp", axis=0, tiled=True)
    frame_axes = ("fy", "core")
    spatial_part = lax.all_to_all(spatial, frame_axes, split_axis=0, concat_axis=0, tiled=True)
    per_dev = tok_count // n_frames
    first_pos = piece_index * tok_count + frame_index * per_dev
    part_shape = (n_frames, per_dev, HEADS, HD)
    temporal = temporal_block(
        q_both[tok_count:].reshape(part_shape),
        key_cross.reshape(part_shape),
        spatial_part.reshape(part_shape),
        clip_counts,
        first_pos,
    )
    flat_temporal = lax.all_to_all(
        temporal.reshape(tok_count, feat_count), frame_axes, split_axis=0, concat_axis=0, tiled=True
    )
    projected = jnp.dot(flat_temporal, w_out_full, preferred_element_type=jnp.float32)
    return projected.astype(jnp.bfloat16).reshape(1, tok_count, feat_count)


def solution(mesh):
    n_fsdp = mesh.shape["fsdp"]
    n_sp = mesh.shape["sp"]
    split = Mesh(
        mesh.devices.reshape(n_fsdp, PIECES, n_sp // PIECES // 2, 2),
        ("fsdp", "piece", "fy", "core"),
    )
    seq = ("piece", "fy", "core")
    placed = (
        P("fsdp", seq, None),
        P("fsdp", None),
        P("fsdp", None),
        P(None, "fsdp"),
        P("fsdp", None),
        P("fsdp", seq, None),
        P("fsdp", None),
    )
    return jax.shard_map(
        local, mesh=split, in_specs=placed, out_specs=P("fsdp", seq, None), check_vma=False
    )
```

```python
import math

import jax
import jax.numpy as jnp
from jax import lax
from jax.experimental import pallas as pl
from jax.experimental.pallas import tpu as pltpu
from jax.sharding import Mesh
from jax.sharding import PartitionSpec as P

HEADS = 12
HD = 128
TILE = 128
TGW = 5
NBR = 6
PIECES = 4


def passed_along(block, axis, distance):
    devices = range(lax.axis_size(axis))
    route = [(i - distance, i) for i in devices if i - distance in devices]
    return lax.ppermute(block, axis, route)


def layer_norm(tokens, mod_scale, mod_shift):
    values_f32 = tokens.astype(jnp.float32)
    center = jnp.mean(values_f32, axis=-1, keepdims=True)
    spread = jnp.mean((values_f32 - center) ** 2, axis=-1, keepdims=True)
    normal = (values_f32 - center) / jnp.sqrt(spread + 1e-06)
    return (normal * (1.0 + mod_scale) + mod_shift).astype(jnp.bfloat16)


def spatial_kernel(list_ref, scalar_ref, q_ref, k_ref, v_ref, o_ref):
    scaling = 1.0 / math.sqrt(HD)
    first_tile = scalar_ref[0]
    count_here = scalar_ref[1]
    local_tiles = q_ref.shape[0] // TILE
    for t, c in [(t, c) for c in range(q_ref.shape[1] // HD) for t in range(local_tiles)]:
        cols = slice(c * HD, (c + 1) * HD)
        query = q_ref[t * TILE : (t + 1) * TILE, cols]
        parts = []
        block_max = None
        for n in range(NBR):
            tile_id = list_ref[t * NBR + n]
            start = pl.multiple_of((tile_id - first_tile) * TILE, TILE)
            key = k_ref[pl.ds(start, TILE), cols]
            scores = (
                lax.dot_general(
                    query, key, (((1,), (1,)), ((), ())), preferred_element_type=jnp.float32
                )
                * scaling
            )
            key_pos = tile_id * TILE + lax.broadcasted_iota(jnp.int32, (1, TILE), 1)
            scores = scores + jnp.where(key_pos < count_here, 0.0, -1e30)
            block_max = scores if block_max is None else jnp.maximum(block_max, scores)
            parts.append((scores, start))
        row_max = jnp.max(block_max, axis=-1, keepdims=True)
        exp_total = None
        summed = None
        for scores, start in parts:
            exp_terms = jnp.exp(scores - row_max)
            value = v_ref[pl.ds(start, TILE), cols]
            part_out = jnp.dot(
                exp_terms.astype(jnp.bfloat16), value, preferred_element_type=jnp.float32
            )
            exp_total = exp_terms if exp_total is None else exp_total + exp_terms
            summed = part_out if summed is None else summed + part_out
        denominator = jnp.sum(exp_total, axis=-1, keepdims=True)
        o_ref[t * TILE : (t + 1) * TILE, cols] = (summed / denominator).astype(o_ref.dtype)


def spatial_rows(queries, kv_all, tile_list, first_tile, count_here):
    buffer_rows = kv_all.shape[1]
    rows, feat = queries.shape
    scalars = jnp.stack([first_tile, count_here]).astype(jnp.int32)
    width = 3 * HD
    per_shard = kv_all.shape[2] // width
    k0 = feat // width
    grid_spec = pltpu.PrefetchScalarGridSpec(
        num_scalar_prefetch=2,
        grid=(feat // width,),
        in_specs=[
            pl.BlockSpec((rows, width), lambda g, lst, sc: (0, g)),
            pl.BlockSpec(
                (None, buffer_rows, width),
                lambda g, lst, sc: ((k0 + g) // per_shard - 1, 0, (k0 + g) % per_shard),
            ),
            pl.BlockSpec(
                (None, buffer_rows, width),
                lambda g, lst, sc: ((2 * k0 + g) // per_shard - 1, 0, (2 * k0 + g) % per_shard),
            ),
        ],
        out_specs=pl.BlockSpec((rows, width), lambda g, lst, sc: (0, g)),
    )
    flops = 4 * rows * NBR * TILE * feat
    return pl.pallas_call(
        spatial_kernel,
        grid_spec=grid_spec,
        out_shape=jax.ShapeDtypeStruct((rows, feat), jnp.bfloat16),
        cost_estimate=pl.CostEstimate(
            flops=flops,
            transcendentals=rows * NBR * TILE * HEADS,
            bytes_accessed=2 * (rows * feat * 2 + buffer_rows * feat * 2),
        ),
    )(tile_list.reshape(-1).astype(jnp.int32), scalars, queries, kv_all, kv_all)


MESH_IDS = pl.DeviceIdType.MESH


def exchange_kernel(tok_ref, rim_ref, cross_ref, send_sem, recv_sem, cross_send, cross_recv, own_sem):
    n_piece = lax.axis_size("piece")
    n_core = lax.axis_size("core")
    n_frames = lax.axis_size("fy") * n_core
    piece = lax.axis_index("piece")
    frame = lax.axis_index("fy") * n_core + lax.axis_index("core")
    fsdp = lax.axis_index("fsdp")
    here = (fsdp, piece, lax.axis_index("fy"), lax.axis_index("core"))
    up = (fsdp, piece - 1, here[2], here[3])
    down = (fsdp, piece + 1, here[2], here[3])
    has_up = piece > 0
    has_down = piece < n_piece - 1
    per = tok_ref.shape[0] // n_frames
    peers = [(frame + k) % n_frames for k in range(1, n_frames)]
    barrier = pltpu.get_barrier_semaphore()

    @pl.when(has_up)
    def _():
        pl.semaphore_signal(barrier, inc=1, device_id=up, device_id_type=MESH_IDS)

    @pl.when(has_down)
    def _():
        pl.semaphore_signal(barrier, inc=1, device_id=down, device_id_type=MESH_IDS)

    for d in peers:
        pl.semaphore_signal(
            barrier, inc=1, device_id=(fsdp, piece, d // n_core, d % n_core), device_id_type=MESH_IDS
        )
    rim_peers = (piece + n_piece - 1) // n_piece + (2 * n_piece - 2 - piece) // n_piece
    pl.semaphore_wait(barrier, rim_peers + n_frames - 1)

    to_down = pltpu.make_async_remote_copy(
        src_ref=tok_ref,
        dst_ref=rim_ref.at[0],
        send_sem=send_sem.at[0],
        recv_sem=recv_sem.at[0],
        device_id=down,
        device_id_type=MESH_IDS,
    )
    to_up = pltpu.make_async_remote_copy(
        src_ref=tok_ref,
        dst_ref=rim_ref.at[1],
        send_sem=send_sem.at[1],
        recv_sem=recv_sem.at[1],
        device_id=up,
        device_id_type=MESH_IDS,
    )

    @pl.when(has_down)
    def _():
        to_down.start()

    @pl.when(has_up)
    def _():
        to_up.start()

    crosses = []
    for k, d in enumerate(peers):
        copy = pltpu.make_async_remote_copy(
            src_ref=tok_ref.at[pl.ds(pl.multiple_of(d * per, 16), per)],
            dst_ref=cross_ref.at[pl.ds(pl.multiple_of(frame * per, 16), per)],
            send_sem=cross_send.at[k],
            recv_sem=cross_recv.at[k],
            device_id=(fsdp, piece, d // n_core, d % n_core),
            device_id_type=MESH_IDS,
        )
        copy.start()
        crosses.append(copy)
    own_rows = pl.ds(pl.multiple_of(frame * per, 16), per)
    own_copy = pltpu.make_async_copy(tok_ref.at[own_rows], cross_ref.at[own_rows], own_sem)
    own_copy.start()

    @pl.when(has_down)
    def _():
        to_down.wait_send()
        to_up.wait_recv()

    @pl.when(has_up)
    def _():
        to_up.wait_send()
        to_down.wait_recv()

    for copy in crosses:
        copy.wait()
    own_copy.wait()


def exchange_tokens(own):
    rows, feat = own.shape
    return pl.pallas_call(
        exchange_kernel,
        out_shape=(
            jax.ShapeDtypeStruct((2, rows, feat), own.dtype),
            jax.ShapeDtypeStruct((rows, feat), own.dtype),
        ),
        in_specs=[pl.BlockSpec(memory_space=pl.ANY)],
        out_specs=(pl.BlockSpec(memory_space=pl.ANY), pl.BlockSpec(memory_space=pl.ANY)),
        scratch_shapes=[
            pltpu.SemaphoreType.DMA((2,)),
            pltpu.SemaphoreType.DMA((2,)),
            pltpu.SemaphoreType.DMA((8,)),
            pltpu.SemaphoreType.DMA((8,)),
            pltpu.SemaphoreType.DMA(()),
        ],
        compiler_params=pltpu.CompilerParams(collective_id=0, has_side_effects=True),
        cost_estimate=pl.CostEstimate(flops=0, transcendentals=0, bytes_accessed=80 * rows * feat * 2),
    )(own)


def temporal_block(query_part, key_part, spatial_part, clip_counts, first_pos):
    n_frames, per_dev = query_part.shape[0], query_part.shape[1]
    scaling = 1.0 / math.sqrt(HD)
    position = first_pos + jnp.arange(per_dev, dtype=jnp.int32)
    live_mask = (position[:, None] < clip_counts[None, :])[:, None, None, :]
    scores = (
        jnp.einsum(
            "fphd,gphd->phfg", query_part, key_part, preferred_element_type=jnp.float32
        )
        * scaling
    )
    scores = jnp.where(live_mask, scores, -1e30)
    row_max = jnp.max(scores, axis=-1, keepdims=True)
    exp_terms = jnp.where(live_mask, jnp.exp(scores - row_max), 0.0)
    denominator = jnp.sum(exp_terms, axis=-1, keepdims=True)
    weights = exp_terms.astype(jnp.bfloat16)
    summed = jnp.einsum(
        "phfg,gphd->fphd", weights, spatial_part, preferred_element_type=jnp.float32
    )
    result = summed / jnp.transpose(denominator, (2, 0, 1, 3))
    return result.astype(jnp.bfloat16)


def local(tokens, mod_scale, mod_shift, w_qkv, w_out, neighbors, counts):
    tok_count = tokens.shape[1]
    feat_count = tokens.shape[2]
    n_frames = lax.axis_size("fy") * lax.axis_size("core")
    own = tokens[0]
    rims, crossed = exchange_tokens(own)
    piece_index = lax.axis_index("piece")
    above = jnp.where(piece_index > 0, rims[0], jnp.zeros_like(own))
    below = jnp.where(piece_index < lax.axis_size("piece") - 1, rims[1], jnp.zeros_like(own))
    core = lax.axis_index("core")
    half_rows = w_qkv.shape[0] // 2
    w_half = lax.dynamic_slice_in_dim(w_qkv, core * half_rows, half_rows, axis=0)
    w_pieces = lax.all_gather(w_half, ("fsdp", "core"), axis=0, tiled=False)
    w_full = w_pieces.reshape(lax.axis_size("fsdp"), w_qkv.shape[0], w_qkv.shape[1])
    w_out, w_full = lax.optimization_barrier((w_out, w_full))
    w_out_full = lax.all_gather(w_out, "fsdp", axis=0, tiled=True)
    normed_all = layer_norm(
        jnp.concatenate([above, own, below], axis=0), mod_scale[0], mod_shift[0]
    )
    shard_cols = w_full.shape[2]
    w_query = jnp.concatenate(
        [w_full[0], w_full[1, :, : feat_count - shard_cols]], axis=1
    )
    normed_cross = layer_norm(crossed, mod_scale[0], mod_shift[0])
    w_key = jnp.concatenate(
        [w_full[1, :, feat_count - shard_cols :], w_full[2, :, : 2 * shard_cols - feat_count]], axis=1
    )
    q_both = jnp.dot(
        jnp.concatenate([normed_all[tok_count : 2 * tok_count], normed_cross], axis=0),
        w_query,
        preferred_element_type=jnp.float32,
    ).astype(jnp.bfloat16)
    queries = q_both[:tok_count]
    key_cross = jnp.dot(normed_cross, w_key, preferred_element_type=jnp.float32).astype(jnp.bfloat16)
    kv_all = jnp.einsum(
        "tk,jkc->jtc", normed_all, w_full[1:], preferred_element_type=jnp.float32
    ).astype(jnp.bfloat16)
    frame_index = lax.axis_index("fy") * lax.axis_size("core") + lax.axis_index("core")
    piece_index = lax.axis_index("piece")
    clip_counts = counts[0]
    count_here = lax.dynamic_index_in_dim(clip_counts, frame_index, 0, keepdims=False)
    rows_here = tok_count // (TGW * TILE)
    first_tile = (piece_index * rows_here - 1) * TGW
    spatial = spatial_rows(queries, kv_all, neighbors[0], first_tile, count_here)
    frame_axes = ("fy", "core")
    spatial_part = lax.all_to_all(spatial, frame_axes, split_axis=0, concat_axis=0, tiled=True)
    per_dev = tok_count // n_frames
    first_pos = piece_index * tok_count + frame_index * per_dev
    part_shape = (n_frames, per_dev, HEADS, HD)
    temporal = temporal_block(
        q_both[tok_count:].reshape(part_shape),
        key_cross.reshape(part_shape),
        spatial_part.reshape(part_shape),
        clip_counts,
        first_pos,
    )
    flat_temporal = lax.all_to_all(
        temporal.reshape(tok_count, feat_count), frame_axes, split_axis=0, concat_axis=0, tiled=True
    )
    projected = jnp.dot(flat_temporal, w_out_full, preferred_element_type=jnp.float32)
    return projected.astype(jnp.bfloat16).reshape(1, tok_count, feat_count)


def solution(mesh):
    n_fsdp = mesh.shape["fsdp"]
    n_sp = mesh.shape["sp"]
    split = Mesh(
        mesh.devices.reshape(n_fsdp, PIECES, n_sp // PIECES // 2, 2),
        ("fsdp", "piece", "fy", "core"),
    )
    seq = ("piece", "fy", "core")
    placed = (
        P("fsdp", seq, None),
        P("fsdp", None),
        P("fsdp", None),
        P(None, "fsdp"),
        P("fsdp", None),
        P("fsdp", seq, None),
        P("fsdp", None),
    )
    return jax.shard_map(
        local, mesh=split, in_specs=placed, out_specs=P("fsdp", seq, None), check_vma=False
    )
```

```python
import math

import jax
import jax.numpy as jnp
from jax import lax
from jax.experimental import pallas as pl
from jax.experimental.pallas import tpu as pltpu
from jax.sharding import Mesh
from jax.sharding import PartitionSpec as P

HEADS = 12
HD = 128
TILE = 128
TGW = 5
NBR = 6
PIECES = 4


def passed_along(block, axis, distance):
    devices = range(lax.axis_size(axis))
    route = [(i - distance, i) for i in devices if i - distance in devices]
    return lax.ppermute(block, axis, route)


def layer_norm(tokens, mod_scale, mod_shift):
    values_f32 = tokens.astype(jnp.float32)
    center = jnp.mean(values_f32, axis=-1, keepdims=True)
    spread = jnp.mean((values_f32 - center) ** 2, axis=-1, keepdims=True)
    normal = (values_f32 - center) / jnp.sqrt(spread + 1e-06)
    return (normal * (1.0 + mod_scale) + mod_shift).astype(jnp.bfloat16)


def spatial_kernel(list_ref, scalar_ref, q_ref, k_ref, v_ref, o_ref):
    scaling = 1.0 / math.sqrt(HD)
    first_tile = scalar_ref[0]
    count_here = scalar_ref[1]
    local_tiles = q_ref.shape[0] // TILE
    for t, c in [(t, c) for c in range(q_ref.shape[1] // HD) for t in range(local_tiles)]:
        cols = slice(c * HD, (c + 1) * HD)
        query = q_ref[t * TILE : (t + 1) * TILE, cols]
        parts = []
        block_max = None
        for n in range(NBR):
            tile_id = list_ref[t * NBR + n]
            start = pl.multiple_of((tile_id - first_tile) * TILE, TILE)
            key = k_ref[pl.ds(start, TILE), cols]
            scores = (
                lax.dot_general(
                    query, key, (((1,), (1,)), ((), ())), preferred_element_type=jnp.float32
                )
                * scaling
            )
            key_pos = tile_id * TILE + lax.broadcasted_iota(jnp.int32, (1, TILE), 1)
            scores = scores + jnp.where(key_pos < count_here, 0.0, -1e30)
            block_max = scores if block_max is None else jnp.maximum(block_max, scores)
            parts.append((scores, start))
        row_max = jnp.max(block_max, axis=-1, keepdims=True)
        exp_total = None
        summed = None
        for scores, start in parts:
            exp_terms = jnp.exp(scores - row_max)
            value = v_ref[pl.ds(start, TILE), cols]
            part_out = jnp.dot(
                exp_terms.astype(jnp.bfloat16), value, preferred_element_type=jnp.float32
            )
            exp_total = exp_terms if exp_total is None else exp_total + exp_terms
            summed = part_out if summed is None else summed + part_out
        denominator = jnp.sum(exp_total, axis=-1, keepdims=True)
        o_ref[t * TILE : (t + 1) * TILE, cols] = (summed / denominator).astype(o_ref.dtype)


def spatial_rows(queries, kv_all, tile_list, first_tile, count_here):
    buffer_rows = kv_all.shape[1]
    rows, feat = queries.shape
    scalars = jnp.stack([first_tile, count_here]).astype(jnp.int32)
    width = 3 * HD
    per_shard = kv_all.shape[2] // width
    k0 = feat // width
    grid_spec = pltpu.PrefetchScalarGridSpec(
        num_scalar_prefetch=2,
        grid=(feat // width,),
        in_specs=[
            pl.BlockSpec((rows, width), lambda g, lst, sc: (0, g)),
            pl.BlockSpec(
                (None, buffer_rows, width),
                lambda g, lst, sc: ((k0 + g) // per_shard - 1, 0, (k0 + g) % per_shard),
            ),
            pl.BlockSpec(
                (None, buffer_rows, width),
                lambda g, lst, sc: ((2 * k0 + g) // per_shard - 1, 0, (2 * k0 + g) % per_shard),
            ),
        ],
        out_specs=pl.BlockSpec((rows, width), lambda g, lst, sc: (0, g)),
    )
    flops = 4 * rows * NBR * TILE * feat
    return pl.pallas_call(
        spatial_kernel,
        grid_spec=grid_spec,
        out_shape=jax.ShapeDtypeStruct((rows, feat), jnp.bfloat16),
        cost_estimate=pl.CostEstimate(
            flops=flops,
            transcendentals=rows * NBR * TILE * HEADS,
            bytes_accessed=2 * (rows * feat * 2 + buffer_rows * feat * 2),
        ),
    )(tile_list.reshape(-1).astype(jnp.int32), scalars, queries, kv_all, kv_all)


MESH_IDS = pl.DeviceIdType.MESH


def exchange_kernel(tok_ref, rim_ref, cross_ref, send_sem, recv_sem, cross_send, cross_recv, own_sem):
    n_piece = lax.axis_size("piece")
    n_core = lax.axis_size("core")
    n_frames = lax.axis_size("fy") * n_core
    piece = lax.axis_index("piece")
    frame = lax.axis_index("fy") * n_core + lax.axis_index("core")
    fsdp = lax.axis_index("fsdp")
    here = (fsdp, piece, lax.axis_index("fy"), lax.axis_index("core"))
    up = (fsdp, piece - 1, here[2], here[3])
    down = (fsdp, piece + 1, here[2], here[3])
    has_up = piece > 0
    has_down = piece < n_piece - 1
    per = tok_ref.shape[0] // n_frames
    peers = [(frame + k) % n_frames for k in range(1, n_frames)]
    barrier = pltpu.get_barrier_semaphore()

    @pl.when(has_up)
    def _():
        pl.semaphore_signal(barrier, inc=1, device_id=up, device_id_type=MESH_IDS)

    @pl.when(has_down)
    def _():
        pl.semaphore_signal(barrier, inc=1, device_id=down, device_id_type=MESH_IDS)

    for d in peers:
        pl.semaphore_signal(
            barrier, inc=1, device_id=(fsdp, piece, d // n_core, d % n_core), device_id_type=MESH_IDS
        )
    rim_peers = (piece + n_piece - 1) // n_piece + (2 * n_piece - 2 - piece) // n_piece
    pl.semaphore_wait(barrier, rim_peers + n_frames - 1)

    to_down = pltpu.make_async_remote_copy(
        src_ref=tok_ref,
        dst_ref=rim_ref.at[0],
        send_sem=send_sem.at[0],
        recv_sem=recv_sem.at[0],
        device_id=down,
        device_id_type=MESH_IDS,
    )
    to_up = pltpu.make_async_remote_copy(
        src_ref=tok_ref,
        dst_ref=rim_ref.at[1],
        send_sem=send_sem.at[1],
        recv_sem=recv_sem.at[1],
        device_id=up,
        device_id_type=MESH_IDS,
    )

    @pl.when(has_down)
    def _():
        to_down.start()

    @pl.when(has_up)
    def _():
        to_up.start()

    crosses = []
    for k, d in enumerate(peers):
        copy = pltpu.make_async_remote_copy(
            src_ref=tok_ref.at[pl.ds(pl.multiple_of(d * per, 16), per)],
            dst_ref=cross_ref.at[pl.ds(pl.multiple_of(frame * per, 16), per)],
            send_sem=cross_send.at[k],
            recv_sem=cross_recv.at[k],
            device_id=(fsdp, piece, d // n_core, d % n_core),
            device_id_type=MESH_IDS,
        )
        copy.start()
        crosses.append(copy)
    own_rows = pl.ds(pl.multiple_of(frame * per, 16), per)
    own_copy = pltpu.make_async_copy(tok_ref.at[own_rows], cross_ref.at[own_rows], own_sem)
    own_copy.start()

    @pl.when(has_down)
    def _():
        to_down.wait_send()
        to_up.wait_recv()

    @pl.when(has_up)
    def _():
        to_up.wait_send()
        to_down.wait_recv()

    for copy in crosses:
        copy.wait()
    own_copy.wait()


def exchange_tokens(own):
    rows, feat = own.shape
    return pl.pallas_call(
        exchange_kernel,
        out_shape=(
            jax.ShapeDtypeStruct((2, rows, feat), own.dtype),
            jax.ShapeDtypeStruct((rows, feat), own.dtype),
        ),
        in_specs=[pl.BlockSpec(memory_space=pl.ANY)],
        out_specs=(pl.BlockSpec(memory_space=pl.ANY), pl.BlockSpec(memory_space=pl.ANY)),
        scratch_shapes=[
            pltpu.SemaphoreType.DMA((2,)),
            pltpu.SemaphoreType.DMA((2,)),
            pltpu.SemaphoreType.DMA((8,)),
            pltpu.SemaphoreType.DMA((8,)),
            pltpu.SemaphoreType.DMA(()),
        ],
        compiler_params=pltpu.CompilerParams(collective_id=0, has_side_effects=True),
        cost_estimate=pl.CostEstimate(flops=0, transcendentals=0, bytes_accessed=80 * rows * feat * 2),
    )(own)


def temporal_block(query_part, key_part, spatial_part, clip_counts, first_pos):
    n_frames, per_dev = query_part.shape[0], query_part.shape[1]
    scaling = 1.0 / math.sqrt(HD)
    position = first_pos + jnp.arange(per_dev, dtype=jnp.int32)
    live_mask = (position[:, None] < clip_counts[None, :])[:, None, None, :]
    scores = (
        jnp.einsum(
            "fphd,gphd->phfg", query_part, key_part, preferred_element_type=jnp.float32
        )
        * scaling
    )
    scores = jnp.where(live_mask, scores, -1e30)
    row_max = jnp.max(scores, axis=-1, keepdims=True)
    exp_terms = jnp.where(live_mask, jnp.exp(scores - row_max), 0.0)
    denominator = jnp.sum(exp_terms, axis=-1, keepdims=True)
    weights = exp_terms.astype(jnp.bfloat16)
    summed = jnp.einsum(
        "phfg,gphd->fphd", weights, spatial_part, preferred_element_type=jnp.float32
    )
    result = summed / jnp.transpose(denominator, (2, 0, 1, 3))
    return result.astype(jnp.bfloat16)


def swap_kernel(x_ref, y_ref, cross_send, cross_recv, own_sem):
    n_core = lax.axis_size("core")
    n_frames = lax.axis_size("fy") * n_core
    piece = lax.axis_index("piece")
    frame = lax.axis_index("fy") * n_core + lax.axis_index("core")
    fsdp = lax.axis_index("fsdp")
    per = x_ref.shape[0] // n_frames
    peers = [(frame + k) % n_frames for k in range(1, n_frames)]
    barrier = pltpu.get_barrier_semaphore()
    for d in peers:
        pl.semaphore_signal(
            barrier, inc=1, device_id=(fsdp, piece, d // n_core, d % n_core), device_id_type=MESH_IDS
        )
    pl.semaphore_wait(barrier, n_frames - 1)
    crosses = []
    for k, d in enumerate(peers):
        copy = pltpu.make_async_remote_copy(
            src_ref=x_ref.at[pl.ds(pl.multiple_of(d * per, 16), per)],
            dst_ref=y_ref.at[pl.ds(pl.multiple_of(frame * per, 16), per)],
            send_sem=cross_send.at[k],
            recv_sem=cross_recv.at[k],
            device_id=(fsdp, piece, d // n_core, d % n_core),
            device_id_type=MESH_IDS,
        )
        copy.start()
        crosses.append(copy)
    own_rows = pl.ds(pl.multiple_of(frame * per, 16), per)
    own_copy = pltpu.make_async_copy(x_ref.at[own_rows], y_ref.at[own_rows], own_sem)
    own_copy.start()
    for copy in crosses:
        copy.wait()
    own_copy.wait()


def swap_frames(x):
    rows, feat = x.shape
    return pl.pallas_call(
        swap_kernel,
        out_shape=jax.ShapeDtypeStruct((rows, feat), x.dtype),
        in_specs=[pl.BlockSpec(memory_space=pl.ANY)],
        out_specs=pl.BlockSpec(memory_space=pl.ANY),
        scratch_shapes=[
            pltpu.SemaphoreType.DMA((8,)),
            pltpu.SemaphoreType.DMA((8,)),
            pltpu.SemaphoreType.DMA(()),
        ],
        compiler_params=pltpu.CompilerParams(collective_id=1, has_side_effects=True),
        cost_estimate=pl.CostEstimate(flops=0, transcendentals=0, bytes_accessed=2 * rows * feat * 2),
    )(x)


def local(tokens, mod_scale, mod_shift, w_qkv, w_out, neighbors, counts):
    tok_count = tokens.shape[1]
    feat_count = tokens.shape[2]
    n_frames = lax.axis_size("fy") * lax.axis_size("core")
    own = tokens[0]
    rims, crossed = exchange_tokens(own)
    piece_index = lax.axis_index("piece")
    above = jnp.where(piece_index > 0, rims[0], jnp.zeros_like(own))
    below = jnp.where(piece_index < lax.axis_size("piece") - 1, rims[1], jnp.zeros_like(own))
    core = lax.axis_index("core")
    half_rows = w_qkv.shape[0] // 2
    w_half = lax.dynamic_slice_in_dim(w_qkv, core * half_rows, half_rows, axis=0)
    w_pieces = lax.all_gather(w_half, ("fsdp", "core"), axis=0, tiled=False)
    w_full = w_pieces.reshape(lax.axis_size("fsdp"), w_qkv.shape[0], w_qkv.shape[1])
    w_out, w_full = lax.optimization_barrier((w_out, w_full))
    w_out_full = lax.all_gather(w_out, "fsdp", axis=0, tiled=True)
    normed_all = layer_norm(
        jnp.concatenate([above, own, below], axis=0), mod_scale[0], mod_shift[0]
    )
    shard_cols = w_full.shape[2]
    w_query = jnp.concatenate(
        [w_full[0], w_full[1, :, : feat_count - shard_cols]], axis=1
    )
    normed_cross = layer_norm(crossed, mod_scale[0], mod_shift[0])
    w_key = jnp.concatenate(
        [w_full[1, :, feat_count - shard_cols :], w_full[2, :, : 2 * shard_cols - feat_count]], axis=1
    )
    q_both = jnp.dot(
        jnp.concatenate([normed_all[tok_count : 2 * tok_count], normed_cross], axis=0),
        w_query,
        preferred_element_type=jnp.float32,
    ).astype(jnp.bfloat16)
    queries = q_both[:tok_count]
    key_cross = jnp.dot(normed_cross, w_key, preferred_element_type=jnp.float32).astype(jnp.bfloat16)
    kv_all = jnp.einsum(
        "tk,jkc->jtc", normed_all, w_full[1:], preferred_element_type=jnp.float32
    ).astype(jnp.bfloat16)
    frame_index = lax.axis_index("fy") * lax.axis_size("core") + lax.axis_index("core")
    piece_index = lax.axis_index("piece")
    clip_counts = counts[0]
    count_here = lax.dynamic_index_in_dim(clip_counts, frame_index, 0, keepdims=False)
    rows_here = tok_count // (TGW * TILE)
    first_tile = (piece_index * rows_here - 1) * TGW
    spatial = spatial_rows(queries, kv_all, neighbors[0], first_tile, count_here)
    frame_axes = ("fy", "core")
    spatial_part = lax.all_to_all(spatial, frame_axes, split_axis=0, concat_axis=0, tiled=True)
    per_dev = tok_count // n_frames
    first_pos = piece_index * tok_count + frame_index * per_dev
    part_shape = (n_frames, per_dev, HEADS, HD)
    temporal = temporal_block(
        q_both[tok_count:].reshape(part_shape),
        key_cross.reshape(part_shape),
        spatial_part.reshape(part_shape),
        clip_counts,
        first_pos,
    )
    flat_temporal = swap_frames(temporal.reshape(tok_count, feat_count))
    projected = jnp.dot(flat_temporal, w_out_full, preferred_element_type=jnp.float32)
    return projected.astype(jnp.bfloat16).reshape(1, tok_count, feat_count)


def solution(mesh):
    n_fsdp = mesh.shape["fsdp"]
    n_sp = mesh.shape["sp"]
    split = Mesh(
        mesh.devices.reshape(n_fsdp, PIECES, n_sp // PIECES // 2, 2),
        ("fsdp", "piece", "fy", "core"),
    )
    seq = ("piece", "fy", "core")
    placed = (
        P("fsdp", seq, None),
        P("fsdp", None),
        P("fsdp", None),
        P(None, "fsdp"),
        P("fsdp", None),
        P("fsdp", seq, None),
        P("fsdp", None),
    )
    return jax.shard_map(
        local, mesh=split, in_specs=placed, out_specs=P("fsdp", seq, None), check_vma=False
    )
```

```python
import math

import jax
import jax.numpy as jnp
from jax import lax
from jax.experimental import pallas as pl
from jax.experimental.pallas import tpu as pltpu
from jax.sharding import Mesh
from jax.sharding import PartitionSpec as P

HEADS = 12
HD = 128
TILE = 128
TGW = 5
NBR = 6
PIECES = 4


def passed_along(block, axis, distance):
    devices = range(lax.axis_size(axis))
    route = [(i - distance, i) for i in devices if i - distance in devices]
    return lax.ppermute(block, axis, route)


def layer_norm(tokens, mod_scale, mod_shift):
    values_f32 = tokens.astype(jnp.float32)
    center = jnp.mean(values_f32, axis=-1, keepdims=True)
    spread = jnp.mean((values_f32 - center) ** 2, axis=-1, keepdims=True)
    normal = (values_f32 - center) / jnp.sqrt(spread + 1e-06)
    return (normal * (1.0 + mod_scale) + mod_shift).astype(jnp.bfloat16)


def spatial_kernel(list_ref, scalar_ref, q_ref, k_ref, v_ref, o_ref):
    scaling = 1.0 / math.sqrt(HD)
    first_tile = scalar_ref[0]
    count_here = scalar_ref[1]
    local_tiles = q_ref.shape[0] // TILE
    for t, c in [(t, c) for c in range(q_ref.shape[1] // HD) for t in range(local_tiles)]:
        cols = slice(c * HD, (c + 1) * HD)
        query = q_ref[t * TILE : (t + 1) * TILE, cols]
        parts = []
        block_max = None
        for n in range(NBR):
            tile_id = list_ref[t * NBR + n]
            start = pl.multiple_of((tile_id - first_tile) * TILE, TILE)
            key = k_ref[pl.ds(start, TILE), cols]
            scores = (
                lax.dot_general(
                    query, key, (((1,), (1,)), ((), ())), preferred_element_type=jnp.float32
                )
                * scaling
            )
            key_pos = tile_id * TILE + lax.broadcasted_iota(jnp.int32, (1, TILE), 1)
            scores = scores + jnp.where(key_pos < count_here, 0.0, -1e30)
            block_max = scores if block_max is None else jnp.maximum(block_max, scores)
            parts.append((scores, start))
        row_max = jnp.max(block_max, axis=-1, keepdims=True)
        exp_total = None
        summed = None
        for scores, start in parts:
            exp_terms = jnp.exp(scores - row_max)
            value = v_ref[pl.ds(start, TILE), cols]
            part_out = jnp.dot(
                exp_terms.astype(jnp.bfloat16), value, preferred_element_type=jnp.float32
            )
            exp_total = exp_terms if exp_total is None else exp_total + exp_terms
            summed = part_out if summed is None else summed + part_out
        denominator = jnp.sum(exp_total, axis=-1, keepdims=True)
        o_ref[c, t * TILE : (t + 1) * TILE, :] = (summed / denominator).astype(o_ref.dtype)


def spatial_rows(queries, kv_all, tile_list, first_tile, count_here):
    buffer_rows = kv_all.shape[1]
    rows, feat = queries.shape
    scalars = jnp.stack([first_tile, count_here]).astype(jnp.int32)
    width = 3 * HD
    per_shard = kv_all.shape[2] // width
    k0 = feat // width
    grid_spec = pltpu.PrefetchScalarGridSpec(
        num_scalar_prefetch=2,
        grid=(feat // width,),
        in_specs=[
            pl.BlockSpec((rows, width), lambda g, lst, sc: (0, g)),
            pl.BlockSpec(
                (None, buffer_rows, width),
                lambda g, lst, sc: ((k0 + g) // per_shard - 1, 0, (k0 + g) % per_shard),
            ),
            pl.BlockSpec(
                (None, buffer_rows, width),
                lambda g, lst, sc: ((2 * k0 + g) // per_shard - 1, 0, (2 * k0 + g) % per_shard),
            ),
        ],
        out_specs=pl.BlockSpec((width // HD, rows, HD), lambda g, lst, sc: (g, 0, 0)),
    )
    flops = 4 * rows * NBR * TILE * feat
    return pl.pallas_call(
        spatial_kernel,
        grid_spec=grid_spec,
        out_shape=jax.ShapeDtypeStruct((feat // HD, rows, HD), jnp.bfloat16),
        cost_estimate=pl.CostEstimate(
            flops=flops,
            transcendentals=rows * NBR * TILE * HEADS,
            bytes_accessed=2 * (rows * feat * 2 + buffer_rows * feat * 2),
        ),
    )(tile_list.reshape(-1).astype(jnp.int32), scalars, queries, kv_all, kv_all)


MESH_IDS = pl.DeviceIdType.MESH


def exchange_kernel(tok_ref, rim_ref, cross_ref, send_sem, recv_sem, cross_send, cross_recv, own_sem):
    n_piece = lax.axis_size("piece")
    n_core = lax.axis_size("core")
    n_frames = lax.axis_size("fy") * n_core
    piece = lax.axis_index("piece")
    frame = lax.axis_index("fy") * n_core + lax.axis_index("core")
    fsdp = lax.axis_index("fsdp")
    here = (fsdp, piece, lax.axis_index("fy"), lax.axis_index("core"))
    up = (fsdp, piece - 1, here[2], here[3])
    down = (fsdp, piece + 1, here[2], here[3])
    has_up = piece > 0
    has_down = piece < n_piece - 1
    per = tok_ref.shape[0] // n_frames
    peers = [(frame + k) % n_frames for k in range(1, n_frames)]
    barrier = pltpu.get_barrier_semaphore()

    @pl.when(has_up)
    def _():
        pl.semaphore_signal(barrier, inc=1, device_id=up, device_id_type=MESH_IDS)

    @pl.when(has_down)
    def _():
        pl.semaphore_signal(barrier, inc=1, device_id=down, device_id_type=MESH_IDS)

    for d in peers:
        pl.semaphore_signal(
            barrier, inc=1, device_id=(fsdp, piece, d // n_core, d % n_core), device_id_type=MESH_IDS
        )
    rim_peers = (piece + n_piece - 1) // n_piece + (2 * n_piece - 2 - piece) // n_piece
    pl.semaphore_wait(barrier, rim_peers + n_frames - 1)

    to_down = pltpu.make_async_remote_copy(
        src_ref=tok_ref,
        dst_ref=rim_ref.at[0],
        send_sem=send_sem.at[0],
        recv_sem=recv_sem.at[0],
        device_id=down,
        device_id_type=MESH_IDS,
    )
    to_up = pltpu.make_async_remote_copy(
        src_ref=tok_ref,
        dst_ref=rim_ref.at[1],
        send_sem=send_sem.at[1],
        recv_sem=recv_sem.at[1],
        device_id=up,
        device_id_type=MESH_IDS,
    )

    @pl.when(has_down)
    def _():
        to_down.start()

    @pl.when(has_up)
    def _():
        to_up.start()

    crosses = []
    for k, d in enumerate(peers):
        copy = pltpu.make_async_remote_copy(
            src_ref=tok_ref.at[pl.ds(pl.multiple_of(d * per, 16), per)],
            dst_ref=cross_ref.at[pl.ds(pl.multiple_of(frame * per, 16), per)],
            send_sem=cross_send.at[k],
            recv_sem=cross_recv.at[k],
            device_id=(fsdp, piece, d // n_core, d % n_core),
            device_id_type=MESH_IDS,
        )
        copy.start()
        crosses.append(copy)
    own_rows = pl.ds(pl.multiple_of(frame * per, 16), per)
    own_copy = pltpu.make_async_copy(tok_ref.at[own_rows], cross_ref.at[own_rows], own_sem)
    own_copy.start()

    @pl.when(has_down)
    def _():
        to_down.wait_send()
        to_up.wait_recv()

    @pl.when(has_up)
    def _():
        to_up.wait_send()
        to_down.wait_recv()

    for copy in crosses:
        copy.wait()
    own_copy.wait()


def exchange_tokens(own):
    rows, feat = own.shape
    return pl.pallas_call(
        exchange_kernel,
        out_shape=(
            jax.ShapeDtypeStruct((2, rows, feat), own.dtype),
            jax.ShapeDtypeStruct((rows, feat), own.dtype),
        ),
        in_specs=[pl.BlockSpec(memory_space=pl.ANY)],
        out_specs=(pl.BlockSpec(memory_space=pl.ANY), pl.BlockSpec(memory_space=pl.ANY)),
        scratch_shapes=[
            pltpu.SemaphoreType.DMA((2,)),
            pltpu.SemaphoreType.DMA((2,)),
            pltpu.SemaphoreType.DMA((8,)),
            pltpu.SemaphoreType.DMA((8,)),
            pltpu.SemaphoreType.DMA(()),
        ],
        compiler_params=pltpu.CompilerParams(collective_id=0, has_side_effects=True),
        cost_estimate=pl.CostEstimate(flops=0, transcendentals=0, bytes_accessed=80 * rows * feat * 2),
    )(own)


def temporal_block(query_part, key_part, spatial_part, clip_counts, first_pos):
    per_dev = query_part.shape[2]
    scaling = 1.0 / math.sqrt(HD)
    position = first_pos + jnp.arange(per_dev, dtype=jnp.int32)
    live_mask = (position[:, None] < clip_counts[None, :])[None, :, None, :]
    scores = (
        jnp.einsum(
            "hfpd,hgpd->hpfg", query_part, key_part, preferred_element_type=jnp.float32
        )
        * scaling
    )
    scores = jnp.where(live_mask, scores, -1e30)
    row_max = jnp.max(scores, axis=-1, keepdims=True)
    exp_terms = jnp.where(live_mask, jnp.exp(scores - row_max), 0.0)
    denominator = jnp.sum(exp_terms, axis=-1, keepdims=True)
    weights = exp_terms.astype(jnp.bfloat16)
    summed = jnp.einsum(
        "hpfg,hgpd->hfpd", weights, spatial_part, preferred_element_type=jnp.float32
    )
    result = summed / jnp.transpose(denominator, (0, 2, 1, 3))
    return result.astype(jnp.bfloat16)


def swap_kernel(x_ref, y_ref, cross_send, cross_recv, own_sem):
    n_core = lax.axis_size("core")
    n_frames = lax.axis_size("fy") * n_core
    piece = lax.axis_index("piece")
    frame = lax.axis_index("fy") * n_core + lax.axis_index("core")
    fsdp = lax.axis_index("fsdp")
    per = x_ref.shape[1] // n_frames
    peers = [(frame + k) % n_frames for k in range(1, n_frames)]
    barrier = pltpu.get_barrier_semaphore()
    for d in peers:
        pl.semaphore_signal(
            barrier, inc=1, device_id=(fsdp, piece, d // n_core, d % n_core), device_id_type=MESH_IDS
        )
    pl.semaphore_wait(barrier, n_frames - 1)
    crosses = []
    for k, d in enumerate(peers):
        copy = pltpu.make_async_remote_copy(
            src_ref=x_ref.at[:, pl.ds(pl.multiple_of(d * per, 16), per)],
            dst_ref=y_ref.at[:, pl.ds(pl.multiple_of(frame * per, 16), per)],
            send_sem=cross_send.at[k],
            recv_sem=cross_recv.at[k],
            device_id=(fsdp, piece, d // n_core, d % n_core),
            device_id_type=MESH_IDS,
        )
        copy.start()
        crosses.append(copy)
    own_rows = pl.ds(pl.multiple_of(frame * per, 16), per)
    own_copy = pltpu.make_async_copy(x_ref.at[:, own_rows], y_ref.at[:, own_rows], own_sem)
    own_copy.start()
    for copy in crosses:
        copy.wait()
    own_copy.wait()


def swap_frames(x):
    heads, rows, width = x.shape
    feat = heads * width
    return pl.pallas_call(
        swap_kernel,
        out_shape=jax.ShapeDtypeStruct(x.shape, x.dtype),
        in_specs=[pl.BlockSpec(memory_space=pl.ANY)],
        out_specs=pl.BlockSpec(memory_space=pl.ANY),
        scratch_shapes=[
            pltpu.SemaphoreType.DMA((8,)),
            pltpu.SemaphoreType.DMA((8,)),
            pltpu.SemaphoreType.DMA(()),
        ],
        compiler_params=pltpu.CompilerParams(collective_id=1, has_side_effects=True),
        cost_estimate=pl.CostEstimate(flops=0, transcendentals=0, bytes_accessed=2 * rows * feat * 2),
    )(x)


def local(tokens, mod_scale, mod_shift, w_qkv, w_out, neighbors, counts):
    tok_count = tokens.shape[1]
    feat_count = tokens.shape[2]
    n_frames = lax.axis_size("fy") * lax.axis_size("core")
    own = tokens[0]
    rims, crossed = exchange_tokens(own)
    piece_index = lax.axis_index("piece")
    above = jnp.where(piece_index > 0, rims[0], jnp.zeros_like(own))
    below = jnp.where(piece_index < lax.axis_size("piece") - 1, rims[1], jnp.zeros_like(own))
    core = lax.axis_index("core")
    half_rows = w_qkv.shape[0] // 2
    w_half = lax.dynamic_slice_in_dim(w_qkv, core * half_rows, half_rows, axis=0)
    w_pieces = lax.all_gather(w_half, ("fsdp", "core"), axis=0, tiled=False)
    w_full = w_pieces.reshape(lax.axis_size("fsdp"), w_qkv.shape[0], w_qkv.shape[1])
    w_out, w_full = lax.optimization_barrier((w_out, w_full))
    w_out_full = lax.all_gather(w_out, "fsdp", axis=0, tiled=True)
    normed_all = layer_norm(
        jnp.concatenate([above, own, below], axis=0), mod_scale[0], mod_shift[0]
    )
    shard_cols = w_full.shape[2]
    w_query = jnp.concatenate(
        [w_full[0], w_full[1, :, : feat_count - shard_cols]], axis=1
    )
    normed_cross = layer_norm(crossed, mod_scale[0], mod_shift[0])
    w_key = jnp.concatenate(
        [w_full[1, :, feat_count - shard_cols :], w_full[2, :, : 2 * shard_cols - feat_count]], axis=1
    )
    queries = jnp.dot(
        normed_all[tok_count : 2 * tok_count], w_query, preferred_element_type=jnp.float32
    ).astype(jnp.bfloat16)
    head_w = (feat_count, HEADS, HD)
    query_cross = jnp.einsum(
        "tk,khd->htd", normed_cross, w_query.reshape(head_w), preferred_element_type=jnp.float32
    ).astype(jnp.bfloat16)
    key_cross = jnp.einsum(
        "tk,khd->htd", normed_cross, w_key.reshape(head_w), preferred_element_type=jnp.float32
    ).astype(jnp.bfloat16)
    kv_all = jnp.einsum(
        "tk,jkc->jtc", normed_all, w_full[1:], preferred_element_type=jnp.float32
    ).astype(jnp.bfloat16)
    frame_index = lax.axis_index("fy") * lax.axis_size("core") + lax.axis_index("core")
    piece_index = lax.axis_index("piece")
    clip_counts = counts[0]
    count_here = lax.dynamic_index_in_dim(clip_counts, frame_index, 0, keepdims=False)
    rows_here = tok_count // (TGW * TILE)
    first_tile = (piece_index * rows_here - 1) * TGW
    spatial = spatial_rows(queries, kv_all, neighbors[0], first_tile, count_here)
    frame_axes = ("fy", "core")
    spatial_part = lax.all_to_all(spatial, frame_axes, split_axis=1, concat_axis=1, tiled=True)
    per_dev = tok_count // n_frames
    first_pos = piece_index * tok_count + frame_index * per_dev
    part_shape = (HEADS, n_frames, per_dev, HD)
    temporal = temporal_block(
        query_cross.reshape(part_shape),
        key_cross.reshape(part_shape),
        spatial_part.reshape(part_shape),
        clip_counts,
        first_pos,
    )
    flat_temporal = swap_frames(temporal.reshape(HEADS, tok_count, HD))
    projected = jnp.einsum(
        "htd,hde->te",
        flat_temporal,
        w_out_full.reshape(HEADS, HD, feat_count),
        preferred_element_type=jnp.float32,
    )
    return projected.astype(jnp.bfloat16).reshape(1, tok_count, feat_count)


def solution(mesh):
    n_fsdp = mesh.shape["fsdp"]
    n_sp = mesh.shape["sp"]
    split = Mesh(
        mesh.devices.reshape(n_fsdp, PIECES, n_sp // PIECES // 2, 2),
        ("fsdp", "piece", "fy", "core"),
    )
    seq = ("piece", "fy", "core")
    placed = (
        P("fsdp", seq, None),
        P("fsdp", None),
        P("fsdp", None),
        P(None, "fsdp"),
        P("fsdp", None),
        P("fsdp", seq, None),
        P("fsdp", None),
    )
    return jax.shard_map(
        local, mesh=split, in_specs=placed, out_specs=P("fsdp", seq, None), check_vma=False
    )
```

```python
import math

import jax
import jax.numpy as jnp
from jax import lax
from jax.experimental import pallas as pl
from jax.experimental.pallas import tpu as pltpu
from jax.sharding import Mesh
from jax.sharding import PartitionSpec as P

HEADS = 12
HD = 128
TILE = 128
TGW = 5
NBR = 6
PIECES = 4


def passed_along(block, axis, distance):
    devices = range(lax.axis_size(axis))
    route = [(i - distance, i) for i in devices if i - distance in devices]
    return lax.ppermute(block, axis, route)


def layer_norm(tokens, mod_scale, mod_shift):
    values_f32 = tokens.astype(jnp.float32)
    center = jnp.mean(values_f32, axis=-1, keepdims=True)
    spread = jnp.mean((values_f32 - center) ** 2, axis=-1, keepdims=True)
    normal = (values_f32 - center) / jnp.sqrt(spread + 1e-06)
    return (normal * (1.0 + mod_scale) + mod_shift).astype(jnp.bfloat16)


def spatial_kernel(list_ref, scalar_ref, q_ref, k_ref, v_ref, o_ref):
    scaling = 1.0 / math.sqrt(HD)
    first_tile = scalar_ref[0]
    count_here = scalar_ref[1]
    local_tiles = q_ref.shape[0] // TILE
    for t, c in [(t, c) for c in range(q_ref.shape[1] // HD) for t in range(local_tiles)]:
        cols = slice(c * HD, (c + 1) * HD)
        query = q_ref[t * TILE : (t + 1) * TILE, cols]
        parts = []
        block_max = None
        for n in range(NBR):
            tile_id = list_ref[t * NBR + n]
            start = pl.multiple_of((tile_id - first_tile) * TILE, TILE)
            key = k_ref[pl.ds(start, TILE), cols]
            scores = (
                lax.dot_general(
                    query, key, (((1,), (1,)), ((), ())), preferred_element_type=jnp.float32
                )
                * scaling
            )
            key_pos = tile_id * TILE + lax.broadcasted_iota(jnp.int32, (1, TILE), 1)
            scores = scores + jnp.where(key_pos < count_here, 0.0, -1e30)
            block_max = scores if block_max is None else jnp.maximum(block_max, scores)
            parts.append((scores, start))
        row_max = jnp.max(block_max, axis=-1, keepdims=True)
        exp_total = None
        summed = None
        for scores, start in parts:
            exp_terms = jnp.exp(scores - row_max)
            value = v_ref[pl.ds(start, TILE), cols]
            part_out = jnp.dot(
                exp_terms.astype(jnp.bfloat16), value, preferred_element_type=jnp.float32
            )
            exp_total = exp_terms if exp_total is None else exp_total + exp_terms
            summed = part_out if summed is None else summed + part_out
        denominator = jnp.sum(exp_total, axis=-1, keepdims=True)
        o_ref[t * TILE : (t + 1) * TILE, cols] = (summed / denominator).astype(o_ref.dtype)


def spatial_rows(queries, kv_all, tile_list, first_tile, count_here):
    buffer_rows = kv_all.shape[1]
    rows, feat = queries.shape
    scalars = jnp.stack([first_tile, count_here]).astype(jnp.int32)
    width = 3 * HD
    per_shard = kv_all.shape[2] // width
    k0 = feat // width
    grid_spec = pltpu.PrefetchScalarGridSpec(
        num_scalar_prefetch=2,
        grid=(feat // width,),
        in_specs=[
            pl.BlockSpec((rows, width), lambda g, lst, sc: (0, g)),
            pl.BlockSpec(
                (None, buffer_rows, width),
                lambda g, lst, sc: ((k0 + g) // per_shard - 1, 0, (k0 + g) % per_shard),
            ),
            pl.BlockSpec(
                (None, buffer_rows, width),
                lambda g, lst, sc: ((2 * k0 + g) // per_shard - 1, 0, (2 * k0 + g) % per_shard),
            ),
        ],
        out_specs=pl.BlockSpec((rows, width), lambda g, lst, sc: (0, g)),
    )
    flops = 4 * rows * NBR * TILE * feat
    return pl.pallas_call(
        spatial_kernel,
        grid_spec=grid_spec,
        out_shape=jax.ShapeDtypeStruct((rows, feat), jnp.bfloat16),
        cost_estimate=pl.CostEstimate(
            flops=flops,
            transcendentals=rows * NBR * TILE * HEADS,
            bytes_accessed=2 * (rows * feat * 2 + buffer_rows * feat * 2),
        ),
    )(tile_list.reshape(-1).astype(jnp.int32), scalars, queries, kv_all, kv_all)


MESH_IDS = pl.DeviceIdType.MESH


def exchange_kernel(tok_ref, rim_ref, cross_ref, send_sem, recv_sem, cross_send, cross_recv, own_sem):
    n_piece = lax.axis_size("piece")
    n_core = lax.axis_size("core")
    n_frames = lax.axis_size("fy") * n_core
    piece = lax.axis_index("piece")
    frame = lax.axis_index("fy") * n_core + lax.axis_index("core")
    fsdp = lax.axis_index("fsdp")
    here = (fsdp, piece, lax.axis_index("fy"), lax.axis_index("core"))
    up = (fsdp, piece - 1, here[2], here[3])
    down = (fsdp, piece + 1, here[2], here[3])
    has_up = piece > 0
    has_down = piece < n_piece - 1
    per = tok_ref.shape[0] // n_frames
    peers = [(frame + k) % n_frames for k in range(1, n_frames)]
    barrier = pltpu.get_barrier_semaphore()

    @pl.when(has_up)
    def _():
        pl.semaphore_signal(barrier, inc=1, device_id=up, device_id_type=MESH_IDS)

    @pl.when(has_down)
    def _():
        pl.semaphore_signal(barrier, inc=1, device_id=down, device_id_type=MESH_IDS)

    for d in peers:
        pl.semaphore_signal(
            barrier, inc=1, device_id=(fsdp, piece, d // n_core, d % n_core), device_id_type=MESH_IDS
        )
    rim_peers = (piece + n_piece - 1) // n_piece + (2 * n_piece - 2 - piece) // n_piece
    pl.semaphore_wait(barrier, rim_peers + n_frames - 1)

    to_down = pltpu.make_async_remote_copy(
        src_ref=tok_ref,
        dst_ref=rim_ref.at[0],
        send_sem=send_sem.at[0],
        recv_sem=recv_sem.at[0],
        device_id=down,
        device_id_type=MESH_IDS,
    )
    to_up = pltpu.make_async_remote_copy(
        src_ref=tok_ref,
        dst_ref=rim_ref.at[1],
        send_sem=send_sem.at[1],
        recv_sem=recv_sem.at[1],
        device_id=up,
        device_id_type=MESH_IDS,
    )

    @pl.when(has_down)
    def _():
        to_down.start()

    @pl.when(has_up)
    def _():
        to_up.start()

    crosses = []
    for k, d in enumerate(peers):
        copy = pltpu.make_async_remote_copy(
            src_ref=tok_ref.at[pl.ds(pl.multiple_of(d * per, 16), per)],
            dst_ref=cross_ref.at[pl.ds(pl.multiple_of(frame * per, 16), per)],
            send_sem=cross_send.at[k],
            recv_sem=cross_recv.at[k],
            device_id=(fsdp, piece, d // n_core, d % n_core),
            device_id_type=MESH_IDS,
        )
        copy.start()
        crosses.append(copy)
    own_rows = pl.ds(pl.multiple_of(frame * per, 16), per)
    own_copy = pltpu.make_async_copy(tok_ref.at[own_rows], cross_ref.at[own_rows], own_sem)
    own_copy.start()

    @pl.when(has_down)
    def _():
        to_down.wait_send()
        to_up.wait_recv()

    @pl.when(has_up)
    def _():
        to_up.wait_send()
        to_down.wait_recv()

    for copy in crosses:
        copy.wait()
    own_copy.wait()


def exchange_tokens(own):
    rows, feat = own.shape
    return pl.pallas_call(
        exchange_kernel,
        out_shape=(
            jax.ShapeDtypeStruct((2, rows, feat), own.dtype),
            jax.ShapeDtypeStruct((rows, feat), own.dtype),
        ),
        in_specs=[pl.BlockSpec(memory_space=pl.ANY)],
        out_specs=(pl.BlockSpec(memory_space=pl.ANY), pl.BlockSpec(memory_space=pl.ANY)),
        scratch_shapes=[
            pltpu.SemaphoreType.DMA((2,)),
            pltpu.SemaphoreType.DMA((2,)),
            pltpu.SemaphoreType.DMA((8,)),
            pltpu.SemaphoreType.DMA((8,)),
            pltpu.SemaphoreType.DMA(()),
        ],
        compiler_params=pltpu.CompilerParams(collective_id=0, has_side_effects=True),
        cost_estimate=pl.CostEstimate(flops=0, transcendentals=0, bytes_accessed=80 * rows * feat * 2),
    )(own)


def temporal_block(query_part, key_part, spatial_part, clip_counts, first_pos):
    n_frames, per_dev = query_part.shape[0], query_part.shape[1]
    scaling = 1.0 / math.sqrt(HD)
    position = first_pos + jnp.arange(per_dev, dtype=jnp.int32)
    live_mask = (position[:, None] < clip_counts[None, :])[:, None, None, :]
    scores = (
        jnp.einsum(
            "fphd,gphd->phfg", query_part, key_part, preferred_element_type=jnp.float32
        )
        * scaling
    )
    scores = jnp.where(live_mask, scores, -1e30)
    row_max = jnp.max(scores, axis=-1, keepdims=True)
    exp_terms = jnp.where(live_mask, jnp.exp(scores - row_max), 0.0)
    denominator = jnp.sum(exp_terms, axis=-1, keepdims=True)
    weights = exp_terms.astype(jnp.bfloat16)
    summed = jnp.einsum(
        "phfg,gphd->fphd", weights, spatial_part, preferred_element_type=jnp.float32
    )
    result = summed / jnp.transpose(denominator, (2, 0, 1, 3))
    return result.astype(jnp.bfloat16)


def swap_kernel(x_ref, y_ref, cross_send, cross_recv, own_sem):
    n_core = lax.axis_size("core")
    n_frames = lax.axis_size("fy") * n_core
    piece = lax.axis_index("piece")
    frame = lax.axis_index("fy") * n_core + lax.axis_index("core")
    fsdp = lax.axis_index("fsdp")
    per = x_ref.shape[0] // n_frames
    peers = [(frame + k) % n_frames for k in range(1, n_frames)]
    barrier = pltpu.get_barrier_semaphore()
    for d in peers:
        pl.semaphore_signal(
            barrier, inc=1, device_id=(fsdp, piece, d // n_core, d % n_core), device_id_type=MESH_IDS
        )
    pl.semaphore_wait(barrier, n_frames - 1)
    crosses = []
    for k, d in enumerate(peers):
        copy = pltpu.make_async_remote_copy(
            src_ref=x_ref.at[pl.ds(pl.multiple_of(d * per, 16), per)],
            dst_ref=y_ref.at[pl.ds(pl.multiple_of(frame * per, 16), per)],
            send_sem=cross_send.at[k],
            recv_sem=cross_recv.at[k],
            device_id=(fsdp, piece, d // n_core, d % n_core),
            device_id_type=MESH_IDS,
        )
        copy.start()
        crosses.append(copy)
    own_rows = pl.ds(pl.multiple_of(frame * per, 16), per)
    own_copy = pltpu.make_async_copy(x_ref.at[own_rows], y_ref.at[own_rows], own_sem)
    own_copy.start()
    for copy in crosses:
        copy.wait()
    own_copy.wait()


def swap_frames(x):
    rows, feat = x.shape
    return pl.pallas_call(
        swap_kernel,
        out_shape=jax.ShapeDtypeStruct((rows, feat), x.dtype),
        in_specs=[pl.BlockSpec(memory_space=pl.ANY)],
        out_specs=pl.BlockSpec(memory_space=pl.ANY),
        scratch_shapes=[
            pltpu.SemaphoreType.DMA((8,)),
            pltpu.SemaphoreType.DMA((8,)),
            pltpu.SemaphoreType.DMA(()),
        ],
        compiler_params=pltpu.CompilerParams(collective_id=1, has_side_effects=True),
        cost_estimate=pl.CostEstimate(flops=0, transcendentals=0, bytes_accessed=2 * rows * feat * 2),
    )(x)


def local(tokens, mod_scale, mod_shift, w_qkv, w_out, neighbors, counts):
    tok_count = tokens.shape[1]
    feat_count = tokens.shape[2]
    n_frames = lax.axis_size("fy") * lax.axis_size("core")
    own = tokens[0]
    rims, crossed = exchange_tokens(own)
    piece_index = lax.axis_index("piece")
    above = jnp.where(piece_index > 0, rims[0], jnp.zeros_like(own))
    below = jnp.where(piece_index < lax.axis_size("piece") - 1, rims[1], jnp.zeros_like(own))
    core = lax.axis_index("core")
    n_share = lax.axis_size("fy") * lax.axis_size("core")
    share = lax.axis_index("fy") * lax.axis_size("core") + core
    share_rows = w_qkv.shape[0] // n_share
    w_half = lax.dynamic_slice_in_dim(w_qkv, share * share_rows, share_rows, axis=0)
    w_pieces = lax.all_gather(w_half, ("fsdp", "fy", "core"), axis=0, tiled=False)
    w_full = w_pieces.reshape(lax.axis_size("fsdp"), w_qkv.shape[0], w_qkv.shape[1])
    w_out, w_full = lax.optimization_barrier((w_out, w_full))
    w_out_full = lax.all_gather(w_out, "fsdp", axis=0, tiled=True)
    normed_all = layer_norm(
        jnp.concatenate([above, own, below], axis=0), mod_scale[0], mod_shift[0]
    )
    shard_cols = w_full.shape[2]
    w_query = jnp.concatenate(
        [w_full[0], w_full[1, :, : feat_count - shard_cols]], axis=1
    )
    normed_cross = layer_norm(crossed, mod_scale[0], mod_shift[0])
    w_key = jnp.concatenate(
        [w_full[1, :, feat_count - shard_cols :], w_full[2, :, : 2 * shard_cols - feat_count]], axis=1
    )
    q_both = jnp.dot(
        jnp.concatenate([normed_all[tok_count : 2 * tok_count], normed_cross], axis=0),
        w_query,
        preferred_element_type=jnp.float32,
    ).astype(jnp.bfloat16)
    queries = q_both[:tok_count]
    key_cross = jnp.dot(normed_cross, w_key, preferred_element_type=jnp.float32).astype(jnp.bfloat16)
    kv_all = jnp.einsum(
        "tk,jkc->jtc", normed_all, w_full[1:], preferred_element_type=jnp.float32
    ).astype(jnp.bfloat16)
    frame_index = lax.axis_index("fy") * lax.axis_size("core") + lax.axis_index("core")
    piece_index = lax.axis_index("piece")
    clip_counts = counts[0]
    count_here = lax.dynamic_index_in_dim(clip_counts, frame_index, 0, keepdims=False)
    rows_here = tok_count // (TGW * TILE)
    first_tile = (piece_index * rows_here - 1) * TGW
    spatial = spatial_rows(queries, kv_all, neighbors[0], first_tile, count_here)
    frame_axes = ("fy", "core")
    spatial_part = lax.all_to_all(spatial, frame_axes, split_axis=0, concat_axis=0, tiled=True)
    per_dev = tok_count // n_frames
    first_pos = piece_index * tok_count + frame_index * per_dev
    part_shape = (n_frames, per_dev, HEADS, HD)
    temporal = temporal_block(
        q_both[tok_count:].reshape(part_shape),
        key_cross.reshape(part_shape),
        spatial_part.reshape(part_shape),
        clip_counts,
        first_pos,
    )
    flat_temporal = swap_frames(temporal.reshape(tok_count, feat_count))
    projected = jnp.dot(flat_temporal, w_out_full, preferred_element_type=jnp.float32)
    return projected.astype(jnp.bfloat16).reshape(1, tok_count, feat_count)


def solution(mesh):
    n_fsdp = mesh.shape["fsdp"]
    n_sp = mesh.shape["sp"]
    split = Mesh(
        mesh.devices.reshape(n_fsdp, PIECES, n_sp // PIECES // 2, 2),
        ("fsdp", "piece", "fy", "core"),
    )
    seq = ("piece", "fy", "core")
    placed = (
        P("fsdp", seq, None),
        P("fsdp", None),
        P("fsdp", None),
        P(None, "fsdp"),
        P("fsdp", None),
        P("fsdp", seq, None),
        P("fsdp", None),
    )
    return jax.shard_map(
        local, mesh=split, in_specs=placed, out_specs=P("fsdp", seq, None), check_vma=False
    )
```

```python
import math

import jax
import jax.numpy as jnp
from jax import lax
from jax.experimental import pallas as pl
from jax.experimental.pallas import tpu as pltpu
from jax.sharding import Mesh
from jax.sharding import PartitionSpec as P

HEADS = 12
HD = 128
TILE = 128
TGW = 5
NBR = 6
PIECES = 4


def passed_along(block, axis, distance):
    devices = range(lax.axis_size(axis))
    route = [(i - distance, i) for i in devices if i - distance in devices]
    return lax.ppermute(block, axis, route)


def layer_norm(tokens, mod_scale, mod_shift):
    values_f32 = tokens.astype(jnp.float32)
    center = jnp.mean(values_f32, axis=-1, keepdims=True)
    spread = jnp.mean((values_f32 - center) ** 2, axis=-1, keepdims=True)
    normal = (values_f32 - center) / jnp.sqrt(spread + 1e-06)
    return (normal * (1.0 + mod_scale) + mod_shift).astype(jnp.bfloat16)


def spatial_kernel(list_ref, scalar_ref, q_ref, k_ref, v_ref, o_ref):
    scaling = 1.0 / math.sqrt(HD)
    first_tile = scalar_ref[0]
    count_here = scalar_ref[1]
    local_tiles = q_ref.shape[0] // TILE
    for t, c in [(t, c) for c in range(q_ref.shape[1] // HD) for t in range(local_tiles)]:
        cols = slice(c * HD, (c + 1) * HD)
        query = q_ref[t * TILE : (t + 1) * TILE, cols]
        parts = []
        block_max = None
        for n in range(NBR):
            tile_id = list_ref[t * NBR + n]
            start = pl.multiple_of((tile_id - first_tile) * TILE, TILE)
            key = k_ref[pl.ds(start, TILE), cols]
            scores = (
                lax.dot_general(
                    query, key, (((1,), (1,)), ((), ())), preferred_element_type=jnp.float32
                )
                * scaling
            )
            key_pos = tile_id * TILE + lax.broadcasted_iota(jnp.int32, (1, TILE), 1)
            scores = scores + jnp.where(key_pos < count_here, 0.0, -1e30)
            block_max = scores if block_max is None else jnp.maximum(block_max, scores)
            parts.append((scores, start))
        row_max = jnp.max(block_max, axis=-1, keepdims=True)
        exp_total = None
        summed = None
        for scores, start in parts:
            exp_terms = jnp.exp(scores - row_max)
            value = v_ref[pl.ds(start, TILE), cols]
            part_out = jnp.dot(
                exp_terms.astype(jnp.bfloat16), value, preferred_element_type=jnp.float32
            )
            exp_total = exp_terms if exp_total is None else exp_total + exp_terms
            summed = part_out if summed is None else summed + part_out
        denominator = jnp.sum(exp_total, axis=-1, keepdims=True)
        o_ref[t * TILE : (t + 1) * TILE, cols] = (summed / denominator).astype(o_ref.dtype)


def spatial_rows(queries, kv_all, tile_list, first_tile, count_here):
    buffer_rows = kv_all.shape[1]
    rows, feat = queries.shape
    scalars = jnp.stack([first_tile, count_here]).astype(jnp.int32)
    width = 3 * HD
    per_shard = kv_all.shape[2] // width
    k0 = feat // width
    grid_spec = pltpu.PrefetchScalarGridSpec(
        num_scalar_prefetch=2,
        grid=(feat // width,),
        in_specs=[
            pl.BlockSpec((rows, width), lambda g, lst, sc: (0, g)),
            pl.BlockSpec(
                (None, buffer_rows, width),
                lambda g, lst, sc: ((k0 + g) // per_shard - 1, 0, (k0 + g) % per_shard),
            ),
            pl.BlockSpec(
                (None, buffer_rows, width),
                lambda g, lst, sc: ((2 * k0 + g) // per_shard - 1, 0, (2 * k0 + g) % per_shard),
            ),
        ],
        out_specs=pl.BlockSpec((rows, width), lambda g, lst, sc: (0, g)),
    )
    flops = 4 * rows * NBR * TILE * feat
    return pl.pallas_call(
        spatial_kernel,
        grid_spec=grid_spec,
        out_shape=jax.ShapeDtypeStruct((rows, feat), jnp.bfloat16),
        cost_estimate=pl.CostEstimate(
            flops=flops,
            transcendentals=rows * NBR * TILE * HEADS,
            bytes_accessed=2 * (rows * feat * 2 + buffer_rows * feat * 2),
        ),
    )(tile_list.reshape(-1).astype(jnp.int32), scalars, queries, kv_all, kv_all)


MESH_IDS = pl.DeviceIdType.MESH


def exchange_kernel(tok_ref, rim_ref, cross_ref, send_sem, recv_sem, cross_send, cross_recv, own_sem):
    n_piece = lax.axis_size("piece")
    n_core = lax.axis_size("core")
    n_frames = lax.axis_size("fy") * n_core
    piece = lax.axis_index("piece")
    frame = lax.axis_index("fy") * n_core + lax.axis_index("core")
    fsdp = lax.axis_index("fsdp")
    here = (fsdp, piece, lax.axis_index("fy"), lax.axis_index("core"))
    up = (fsdp, piece - 1, here[2], here[3])
    down = (fsdp, piece + 1, here[2], here[3])
    has_up = piece > 0
    has_down = piece < n_piece - 1
    per = tok_ref.shape[0] // n_frames
    peers = [(frame + k) % n_frames for k in range(1, n_frames)]
    barrier = pltpu.get_barrier_semaphore()

    @pl.when(has_up)
    def _():
        pl.semaphore_signal(barrier, inc=1, device_id=up, device_id_type=MESH_IDS)

    @pl.when(has_down)
    def _():
        pl.semaphore_signal(barrier, inc=1, device_id=down, device_id_type=MESH_IDS)

    for d in peers:
        pl.semaphore_signal(
            barrier, inc=1, device_id=(fsdp, piece, d // n_core, d % n_core), device_id_type=MESH_IDS
        )
    rim_peers = (piece + n_piece - 1) // n_piece + (2 * n_piece - 2 - piece) // n_piece
    pl.semaphore_wait(barrier, rim_peers + n_frames - 1)

    to_down = pltpu.make_async_remote_copy(
        src_ref=tok_ref,
        dst_ref=rim_ref.at[0],
        send_sem=send_sem.at[0],
        recv_sem=recv_sem.at[0],
        device_id=down,
        device_id_type=MESH_IDS,
    )
    to_up = pltpu.make_async_remote_copy(
        src_ref=tok_ref,
        dst_ref=rim_ref.at[1],
        send_sem=send_sem.at[1],
        recv_sem=recv_sem.at[1],
        device_id=up,
        device_id_type=MESH_IDS,
    )

    @pl.when(has_down)
    def _():
        to_down.start()

    @pl.when(has_up)
    def _():
        to_up.start()

    crosses = []
    for k, d in enumerate(peers):
        copy = pltpu.make_async_remote_copy(
            src_ref=tok_ref.at[pl.ds(pl.multiple_of(d * per, 16), per)],
            dst_ref=cross_ref.at[pl.ds(pl.multiple_of(frame * per, 16), per)],
            send_sem=cross_send.at[k],
            recv_sem=cross_recv.at[k],
            device_id=(fsdp, piece, d // n_core, d % n_core),
            device_id_type=MESH_IDS,
        )
        copy.start()
        crosses.append(copy)
    own_rows = pl.ds(pl.multiple_of(frame * per, 16), per)
    own_copy = pltpu.make_async_copy(tok_ref.at[own_rows], cross_ref.at[own_rows], own_sem)
    own_copy.start()

    @pl.when(has_down)
    def _():
        to_down.wait_send()
        to_up.wait_recv()

    @pl.when(has_up)
    def _():
        to_up.wait_send()
        to_down.wait_recv()

    for copy in crosses:
        copy.wait()
    own_copy.wait()


def exchange_tokens(own):
    rows, feat = own.shape
    return pl.pallas_call(
        exchange_kernel,
        out_shape=(
            jax.ShapeDtypeStruct((2, rows, feat), own.dtype),
            jax.ShapeDtypeStruct((rows, feat), own.dtype),
        ),
        in_specs=[pl.BlockSpec(memory_space=pl.ANY)],
        out_specs=(pl.BlockSpec(memory_space=pl.ANY), pl.BlockSpec(memory_space=pl.ANY)),
        scratch_shapes=[
            pltpu.SemaphoreType.DMA((2,)),
            pltpu.SemaphoreType.DMA((2,)),
            pltpu.SemaphoreType.DMA((8,)),
            pltpu.SemaphoreType.DMA((8,)),
            pltpu.SemaphoreType.DMA(()),
        ],
        compiler_params=pltpu.CompilerParams(collective_id=0, has_side_effects=True),
        cost_estimate=pl.CostEstimate(flops=0, transcendentals=0, bytes_accessed=80 * rows * feat * 2),
    )(own)


def temporal_block(query_part, key_part, spatial_part, clip_counts, first_pos):
    n_frames, per_dev = query_part.shape[0], query_part.shape[1]
    scaling = 1.0 / math.sqrt(HD)
    position = first_pos + jnp.arange(per_dev, dtype=jnp.int32)
    live_mask = (position[:, None] < clip_counts[None, :])[:, None, None, :]
    scores = (
        jnp.einsum(
            "fphd,gphd->phfg", query_part, key_part, preferred_element_type=jnp.float32
        )
        * scaling
    )
    scores = jnp.where(live_mask, scores, -1e30)
    row_max = jnp.max(scores, axis=-1, keepdims=True)
    exp_terms = jnp.where(live_mask, jnp.exp(scores - row_max), 0.0)
    denominator = jnp.sum(exp_terms, axis=-1, keepdims=True)
    weights = exp_terms.astype(jnp.bfloat16)
    summed = jnp.einsum(
        "phfg,gphd->fphd", weights, spatial_part, preferred_element_type=jnp.float32
    )
    result = summed / jnp.transpose(denominator, (2, 0, 1, 3))
    return result.astype(jnp.bfloat16)


def swap_kernel(x_ref, y_ref, cross_send, cross_recv, own_sem):
    n_core = lax.axis_size("core")
    n_frames = lax.axis_size("fy") * n_core
    piece = lax.axis_index("piece")
    frame = lax.axis_index("fy") * n_core + lax.axis_index("core")
    fsdp = lax.axis_index("fsdp")
    per = x_ref.shape[0] // n_frames
    peers = [(frame + k) % n_frames for k in range(1, n_frames)]
    barrier = pltpu.get_barrier_semaphore()
    for d in peers:
        pl.semaphore_signal(
            barrier, inc=1, device_id=(fsdp, piece, d // n_core, d % n_core), device_id_type=MESH_IDS
        )
    pl.semaphore_wait(barrier, n_frames - 1)
    crosses = []
    for k, d in enumerate(peers):
        copy = pltpu.make_async_remote_copy(
            src_ref=x_ref.at[pl.ds(pl.multiple_of(d * per, 16), per)],
            dst_ref=y_ref.at[pl.ds(pl.multiple_of(frame * per, 16), per)],
            send_sem=cross_send.at[k],
            recv_sem=cross_recv.at[k],
            device_id=(fsdp, piece, d // n_core, d % n_core),
            device_id_type=MESH_IDS,
        )
        copy.start()
        crosses.append(copy)
    own_rows = pl.ds(pl.multiple_of(frame * per, 16), per)
    own_copy = pltpu.make_async_copy(x_ref.at[own_rows], y_ref.at[own_rows], own_sem)
    own_copy.start()
    for copy in crosses:
        copy.wait()
    own_copy.wait()


def swap_frames(x):
    rows, feat = x.shape
    return pl.pallas_call(
        swap_kernel,
        out_shape=jax.ShapeDtypeStruct((rows, feat), x.dtype),
        in_specs=[pl.BlockSpec(memory_space=pl.ANY)],
        out_specs=pl.BlockSpec(memory_space=pl.ANY),
        scratch_shapes=[
            pltpu.SemaphoreType.DMA((8,)),
            pltpu.SemaphoreType.DMA((8,)),
            pltpu.SemaphoreType.DMA(()),
        ],
        compiler_params=pltpu.CompilerParams(collective_id=1, has_side_effects=True),
        cost_estimate=pl.CostEstimate(flops=0, transcendentals=0, bytes_accessed=2 * rows * feat * 2),
    )(x)


def local(tokens, mod_scale, mod_shift, w_qkv, w_out, neighbors, counts):
    tok_count = tokens.shape[1]
    feat_count = tokens.shape[2]
    n_frames = lax.axis_size("fy") * lax.axis_size("core")
    own = tokens[0]
    rims, crossed = exchange_tokens(own)
    piece_index = lax.axis_index("piece")
    above = jnp.where(piece_index > 0, rims[0], jnp.zeros_like(own))
    below = jnp.where(piece_index < lax.axis_size("piece") - 1, rims[1], jnp.zeros_like(own))
    core = lax.axis_index("core")
    half_rows = w_qkv.shape[0] // 2
    w_half = lax.dynamic_slice_in_dim(w_qkv, core * half_rows, half_rows, axis=0)
    n_fsdp = lax.axis_size("fsdp")
    fsdp_index = lax.axis_index("fsdp")
    back = (fsdp_index - jnp.arange(n_fsdp, dtype=jnp.int32)) % n_fsdp

    def gather_fsdp(block):
        ring = [block] + [
            lax.ppermute(block, "fsdp", [(d, (d + k) % n_fsdp) for d in range(n_fsdp)])
            for k in range(1, n_fsdp)
        ]
        return jnp.take(jnp.stack(ring), back, axis=0)

    mine = gather_fsdp(w_half)
    other = lax.ppermute(mine, "core", [(0, 1), (1, 0)])
    w_full = jnp.where(
        core == 0,
        jnp.concatenate([mine, other], axis=1),
        jnp.concatenate([other, mine], axis=1),
    )
    w_out, w_full = lax.optimization_barrier((w_out, w_full))
    w_out_full = gather_fsdp(w_out).reshape(n_fsdp * w_out.shape[0], w_out.shape[1])
    normed_all = layer_norm(
        jnp.concatenate([above, own, below], axis=0), mod_scale[0], mod_shift[0]
    )
    shard_cols = w_full.shape[2]
    w_query = jnp.concatenate(
        [w_full[0], w_full[1, :, : feat_count - shard_cols]], axis=1
    )
    normed_cross = layer_norm(crossed, mod_scale[0], mod_shift[0])
    w_key = jnp.concatenate(
        [w_full[1, :, feat_count - shard_cols :], w_full[2, :, : 2 * shard_cols - feat_count]], axis=1
    )
    q_both = jnp.dot(
        jnp.concatenate([normed_all[tok_count : 2 * tok_count], normed_cross], axis=0),
        w_query,
        preferred_element_type=jnp.float32,
    ).astype(jnp.bfloat16)
    queries = q_both[:tok_count]
    key_cross = jnp.dot(normed_cross, w_key, preferred_element_type=jnp.float32).astype(jnp.bfloat16)
    kv_all = jnp.einsum(
        "tk,jkc->jtc", normed_all, w_full[1:], preferred_element_type=jnp.float32
    ).astype(jnp.bfloat16)
    frame_index = lax.axis_index("fy") * lax.axis_size("core") + lax.axis_index("core")
    piece_index = lax.axis_index("piece")
    clip_counts = counts[0]
    count_here = lax.dynamic_index_in_dim(clip_counts, frame_index, 0, keepdims=False)
    rows_here = tok_count // (TGW * TILE)
    first_tile = (piece_index * rows_here - 1) * TGW
    spatial = spatial_rows(queries, kv_all, neighbors[0], first_tile, count_here)
    frame_axes = ("fy", "core")
    spatial_part = lax.all_to_all(spatial, frame_axes, split_axis=0, concat_axis=0, tiled=True)
    per_dev = tok_count // n_frames
    first_pos = piece_index * tok_count + frame_index * per_dev
    part_shape = (n_frames, per_dev, HEADS, HD)
    temporal = temporal_block(
        q_both[tok_count:].reshape(part_shape),
        key_cross.reshape(part_shape),
        spatial_part.reshape(part_shape),
        clip_counts,
        first_pos,
    )
    flat_temporal = swap_frames(temporal.reshape(tok_count, feat_count))
    projected = jnp.dot(flat_temporal, w_out_full, preferred_element_type=jnp.float32)
    return projected.astype(jnp.bfloat16).reshape(1, tok_count, feat_count)


def solution(mesh):
    n_fsdp = mesh.shape["fsdp"]
    n_sp = mesh.shape["sp"]
    split = Mesh(
        mesh.devices.reshape(n_fsdp, PIECES, n_sp // PIECES // 2, 2),
        ("fsdp", "piece", "fy", "core"),
    )
    seq = ("piece", "fy", "core")
    placed = (
        P("fsdp", seq, None),
        P("fsdp", None),
        P("fsdp", None),
        P(None, "fsdp"),
        P("fsdp", None),
        P("fsdp", seq, None),
        P("fsdp", None),
    )
    return jax.shard_map(
        local, mesh=split, in_specs=placed, out_specs=P("fsdp", seq, None), check_vma=False
    )
```

```python
import math

import jax
import jax.numpy as jnp
from jax import lax
from jax.experimental import pallas as pl
from jax.experimental.pallas import tpu as pltpu
from jax.sharding import Mesh
from jax.sharding import PartitionSpec as P

HEADS = 12
HD = 128
TILE = 128
TGW = 5
NBR = 6
PIECES = 4


def passed_along(block, axis, distance):
    devices = range(lax.axis_size(axis))
    route = [(i - distance, i) for i in devices if i - distance in devices]
    return lax.ppermute(block, axis, route)


def layer_norm(tokens, mod_scale, mod_shift):
    values_f32 = tokens.astype(jnp.float32)
    center = jnp.mean(values_f32, axis=-1, keepdims=True)
    spread = jnp.mean((values_f32 - center) ** 2, axis=-1, keepdims=True)
    normal = (values_f32 - center) / jnp.sqrt(spread + 1e-06)
    return (normal * (1.0 + mod_scale) + mod_shift).astype(jnp.bfloat16)


def spatial_kernel(list_ref, scalar_ref, q_ref, k_ref, v_ref, o_ref):
    scaling = 1.0 / math.sqrt(HD)
    first_tile = scalar_ref[0]
    count_here = scalar_ref[1]
    local_tiles = q_ref.shape[0] // TILE
    for t, c in [(t, c) for c in range(q_ref.shape[1] // HD) for t in range(local_tiles)]:
        cols = slice(c * HD, (c + 1) * HD)
        query = q_ref[t * TILE : (t + 1) * TILE, cols]
        parts = []
        block_max = None
        for n in range(NBR):
            tile_id = list_ref[t * NBR + n]
            start = pl.multiple_of((tile_id - first_tile) * TILE, TILE)
            key = k_ref[pl.ds(start, TILE), cols]
            scores = (
                lax.dot_general(
                    query, key, (((1,), (1,)), ((), ())), preferred_element_type=jnp.float32
                )
                * scaling
            )
            key_pos = tile_id * TILE + lax.broadcasted_iota(jnp.int32, (1, TILE), 1)
            scores = scores + jnp.where(key_pos < count_here, 0.0, -1e30)
            block_max = scores if block_max is None else jnp.maximum(block_max, scores)
            parts.append((scores, start))
        row_max = jnp.max(block_max, axis=-1, keepdims=True)
        exp_total = None
        summed = None
        for scores, start in parts:
            exp_terms = jnp.exp(scores - row_max)
            value = v_ref[pl.ds(start, TILE), cols]
            part_out = jnp.dot(
                exp_terms.astype(jnp.bfloat16), value, preferred_element_type=jnp.float32
            )
            exp_total = exp_terms if exp_total is None else exp_total + exp_terms
            summed = part_out if summed is None else summed + part_out
        denominator = jnp.sum(exp_total, axis=-1, keepdims=True)
        o_ref[t * TILE : (t + 1) * TILE, cols] = (summed / denominator).astype(o_ref.dtype)


def spatial_rows(queries, kv_all, tile_list, first_tile, count_here):
    buffer_rows = kv_all.shape[1]
    rows, feat = queries.shape
    scalars = jnp.stack([first_tile, count_here]).astype(jnp.int32)
    width = 3 * HD
    per_shard = kv_all.shape[2] // width
    k0 = feat // width
    grid_spec = pltpu.PrefetchScalarGridSpec(
        num_scalar_prefetch=2,
        grid=(feat // width,),
        in_specs=[
            pl.BlockSpec((rows, width), lambda g, lst, sc: (0, g)),
            pl.BlockSpec(
                (None, buffer_rows, width),
                lambda g, lst, sc: ((k0 + g) // per_shard - 1, 0, (k0 + g) % per_shard),
            ),
            pl.BlockSpec(
                (None, buffer_rows, width),
                lambda g, lst, sc: ((2 * k0 + g) // per_shard - 1, 0, (2 * k0 + g) % per_shard),
            ),
        ],
        out_specs=pl.BlockSpec((rows, width), lambda g, lst, sc: (0, g)),
    )
    flops = 4 * rows * NBR * TILE * feat
    return pl.pallas_call(
        spatial_kernel,
        grid_spec=grid_spec,
        out_shape=jax.ShapeDtypeStruct((rows, feat), jnp.bfloat16),
        cost_estimate=pl.CostEstimate(
            flops=flops,
            transcendentals=rows * NBR * TILE * HEADS,
            bytes_accessed=2 * (rows * feat * 2 + buffer_rows * feat * 2),
        ),
    )(tile_list.reshape(-1).astype(jnp.int32), scalars, queries, kv_all, kv_all)


MESH_IDS = pl.DeviceIdType.MESH


def exchange_kernel(tok_ref, rim_ref, cross_ref, send_sem, recv_sem, cross_send, cross_recv, own_sem):
    n_piece = lax.axis_size("piece")
    n_core = lax.axis_size("core")
    n_frames = lax.axis_size("fy") * n_core
    piece = lax.axis_index("piece")
    frame = lax.axis_index("fy") * n_core + lax.axis_index("core")
    fsdp = lax.axis_index("fsdp")
    here = (fsdp, piece, lax.axis_index("fy"), lax.axis_index("core"))
    up = (fsdp, piece - 1, here[2], here[3])
    down = (fsdp, piece + 1, here[2], here[3])
    has_up = piece > 0
    has_down = piece < n_piece - 1
    per = tok_ref.shape[0] // n_frames
    peers = [(frame + k) % n_frames for k in range(1, n_frames)]
    barrier = pltpu.get_barrier_semaphore()

    @pl.when(has_up)
    def _():
        pl.semaphore_signal(barrier, inc=1, device_id=up, device_id_type=MESH_IDS)

    @pl.when(has_down)
    def _():
        pl.semaphore_signal(barrier, inc=1, device_id=down, device_id_type=MESH_IDS)

    for d in peers:
        pl.semaphore_signal(
            barrier, inc=1, device_id=(fsdp, piece, d // n_core, d % n_core), device_id_type=MESH_IDS
        )
    rim_peers = (piece + n_piece - 1) // n_piece + (2 * n_piece - 2 - piece) // n_piece
    pl.semaphore_wait(barrier, rim_peers + n_frames - 1)

    to_down = pltpu.make_async_remote_copy(
        src_ref=tok_ref,
        dst_ref=rim_ref.at[0],
        send_sem=send_sem.at[0],
        recv_sem=recv_sem.at[0],
        device_id=down,
        device_id_type=MESH_IDS,
    )
    to_up = pltpu.make_async_remote_copy(
        src_ref=tok_ref,
        dst_ref=rim_ref.at[1],
        send_sem=send_sem.at[1],
        recv_sem=recv_sem.at[1],
        device_id=up,
        device_id_type=MESH_IDS,
    )

    @pl.when(has_down)
    def _():
        to_down.start()

    @pl.when(has_up)
    def _():
        to_up.start()

    crosses = []
    for k, d in enumerate(peers):
        copy = pltpu.make_async_remote_copy(
            src_ref=tok_ref.at[pl.ds(pl.multiple_of(d * per, 16), per)],
            dst_ref=cross_ref.at[pl.ds(pl.multiple_of(frame * per, 16), per)],
            send_sem=cross_send.at[k],
            recv_sem=cross_recv.at[k],
            device_id=(fsdp, piece, d // n_core, d % n_core),
            device_id_type=MESH_IDS,
        )
        copy.start()
        crosses.append(copy)
    own_rows = pl.ds(pl.multiple_of(frame * per, 16), per)
    own_copy = pltpu.make_async_copy(tok_ref.at[own_rows], cross_ref.at[own_rows], own_sem)
    own_copy.start()

    @pl.when(has_down)
    def _():
        to_down.wait_send()
        to_up.wait_recv()

    @pl.when(has_up)
    def _():
        to_up.wait_send()
        to_down.wait_recv()

    for copy in crosses:
        copy.wait()
    own_copy.wait()


def exchange_tokens(own):
    rows, feat = own.shape
    return pl.pallas_call(
        exchange_kernel,
        out_shape=(
            jax.ShapeDtypeStruct((2, rows, feat), own.dtype),
            jax.ShapeDtypeStruct((rows, feat), own.dtype),
        ),
        in_specs=[pl.BlockSpec(memory_space=pl.ANY)],
        out_specs=(pl.BlockSpec(memory_space=pl.ANY), pl.BlockSpec(memory_space=pl.ANY)),
        scratch_shapes=[
            pltpu.SemaphoreType.DMA((2,)),
            pltpu.SemaphoreType.DMA((2,)),
            pltpu.SemaphoreType.DMA((8,)),
            pltpu.SemaphoreType.DMA((8,)),
            pltpu.SemaphoreType.DMA(()),
        ],
        compiler_params=pltpu.CompilerParams(collective_id=0, has_side_effects=True),
        cost_estimate=pl.CostEstimate(flops=0, transcendentals=0, bytes_accessed=80 * rows * feat * 2),
    )(own)


def temporal_block(query_part, key_part, spatial_part, clip_counts, first_pos):
    n_frames, per_dev = query_part.shape[0], query_part.shape[1]
    scaling = 1.0 / math.sqrt(HD)
    position = first_pos + jnp.arange(per_dev, dtype=jnp.int32)
    live_mask = (position[:, None] < clip_counts[None, :])[:, None, None, :]
    scores = (
        jnp.einsum(
            "fphd,gphd->phfg", query_part, key_part, preferred_element_type=jnp.float32
        )
        * scaling
    )
    scores = jnp.where(live_mask, scores, -1e30)
    row_max = jnp.max(scores, axis=-1, keepdims=True)
    exp_terms = jnp.where(live_mask, jnp.exp(scores - row_max), 0.0)
    denominator = jnp.sum(exp_terms, axis=-1, keepdims=True)
    weights = exp_terms.astype(jnp.bfloat16)
    summed = jnp.einsum(
        "phfg,gphd->fphd", weights, spatial_part, preferred_element_type=jnp.float32
    )
    result = summed / jnp.transpose(denominator, (2, 0, 1, 3))
    return result.astype(jnp.bfloat16)


def swap_kernel(x_ref, y_ref, cross_send, cross_recv, own_sem):
    n_core = lax.axis_size("core")
    n_frames = lax.axis_size("fy") * n_core
    piece = lax.axis_index("piece")
    frame = lax.axis_index("fy") * n_core + lax.axis_index("core")
    fsdp = lax.axis_index("fsdp")
    per = x_ref.shape[0] // n_frames
    peers = [(frame + k) % n_frames for k in range(1, n_frames)]
    barrier = pltpu.get_barrier_semaphore()
    for d in peers:
        pl.semaphore_signal(
            barrier, inc=1, device_id=(fsdp, piece, d // n_core, d % n_core), device_id_type=MESH_IDS
        )
    pl.semaphore_wait(barrier, n_frames - 1)
    crosses = []
    for k, d in enumerate(peers):
        copy = pltpu.make_async_remote_copy(
            src_ref=x_ref.at[pl.ds(pl.multiple_of(d * per, 16), per)],
            dst_ref=y_ref.at[pl.ds(pl.multiple_of(frame * per, 16), per)],
            send_sem=cross_send.at[k],
            recv_sem=cross_recv.at[k],
            device_id=(fsdp, piece, d // n_core, d % n_core),
            device_id_type=MESH_IDS,
        )
        copy.start()
        crosses.append(copy)
    own_rows = pl.ds(pl.multiple_of(frame * per, 16), per)
    own_copy = pltpu.make_async_copy(x_ref.at[own_rows], y_ref.at[own_rows], own_sem)
    own_copy.start()
    for copy in crosses:
        copy.wait()
    own_copy.wait()


def swap_frames(x):
    rows, feat = x.shape
    return pl.pallas_call(
        swap_kernel,
        out_shape=jax.ShapeDtypeStruct((rows, feat), x.dtype),
        in_specs=[pl.BlockSpec(memory_space=pl.ANY)],
        out_specs=pl.BlockSpec(memory_space=pl.ANY),
        scratch_shapes=[
            pltpu.SemaphoreType.DMA((8,)),
            pltpu.SemaphoreType.DMA((8,)),
            pltpu.SemaphoreType.DMA(()),
        ],
        compiler_params=pltpu.CompilerParams(collective_id=1, has_side_effects=True),
        cost_estimate=pl.CostEstimate(flops=0, transcendentals=0, bytes_accessed=2 * rows * feat * 2),
    )(x)


def swap_project_kernel(x_ref, w_ref, o_ref, recv, cross_send, cross_recv, own_sem):
    n_core = lax.axis_size("core")
    n_frames = lax.axis_size("fy") * n_core
    piece = lax.axis_index("piece")
    frame = lax.axis_index("fy") * n_core + lax.axis_index("core")
    fsdp = lax.axis_index("fsdp")
    per = x_ref.shape[0] // n_frames
    peers = [(frame + k) % n_frames for k in range(1, n_frames)]
    sources = [(frame + n_frames - k) % n_frames for k in range(1, n_frames)]
    barrier = pltpu.get_barrier_semaphore()
    for d in peers:
        pl.semaphore_signal(
            barrier, inc=1, device_id=(fsdp, piece, d // n_core, d % n_core), device_id_type=MESH_IDS
        )
    pl.semaphore_wait(barrier, n_frames - 1)
    crosses = []
    for k, d in enumerate(peers):
        copy = pltpu.make_async_remote_copy(
            src_ref=x_ref.at[pl.ds(pl.multiple_of(d * per, 16), per)],
            dst_ref=recv.at[pl.ds(pl.multiple_of(frame * per, 16), per)],
            send_sem=cross_send.at[k],
            recv_sem=cross_recv.at[k],
            device_id=(fsdp, piece, d // n_core, d % n_core),
            device_id_type=MESH_IDS,
        )
        copy.start()
        crosses.append(copy)
    own_rows = pl.ds(pl.multiple_of(frame * per, 16), per)
    own_copy = pltpu.make_async_copy(x_ref.at[own_rows], recv.at[own_rows], own_sem)
    own_copy.start()
    own_copy.wait()
    o_ref[own_rows, :] = jnp.dot(
        recv[own_rows, :], w_ref[...], preferred_element_type=jnp.float32
    ).astype(o_ref.dtype)
    for k, src in enumerate(sources):
        rows = pl.ds(pl.multiple_of(src * per, 16), per)
        incoming = pltpu.make_async_remote_copy(
            src_ref=x_ref.at[rows],
            dst_ref=recv.at[rows],
            send_sem=cross_send.at[k],
            recv_sem=cross_recv.at[k],
            device_id=(fsdp, piece, src // n_core, src % n_core),
            device_id_type=MESH_IDS,
        )
        incoming.wait_recv()
        o_ref[rows, :] = jnp.dot(
            recv[rows, :], w_ref[...], preferred_element_type=jnp.float32
        ).astype(o_ref.dtype)
    for copy in crosses:
        copy.wait_send()


def swap_project(x, w):
    rows, feat = x.shape
    return pl.pallas_call(
        swap_project_kernel,
        out_shape=jax.ShapeDtypeStruct((rows, w.shape[1]), x.dtype),
        in_specs=[pl.BlockSpec(memory_space=pl.ANY), pl.BlockSpec(memory_space=pltpu.VMEM)],
        out_specs=pl.BlockSpec(memory_space=pltpu.VMEM),
        scratch_shapes=[
            pltpu.VMEM((rows, feat), x.dtype),
            pltpu.SemaphoreType.DMA((8,)),
            pltpu.SemaphoreType.DMA((8,)),
            pltpu.SemaphoreType.DMA(()),
        ],
        compiler_params=pltpu.CompilerParams(collective_id=1, has_side_effects=True),
        cost_estimate=pl.CostEstimate(
            flops=2 * rows * feat * w.shape[1], transcendentals=0, bytes_accessed=2 * rows * feat * 2
        ),
    )(x, w)


def local(tokens, mod_scale, mod_shift, w_qkv, w_out, neighbors, counts):
    tok_count = tokens.shape[1]
    feat_count = tokens.shape[2]
    n_frames = lax.axis_size("fy") * lax.axis_size("core")
    own = tokens[0]
    rims, crossed = exchange_tokens(own)
    piece_index = lax.axis_index("piece")
    above = jnp.where(piece_index > 0, rims[0], jnp.zeros_like(own))
    below = jnp.where(piece_index < lax.axis_size("piece") - 1, rims[1], jnp.zeros_like(own))
    core = lax.axis_index("core")
    half_rows = w_qkv.shape[0] // 2
    w_half = lax.dynamic_slice_in_dim(w_qkv, core * half_rows, half_rows, axis=0)
    w_pieces = lax.all_gather(w_half, ("fsdp", "core"), axis=0, tiled=False)
    w_full = w_pieces.reshape(lax.axis_size("fsdp"), w_qkv.shape[0], w_qkv.shape[1])
    w_out, w_full = lax.optimization_barrier((w_out, w_full))
    w_out_full = lax.all_gather(w_out, "fsdp", axis=0, tiled=True)
    normed_all = layer_norm(
        jnp.concatenate([above, own, below], axis=0), mod_scale[0], mod_shift[0]
    )
    shard_cols = w_full.shape[2]
    w_query = jnp.concatenate(
        [w_full[0], w_full[1, :, : feat_count - shard_cols]], axis=1
    )
    normed_cross = layer_norm(crossed, mod_scale[0], mod_shift[0])
    w_key = jnp.concatenate(
        [w_full[1, :, feat_count - shard_cols :], w_full[2, :, : 2 * shard_cols - feat_count]], axis=1
    )
    q_both = jnp.dot(
        jnp.concatenate([normed_all[tok_count : 2 * tok_count], normed_cross], axis=0),
        w_query,
        preferred_element_type=jnp.float32,
    ).astype(jnp.bfloat16)
    queries = q_both[:tok_count]
    key_cross = jnp.dot(normed_cross, w_key, preferred_element_type=jnp.float32).astype(jnp.bfloat16)
    kv_all = jnp.einsum(
        "tk,jkc->jtc", normed_all, w_full[1:], preferred_element_type=jnp.float32
    ).astype(jnp.bfloat16)
    frame_index = lax.axis_index("fy") * lax.axis_size("core") + lax.axis_index("core")
    piece_index = lax.axis_index("piece")
    clip_counts = counts[0]
    count_here = lax.dynamic_index_in_dim(clip_counts, frame_index, 0, keepdims=False)
    rows_here = tok_count // (TGW * TILE)
    first_tile = (piece_index * rows_here - 1) * TGW
    spatial = spatial_rows(queries, kv_all, neighbors[0], first_tile, count_here)
    frame_axes = ("fy", "core")
    spatial_part = lax.all_to_all(spatial, frame_axes, split_axis=0, concat_axis=0, tiled=True)
    per_dev = tok_count // n_frames
    first_pos = piece_index * tok_count + frame_index * per_dev
    part_shape = (n_frames, per_dev, HEADS, HD)
    temporal = temporal_block(
        q_both[tok_count:].reshape(part_shape),
        key_cross.reshape(part_shape),
        spatial_part.reshape(part_shape),
        clip_counts,
        first_pos,
    )
    projected = swap_project(temporal.reshape(tok_count, feat_count), w_out_full)
    return projected.reshape(1, tok_count, feat_count)


def solution(mesh):
    n_fsdp = mesh.shape["fsdp"]
    n_sp = mesh.shape["sp"]
    split = Mesh(
        mesh.devices.reshape(n_fsdp, PIECES, n_sp // PIECES // 2, 2),
        ("fsdp", "piece", "fy", "core"),
    )
    seq = ("piece", "fy", "core")
    placed = (
        P("fsdp", seq, None),
        P("fsdp", None),
        P("fsdp", None),
        P(None, "fsdp"),
        P("fsdp", None),
        P("fsdp", seq, None),
        P("fsdp", None),
    )
    return jax.shard_map(
        local, mesh=split, in_specs=placed, out_specs=P("fsdp", seq, None), check_vma=False
    )
```

```python
import math

import jax
import jax.numpy as jnp
from jax import lax
from jax.experimental import pallas as pl
from jax.experimental.pallas import tpu as pltpu
from jax.sharding import Mesh
from jax.sharding import PartitionSpec as P

HEADS = 12
HD = 128
TILE = 128
TGW = 5
NBR = 6
PIECES = 4


def passed_along(block, axis, distance):
    devices = range(lax.axis_size(axis))
    route = [(i - distance, i) for i in devices if i - distance in devices]
    return lax.ppermute(block, axis, route)


def layer_norm(tokens, mod_scale, mod_shift):
    values_f32 = tokens.astype(jnp.float32)
    center = jnp.mean(values_f32, axis=-1, keepdims=True)
    spread = jnp.mean((values_f32 - center) ** 2, axis=-1, keepdims=True)
    normal = (values_f32 - center) / jnp.sqrt(spread + 1e-06)
    return (normal * (1.0 + mod_scale) + mod_shift).astype(jnp.bfloat16)


def spatial_kernel(list_ref, scalar_ref, q_ref, k_ref, v_ref, o_ref):
    scaling = 1.0 / math.sqrt(HD)
    first_tile = scalar_ref[0]
    count_here = scalar_ref[1]
    local_tiles = q_ref.shape[0] // TILE
    for t, c in [(t, c) for c in range(q_ref.shape[1] // HD) for t in range(local_tiles)]:
        cols = slice(c * HD, (c + 1) * HD)
        query = q_ref[t * TILE : (t + 1) * TILE, cols]
        parts = []
        block_max = None
        for n in range(NBR):
            tile_id = list_ref[t * NBR + n]
            start = pl.multiple_of((tile_id - first_tile) * TILE, TILE)
            key = k_ref[pl.ds(start, TILE), cols]
            scores = (
                lax.dot_general(
                    query, key, (((1,), (1,)), ((), ())), preferred_element_type=jnp.float32
                )
                * scaling
            )
            key_pos = tile_id * TILE + lax.broadcasted_iota(jnp.int32, (1, TILE), 1)
            scores = scores + jnp.where(key_pos < count_here, 0.0, -1e30)
            block_max = scores if block_max is None else jnp.maximum(block_max, scores)
            parts.append((scores, start))
        row_max = jnp.max(block_max, axis=-1, keepdims=True)
        exp_total = None
        summed = None
        for scores, start in parts:
            exp_terms = jnp.exp(scores - row_max)
            value = v_ref[pl.ds(start, TILE), cols]
            part_out = jnp.dot(
                exp_terms.astype(jnp.bfloat16), value, preferred_element_type=jnp.float32
            )
            exp_total = exp_terms if exp_total is None else exp_total + exp_terms
            summed = part_out if summed is None else summed + part_out
        denominator = jnp.sum(exp_total, axis=-1, keepdims=True)
        o_ref[t * TILE : (t + 1) * TILE, cols] = (summed / denominator).astype(o_ref.dtype)


def spatial_rows(queries, kv_all, tile_list, first_tile, count_here):
    buffer_rows = kv_all.shape[1]
    rows, feat = queries.shape
    scalars = jnp.stack([first_tile, count_here]).astype(jnp.int32)
    width = 3 * HD
    per_shard = kv_all.shape[2] // width
    k0 = feat // width
    grid_spec = pltpu.PrefetchScalarGridSpec(
        num_scalar_prefetch=2,
        grid=(feat // width,),
        in_specs=[
            pl.BlockSpec((rows, width), lambda g, lst, sc: (0, g)),
            pl.BlockSpec(
                (None, buffer_rows, width),
                lambda g, lst, sc: ((k0 + g) // per_shard - 1, 0, (k0 + g) % per_shard),
            ),
            pl.BlockSpec(
                (None, buffer_rows, width),
                lambda g, lst, sc: ((2 * k0 + g) // per_shard - 1, 0, (2 * k0 + g) % per_shard),
            ),
        ],
        out_specs=pl.BlockSpec((rows, width), lambda g, lst, sc: (0, g)),
    )
    flops = 4 * rows * NBR * TILE * feat
    return pl.pallas_call(
        spatial_kernel,
        grid_spec=grid_spec,
        out_shape=jax.ShapeDtypeStruct((rows, feat), jnp.bfloat16),
        cost_estimate=pl.CostEstimate(
            flops=flops,
            transcendentals=rows * NBR * TILE * HEADS,
            bytes_accessed=2 * (rows * feat * 2 + buffer_rows * feat * 2),
        ),
    )(tile_list.reshape(-1).astype(jnp.int32), scalars, queries, kv_all, kv_all)


MESH_IDS = pl.DeviceIdType.MESH


def exchange_kernel(tok_ref, rim_ref, cross_ref, send_sem, recv_sem, cross_send, cross_recv, own_sem):
    n_piece = lax.axis_size("piece")
    n_core = lax.axis_size("core")
    n_frames = lax.axis_size("fy") * n_core
    piece = lax.axis_index("piece")
    frame = lax.axis_index("fy") * n_core + lax.axis_index("core")
    fsdp = lax.axis_index("fsdp")
    here = (fsdp, piece, lax.axis_index("fy"), lax.axis_index("core"))
    up = (fsdp, piece - 1, here[2], here[3])
    down = (fsdp, piece + 1, here[2], here[3])
    has_up = piece > 0
    has_down = piece < n_piece - 1
    per = tok_ref.shape[0] // n_frames
    peers = [(frame + k) % n_frames for k in range(1, n_frames)]
    barrier = pltpu.get_barrier_semaphore()

    @pl.when(has_up)
    def _():
        pl.semaphore_signal(barrier, inc=1, device_id=up, device_id_type=MESH_IDS)

    @pl.when(has_down)
    def _():
        pl.semaphore_signal(barrier, inc=1, device_id=down, device_id_type=MESH_IDS)

    for d in peers:
        pl.semaphore_signal(
            barrier, inc=1, device_id=(fsdp, piece, d // n_core, d % n_core), device_id_type=MESH_IDS
        )
    rim_peers = (piece + n_piece - 1) // n_piece + (2 * n_piece - 2 - piece) // n_piece
    pl.semaphore_wait(barrier, rim_peers + n_frames - 1)

    to_down = pltpu.make_async_remote_copy(
        src_ref=tok_ref,
        dst_ref=rim_ref.at[0],
        send_sem=send_sem.at[0],
        recv_sem=recv_sem.at[0],
        device_id=down,
        device_id_type=MESH_IDS,
    )
    to_up = pltpu.make_async_remote_copy(
        src_ref=tok_ref,
        dst_ref=rim_ref.at[1],
        send_sem=send_sem.at[1],
        recv_sem=recv_sem.at[1],
        device_id=up,
        device_id_type=MESH_IDS,
    )

    @pl.when(has_down)
    def _():
        to_down.start()

    @pl.when(has_up)
    def _():
        to_up.start()

    crosses = []
    for k, d in enumerate(peers):
        copy = pltpu.make_async_remote_copy(
            src_ref=tok_ref.at[pl.ds(pl.multiple_of(d * per, 16), per)],
            dst_ref=cross_ref.at[pl.ds(pl.multiple_of(frame * per, 16), per)],
            send_sem=cross_send.at[k],
            recv_sem=cross_recv.at[k],
            device_id=(fsdp, piece, d // n_core, d % n_core),
            device_id_type=MESH_IDS,
        )
        copy.start()
        crosses.append(copy)
    own_rows = pl.ds(pl.multiple_of(frame * per, 16), per)
    own_copy = pltpu.make_async_copy(tok_ref.at[own_rows], cross_ref.at[own_rows], own_sem)
    own_copy.start()

    @pl.when(has_down)
    def _():
        to_down.wait_send()
        to_up.wait_recv()

    @pl.when(has_up)
    def _():
        to_up.wait_send()
        to_down.wait_recv()

    for copy in crosses:
        copy.wait()
    own_copy.wait()


def exchange_tokens(own):
    rows, feat = own.shape
    return pl.pallas_call(
        exchange_kernel,
        out_shape=(
            jax.ShapeDtypeStruct((2, rows, feat), own.dtype),
            jax.ShapeDtypeStruct((rows, feat), own.dtype),
        ),
        in_specs=[pl.BlockSpec(memory_space=pl.ANY)],
        out_specs=(pl.BlockSpec(memory_space=pl.ANY), pl.BlockSpec(memory_space=pl.ANY)),
        scratch_shapes=[
            pltpu.SemaphoreType.DMA((2,)),
            pltpu.SemaphoreType.DMA((2,)),
            pltpu.SemaphoreType.DMA((8,)),
            pltpu.SemaphoreType.DMA((8,)),
            pltpu.SemaphoreType.DMA(()),
        ],
        compiler_params=pltpu.CompilerParams(collective_id=0, has_side_effects=True),
        cost_estimate=pl.CostEstimate(flops=0, transcendentals=0, bytes_accessed=80 * rows * feat * 2),
    )(own)


def temporal_block(query_part, key_part, spatial_part, clip_counts, first_pos):
    n_frames, per_dev = query_part.shape[0], query_part.shape[1]
    scaling = 1.0 / math.sqrt(HD)
    position = first_pos + jnp.arange(per_dev, dtype=jnp.int32)
    live_mask = (position[:, None] < clip_counts[None, :])[:, None, None, :]
    scores = (
        jnp.einsum(
            "fphd,gphd->phfg", query_part, key_part, preferred_element_type=jnp.float32
        )
        * scaling
    )
    scores = jnp.where(live_mask, scores, -1e30)
    row_max = jnp.max(scores, axis=-1, keepdims=True)
    exp_terms = jnp.where(live_mask, jnp.exp(scores - row_max), 0.0)
    denominator = jnp.sum(exp_terms, axis=-1, keepdims=True)
    weights = exp_terms.astype(jnp.bfloat16)
    summed = jnp.einsum(
        "phfg,gphd->fphd", weights, spatial_part, preferred_element_type=jnp.float32
    )
    result = summed / jnp.transpose(denominator, (2, 0, 1, 3))
    return result.astype(jnp.bfloat16)


def swap_kernel(x_ref, y_ref, cross_send, cross_recv, own_sem):
    n_core = lax.axis_size("core")
    n_frames = lax.axis_size("fy") * n_core
    piece = lax.axis_index("piece")
    frame = lax.axis_index("fy") * n_core + lax.axis_index("core")
    fsdp = lax.axis_index("fsdp")
    per = x_ref.shape[0] // n_frames
    peers = [(frame + k) % n_frames for k in range(1, n_frames)]
    barrier = pltpu.get_barrier_semaphore()
    for d in peers:
        pl.semaphore_signal(
            barrier, inc=1, device_id=(fsdp, piece, d // n_core, d % n_core), device_id_type=MESH_IDS
        )
    pl.semaphore_wait(barrier, n_frames - 1)
    crosses = []
    for k in (3, 2, 4, 1, 5, 0, 6):
        d = peers[k]
        copy = pltpu.make_async_remote_copy(
            src_ref=x_ref.at[pl.ds(pl.multiple_of(d * per, 16), per)],
            dst_ref=y_ref.at[pl.ds(pl.multiple_of(frame * per, 16), per)],
            send_sem=cross_send.at[k],
            recv_sem=cross_recv.at[k],
            device_id=(fsdp, piece, d // n_core, d % n_core),
            device_id_type=MESH_IDS,
        )
        copy.start()
        crosses.append(copy)
    own_rows = pl.ds(pl.multiple_of(frame * per, 16), per)
    own_copy = pltpu.make_async_copy(x_ref.at[own_rows], y_ref.at[own_rows], own_sem)
    own_copy.start()
    for copy in crosses:
        copy.wait()
    own_copy.wait()


def swap_frames(x):
    rows, feat = x.shape
    return pl.pallas_call(
        swap_kernel,
        out_shape=jax.ShapeDtypeStruct((rows, feat), x.dtype),
        in_specs=[pl.BlockSpec(memory_space=pl.ANY)],
        out_specs=pl.BlockSpec(memory_space=pl.ANY),
        scratch_shapes=[
            pltpu.SemaphoreType.DMA((8,)),
            pltpu.SemaphoreType.DMA((8,)),
            pltpu.SemaphoreType.DMA(()),
        ],
        compiler_params=pltpu.CompilerParams(collective_id=1, has_side_effects=True),
        cost_estimate=pl.CostEstimate(flops=0, transcendentals=0, bytes_accessed=2 * rows * feat * 2),
    )(x)


def local(tokens, mod_scale, mod_shift, w_qkv, w_out, neighbors, counts):
    tok_count = tokens.shape[1]
    feat_count = tokens.shape[2]
    n_frames = lax.axis_size("fy") * lax.axis_size("core")
    own = tokens[0]
    rims, crossed = exchange_tokens(own)
    piece_index = lax.axis_index("piece")
    above = jnp.where(piece_index > 0, rims[0], jnp.zeros_like(own))
    below = jnp.where(piece_index < lax.axis_size("piece") - 1, rims[1], jnp.zeros_like(own))
    core = lax.axis_index("core")
    half_rows = w_qkv.shape[0] // 2
    w_half = lax.dynamic_slice_in_dim(w_qkv, core * half_rows, half_rows, axis=0)
    w_pieces = lax.all_gather(w_half, ("fsdp", "core"), axis=0, tiled=False)
    w_full = w_pieces.reshape(lax.axis_size("fsdp"), w_qkv.shape[0], w_qkv.shape[1])
    w_out, w_full = lax.optimization_barrier((w_out, w_full))
    w_out_full = lax.all_gather(w_out, "fsdp", axis=0, tiled=True)
    normed_all = layer_norm(
        jnp.concatenate([above, own, below], axis=0), mod_scale[0], mod_shift[0]
    )
    shard_cols = w_full.shape[2]
    w_query = jnp.concatenate(
        [w_full[0], w_full[1, :, : feat_count - shard_cols]], axis=1
    )
    normed_cross = layer_norm(crossed, mod_scale[0], mod_shift[0])
    w_key = jnp.concatenate(
        [w_full[1, :, feat_count - shard_cols :], w_full[2, :, : 2 * shard_cols - feat_count]], axis=1
    )
    q_both = jnp.dot(
        jnp.concatenate([normed_all[tok_count : 2 * tok_count], normed_cross], axis=0),
        w_query,
        preferred_element_type=jnp.float32,
    ).astype(jnp.bfloat16)
    queries = q_both[:tok_count]
    key_cross = jnp.dot(normed_cross, w_key, preferred_element_type=jnp.float32).astype(jnp.bfloat16)
    kv_all = jnp.einsum(
        "tk,jkc->jtc", normed_all, w_full[1:], preferred_element_type=jnp.float32
    ).astype(jnp.bfloat16)
    frame_index = lax.axis_index("fy") * lax.axis_size("core") + lax.axis_index("core")
    piece_index = lax.axis_index("piece")
    clip_counts = counts[0]
    count_here = lax.dynamic_index_in_dim(clip_counts, frame_index, 0, keepdims=False)
    rows_here = tok_count // (TGW * TILE)
    first_tile = (piece_index * rows_here - 1) * TGW
    spatial = spatial_rows(queries, kv_all, neighbors[0], first_tile, count_here)
    frame_axes = ("fy", "core")
    spatial_part = lax.all_to_all(spatial, frame_axes, split_axis=0, concat_axis=0, tiled=True)
    per_dev = tok_count // n_frames
    first_pos = piece_index * tok_count + frame_index * per_dev
    part_shape = (n_frames, per_dev, HEADS, HD)
    temporal = temporal_block(
        q_both[tok_count:].reshape(part_shape),
        key_cross.reshape(part_shape),
        spatial_part.reshape(part_shape),
        clip_counts,
        first_pos,
    )
    flat_temporal = swap_frames(temporal.reshape(tok_count, feat_count))
    projected = jnp.dot(flat_temporal, w_out_full, preferred_element_type=jnp.float32)
    return projected.astype(jnp.bfloat16).reshape(1, tok_count, feat_count)


def solution(mesh):
    n_fsdp = mesh.shape["fsdp"]
    n_sp = mesh.shape["sp"]
    split = Mesh(
        mesh.devices.reshape(n_fsdp, PIECES, n_sp // PIECES // 2, 2),
        ("fsdp", "piece", "fy", "core"),
    )
    seq = ("piece", "fy", "core")
    placed = (
        P("fsdp", seq, None),
        P("fsdp", None),
        P("fsdp", None),
        P(None, "fsdp"),
        P("fsdp", None),
        P("fsdp", seq, None),
        P("fsdp", None),
    )
    return jax.shard_map(
        local, mesh=split, in_specs=placed, out_specs=P("fsdp", seq, None), check_vma=False
    )
```

```python
import math

import jax
import jax.numpy as jnp
from jax import lax
from jax.experimental import pallas as pl
from jax.experimental.pallas import tpu as pltpu
from jax.sharding import Mesh
from jax.sharding import PartitionSpec as P

HEADS = 12
HD = 128
TILE = 128
TGW = 5
NBR = 6
PIECES = 4


def passed_along(block, axis, distance):
    devices = range(lax.axis_size(axis))
    route = [(i - distance, i) for i in devices if i - distance in devices]
    return lax.ppermute(block, axis, route)


def layer_norm(tokens, mod_scale, mod_shift):
    values_f32 = tokens.astype(jnp.float32)
    center = jnp.mean(values_f32, axis=-1, keepdims=True)
    spread = jnp.mean((values_f32 - center) ** 2, axis=-1, keepdims=True)
    normal = (values_f32 - center) / jnp.sqrt(spread + 1e-06)
    return (normal * (1.0 + mod_scale) + mod_shift).astype(jnp.bfloat16)


def spatial_kernel(list_ref, scalar_ref, q_ref, k_ref, v_ref, o_ref):
    scaling = 1.0 / math.sqrt(HD)
    first_tile = scalar_ref[0]
    count_here = scalar_ref[1]
    local_tiles = q_ref.shape[0] // TILE
    for t, c in [(t, c) for c in range(q_ref.shape[1] // HD) for t in range(local_tiles)]:
        cols = slice(c * HD, (c + 1) * HD)
        query = q_ref[t * TILE : (t + 1) * TILE, cols]
        parts = []
        block_max = None
        for n in range(NBR):
            tile_id = list_ref[t * NBR + n]
            start = pl.multiple_of((tile_id - first_tile) * TILE, TILE)
            key = k_ref[pl.ds(start, TILE), cols]
            scores = (
                lax.dot_general(
                    query, key, (((1,), (1,)), ((), ())), preferred_element_type=jnp.float32
                )
                * scaling
            )
            key_pos = tile_id * TILE + lax.broadcasted_iota(jnp.int32, (1, TILE), 1)
            scores = scores + jnp.where(key_pos < count_here, 0.0, -1e30)
            block_max = scores if block_max is None else jnp.maximum(block_max, scores)
            parts.append((scores, start))
        row_max = jnp.max(block_max, axis=-1, keepdims=True)
        exp_total = None
        summed = None
        for scores, start in parts:
            exp_terms = jnp.exp(scores - row_max)
            value = v_ref[pl.ds(start, TILE), cols]
            part_out = jnp.dot(
                exp_terms.astype(jnp.bfloat16), value, preferred_element_type=jnp.float32
            )
            exp_total = exp_terms if exp_total is None else exp_total + exp_terms
            summed = part_out if summed is None else summed + part_out
        denominator = jnp.sum(exp_total, axis=-1, keepdims=True)
        o_ref[t * TILE : (t + 1) * TILE, cols] = (summed / denominator).astype(o_ref.dtype)


def spatial_rows(queries, kv_all, tile_list, first_tile, count_here):
    buffer_rows = kv_all.shape[1]
    rows, feat = queries.shape
    scalars = jnp.stack([first_tile, count_here]).astype(jnp.int32)
    width = 3 * HD
    per_shard = kv_all.shape[2] // width
    k0 = feat // width
    grid_spec = pltpu.PrefetchScalarGridSpec(
        num_scalar_prefetch=2,
        grid=(feat // width,),
        in_specs=[
            pl.BlockSpec((rows, width), lambda g, lst, sc: (0, g)),
            pl.BlockSpec(
                (None, buffer_rows, width),
                lambda g, lst, sc: ((k0 + g) // per_shard - 1, 0, (k0 + g) % per_shard),
            ),
            pl.BlockSpec(
                (None, buffer_rows, width),
                lambda g, lst, sc: ((2 * k0 + g) // per_shard - 1, 0, (2 * k0 + g) % per_shard),
            ),
        ],
        out_specs=pl.BlockSpec((rows, width), lambda g, lst, sc: (0, g)),
    )
    flops = 4 * rows * NBR * TILE * feat
    return pl.pallas_call(
        spatial_kernel,
        grid_spec=grid_spec,
        out_shape=jax.ShapeDtypeStruct((rows, feat), jnp.bfloat16),
        cost_estimate=pl.CostEstimate(
            flops=flops,
            transcendentals=rows * NBR * TILE * HEADS,
            bytes_accessed=2 * (rows * feat * 2 + buffer_rows * feat * 2),
        ),
    )(tile_list.reshape(-1).astype(jnp.int32), scalars, queries, kv_all, kv_all)


MESH_IDS = pl.DeviceIdType.MESH


def exchange_kernel(tok_ref, rim_ref, cross_ref, send_sem, recv_sem, cross_send, cross_recv, own_sem):
    n_piece = lax.axis_size("piece")
    n_core = lax.axis_size("core")
    n_frames = lax.axis_size("fy") * n_core
    piece = lax.axis_index("piece")
    frame = lax.axis_index("fy") * n_core + lax.axis_index("core")
    fsdp = lax.axis_index("fsdp")
    here = (fsdp, piece, lax.axis_index("fy"), lax.axis_index("core"))
    up = (fsdp, piece - 1, here[2], here[3])
    down = (fsdp, piece + 1, here[2], here[3])
    has_up = piece > 0
    has_down = piece < n_piece - 1
    per = tok_ref.shape[0] // n_frames
    peers = [(frame + k) % n_frames for k in range(1, n_frames)]
    barrier = pltpu.get_barrier_semaphore()

    @pl.when(has_up)
    def _():
        pl.semaphore_signal(barrier, inc=1, device_id=up, device_id_type=MESH_IDS)

    @pl.when(has_down)
    def _():
        pl.semaphore_signal(barrier, inc=1, device_id=down, device_id_type=MESH_IDS)

    for d in peers:
        pl.semaphore_signal(
            barrier, inc=1, device_id=(fsdp, piece, d // n_core, d % n_core), device_id_type=MESH_IDS
        )
    rim_peers = (piece + n_piece - 1) // n_piece + (2 * n_piece - 2 - piece) // n_piece
    pl.semaphore_wait(barrier, rim_peers + n_frames - 1)

    to_down = pltpu.make_async_remote_copy(
        src_ref=tok_ref,
        dst_ref=rim_ref.at[0],
        send_sem=send_sem.at[0],
        recv_sem=recv_sem.at[0],
        device_id=down,
        device_id_type=MESH_IDS,
    )
    to_up = pltpu.make_async_remote_copy(
        src_ref=tok_ref,
        dst_ref=rim_ref.at[1],
        send_sem=send_sem.at[1],
        recv_sem=recv_sem.at[1],
        device_id=up,
        device_id_type=MESH_IDS,
    )

    @pl.when(has_down)
    def _():
        to_down.start()

    @pl.when(has_up)
    def _():
        to_up.start()

    crosses = []
    for k, d in enumerate(peers):
        copy = pltpu.make_async_remote_copy(
            src_ref=tok_ref.at[pl.ds(pl.multiple_of(d * per, 16), per)],
            dst_ref=cross_ref.at[pl.ds(pl.multiple_of(frame * per, 16), per)],
            send_sem=cross_send.at[k],
            recv_sem=cross_recv.at[k],
            device_id=(fsdp, piece, d // n_core, d % n_core),
            device_id_type=MESH_IDS,
        )
        copy.start()
        crosses.append(copy)
    own_rows = pl.ds(pl.multiple_of(frame * per, 16), per)
    own_copy = pltpu.make_async_copy(tok_ref.at[own_rows], cross_ref.at[own_rows], own_sem)
    own_copy.start()

    @pl.when(has_down)
    def _():
        to_down.wait_send()
        to_up.wait_recv()

    @pl.when(has_up)
    def _():
        to_up.wait_send()
        to_down.wait_recv()

    for copy in crosses:
        copy.wait()
    own_copy.wait()


def exchange_tokens(own):
    rows, feat = own.shape
    return pl.pallas_call(
        exchange_kernel,
        out_shape=(
            jax.ShapeDtypeStruct((2, rows, feat), own.dtype),
            jax.ShapeDtypeStruct((rows, feat), own.dtype),
        ),
        in_specs=[pl.BlockSpec(memory_space=pl.ANY)],
        out_specs=(pl.BlockSpec(memory_space=pl.ANY), pl.BlockSpec(memory_space=pl.ANY)),
        scratch_shapes=[
            pltpu.SemaphoreType.DMA((2,)),
            pltpu.SemaphoreType.DMA((2,)),
            pltpu.SemaphoreType.DMA((8,)),
            pltpu.SemaphoreType.DMA((8,)),
            pltpu.SemaphoreType.DMA(()),
        ],
        compiler_params=pltpu.CompilerParams(collective_id=0, has_side_effects=True),
        cost_estimate=pl.CostEstimate(flops=0, transcendentals=0, bytes_accessed=80 * rows * feat * 2),
    )(own)


def temporal_block(query_part, key_part, spatial_part, clip_counts, first_pos):
    n_frames, per_dev = query_part.shape[0], query_part.shape[1]
    scaling = 1.0 / math.sqrt(HD)
    position = first_pos + jnp.arange(per_dev, dtype=jnp.int32)
    live_mask = (position[:, None] < clip_counts[None, :])[:, None, None, :]
    scores = (
        jnp.einsum(
            "fphd,gphd->phfg", query_part, key_part, preferred_element_type=jnp.float32
        )
        * scaling
    )
    scores = jnp.where(live_mask, scores, -1e30)
    row_max = jnp.max(scores, axis=-1, keepdims=True)
    exp_terms = jnp.where(live_mask, jnp.exp(scores - row_max), 0.0)
    denominator = jnp.sum(exp_terms, axis=-1, keepdims=True)
    weights = exp_terms.astype(jnp.bfloat16)
    summed = jnp.einsum(
        "phfg,gphd->fphd", weights, spatial_part, preferred_element_type=jnp.float32
    )
    result = summed / jnp.transpose(denominator, (2, 0, 1, 3))
    return result.astype(jnp.bfloat16)


def swap_kernel(x_ref, y_ref, cross_send, cross_recv, own_sem):
    n_core = lax.axis_size("core")
    n_frames = lax.axis_size("fy") * n_core
    piece = lax.axis_index("piece")
    frame = lax.axis_index("fy") * n_core + lax.axis_index("core")
    fsdp = lax.axis_index("fsdp")
    per = x_ref.shape[0] // n_frames
    peers = [(frame + k) % n_frames for k in range(1, n_frames)]
    barrier = pltpu.get_barrier_semaphore()
    for d in peers:
        pl.semaphore_signal(
            barrier, inc=1, device_id=(fsdp, piece, d // n_core, d % n_core), device_id_type=MESH_IDS
        )
    pl.semaphore_wait(barrier, n_frames - 1)
    crosses = []
    for k, d in enumerate(peers):
        copy = pltpu.make_async_remote_copy(
            src_ref=x_ref.at[pl.ds(pl.multiple_of(d * per, 16), per)],
            dst_ref=y_ref.at[pl.ds(pl.multiple_of(frame * per, 16), per)],
            send_sem=cross_send.at[k],
            recv_sem=cross_recv.at[k],
            device_id=(fsdp, piece, d // n_core, d % n_core),
            device_id_type=MESH_IDS,
        )
        copy.start()
        crosses.append(copy)
    own_rows = pl.ds(pl.multiple_of(frame * per, 16), per)
    own_copy = pltpu.make_async_copy(x_ref.at[own_rows], y_ref.at[own_rows], own_sem)
    own_copy.start()
    for copy in crosses:
        copy.wait()
    own_copy.wait()


def swap_frames(x):
    rows, feat = x.shape
    return pl.pallas_call(
        swap_kernel,
        out_shape=jax.ShapeDtypeStruct((rows, feat), x.dtype),
        in_specs=[pl.BlockSpec(memory_space=pl.ANY)],
        out_specs=pl.BlockSpec(memory_space=pl.ANY),
        scratch_shapes=[
            pltpu.SemaphoreType.DMA((8,)),
            pltpu.SemaphoreType.DMA((8,)),
            pltpu.SemaphoreType.DMA(()),
        ],
        compiler_params=pltpu.CompilerParams(collective_id=1, has_side_effects=True),
        cost_estimate=pl.CostEstimate(flops=0, transcendentals=0, bytes_accessed=2 * rows * feat * 2),
    )(x)


def local(tokens, mod_scale, mod_shift, w_qkv, w_out, neighbors, counts):
    tok_count = tokens.shape[1]
    feat_count = tokens.shape[2]
    n_frames = lax.axis_size("fy") * lax.axis_size("core")
    own = tokens[0]
    rims, crossed = exchange_tokens(own)
    piece_index = lax.axis_index("piece")
    above = jnp.where(piece_index > 0, rims[0], jnp.zeros_like(own))
    below = jnp.where(piece_index < lax.axis_size("piece") - 1, rims[1], jnp.zeros_like(own))
    core = lax.axis_index("core")
    half_rows = w_qkv.shape[0] // 2
    w_half = lax.dynamic_slice_in_dim(w_qkv, core * half_rows, half_rows, axis=0)
    w_pieces = lax.all_gather(w_half, ("fsdp", "core"), axis=0, tiled=False)
    w_full = w_pieces.reshape(lax.axis_size("fsdp"), w_qkv.shape[0], w_qkv.shape[1])
    w_out, w_full = lax.optimization_barrier((w_out, w_full))
    w_out_full = lax.all_gather(w_out, "fsdp", axis=0, tiled=True)
    normed_all = layer_norm(
        jnp.concatenate([above, own, below], axis=0), mod_scale[0], mod_shift[0]
    )
    shard_cols = w_full.shape[2]
    w_query = jnp.concatenate(
        [w_full[0], w_full[1, :, : feat_count - shard_cols]], axis=1
    )
    normed_cross = layer_norm(crossed, mod_scale[0], mod_shift[0])
    w_key = jnp.concatenate(
        [w_full[1, :, feat_count - shard_cols :], w_full[2, :, : 2 * shard_cols - feat_count]], axis=1
    )
    queries = jnp.dot(
        normed_all[tok_count : 2 * tok_count], w_query, preferred_element_type=jnp.float32
    ).astype(jnp.bfloat16)
    query_cross = jnp.dot(normed_cross, w_query, preferred_element_type=jnp.float32).astype(
        jnp.bfloat16
    )
    key_cross = jnp.dot(normed_cross, w_key, preferred_element_type=jnp.float32).astype(jnp.bfloat16)
    kv_all = jnp.einsum(
        "tk,jkc->jtc", normed_all, w_full[1:], preferred_element_type=jnp.float32
    ).astype(jnp.bfloat16)
    frame_index = lax.axis_index("fy") * lax.axis_size("core") + lax.axis_index("core")
    piece_index = lax.axis_index("piece")
    clip_counts = counts[0]
    count_here = lax.dynamic_index_in_dim(clip_counts, frame_index, 0, keepdims=False)
    rows_here = tok_count // (TGW * TILE)
    first_tile = (piece_index * rows_here - 1) * TGW
    spatial = spatial_rows(queries, kv_all, neighbors[0], first_tile, count_here)
    frame_axes = ("fy", "core")
    spatial_part = lax.all_to_all(spatial, frame_axes, split_axis=0, concat_axis=0, tiled=True)
    per_dev = tok_count // n_frames
    first_pos = piece_index * tok_count + frame_index * per_dev
    part_shape = (n_frames, per_dev, HEADS, HD)
    temporal = temporal_block(
        query_cross.reshape(part_shape),
        key_cross.reshape(part_shape),
        spatial_part.reshape(part_shape),
        clip_counts,
        first_pos,
    )
    flat_temporal = swap_frames(temporal.reshape(tok_count, feat_count))
    projected = jnp.dot(flat_temporal, w_out_full, preferred_element_type=jnp.float32)
    return projected.astype(jnp.bfloat16).reshape(1, tok_count, feat_count)


def solution(mesh):
    n_fsdp = mesh.shape["fsdp"]
    n_sp = mesh.shape["sp"]
    split = Mesh(
        mesh.devices.reshape(n_fsdp, PIECES, n_sp // PIECES // 2, 2),
        ("fsdp", "piece", "fy", "core"),
    )
    seq = ("piece", "fy", "core")
    placed = (
        P("fsdp", seq, None),
        P("fsdp", None),
        P("fsdp", None),
        P(None, "fsdp"),
        P("fsdp", None),
        P("fsdp", seq, None),
        P("fsdp", None),
    )
    return jax.shard_map(
        local, mesh=split, in_specs=placed, out_specs=P("fsdp", seq, None), check_vma=False
    )
```
